128 devices in a mesh: lon: 16 (over z_hi, y, core), lat: 8 (over z_lo, x).
Axes of the slice: x: 4, y: 4, z: 4 (z_hi: 2, z_lo: 2; z = z_hi * 2 + z_lo), core: 2. Of those that a mesh axis runs over, the one named last changes fastest.
Arguments:
- temp: float32 [6, 3072, 4096], P(None, 'lat', 'lon'), may hold values from -6 to 6
- salt: float32 [6, 3072, 4096], P(None, 'lat', 'lon'), may hold values from 32 to 36
- east_vel: float32 [6, 3072, 4096], P(None, 'lat', 'lon'), may hold values from -0.2 to 0.2
- north_vel: float32 [6, 3072, 4096], P(None, 'lat', 'lon'), may hold values from -0.2 to 0.2
- land_mask: int32 [3072, 4096], P('lat', 'lon'), may hold values 0 or 1
- ice_mask: int32 [3072, 4096], P('lat', 'lon'), may hold values 0 or 1
- ice_u: float32 [3072, 4096], P('lat', 'lon'), may hold values from -3 to 3
- ice_v: float32 [3072, 4096], P('lat', 'lon'), may hold values from -3 to 3
- ice_pressure_field: float32 [3072, 4096], P('lat', 'lon'), may hold values from 1 to 3
- wind_x: float32 [3072, 4096], P('lat', 'lon'), may hold values from -3 to 3
- wind_y: float32 [3072, 4096], P('lat', 'lon'), may hold values from -3 to 3
Outputs:
- temp_out: float32 [6, 3072, 4096], P(None, 'lat', 'lon')
- salt_out: float32 [6, 3072, 4096], P(None, 'lat', 'lon')
- ice_u_out: float32 [3072, 4096], P('lat', 'lon')
- ice_v_out: float32 [3072, 4096], P('lat', 'lon')
The draws below stay inside these ranges and needn't reach their ends.
All inputs are finite; a program needn't handle non-finite values. No bound on the sum of `land_mask` or of `ice_mask` on one device may be relied on, other than what follows from the above.
Results may differ from the reference program's by a relative error of at most 0.0003.
Values sent between devices are 32-bit elements; how exact they have to be, the bound alone decides.
A program may use at most 192 MiB of HBM per device.

```python
import math
import jax
import jax.numpy as jnp

LEVELS = 6
SUBCYCLES = 4
GRID_X = 4096
GRID_Y = 3072


def place_ends(drawn, key, least, high):
    spot = [jax.random.randint(jax.random.fold_in(key, axis), (), 0, length) for axis, length in enumerate(drawn.shape)]
    longest = drawn.shape.index(max(drawn.shape))
    neighbour = spot[:longest] + [(spot[longest] + 1) % drawn.shape[longest]] + spot[longest + 1:]
    return drawn.at[tuple(spot)].set(least).at[tuple(neighbour)].set(high)


def levels(rng, shape, shards, smallest, largest):
    gain = 1.0
    for dim, shards_of in shards:
        heights = jax.random.uniform(jax.random.fold_in(jax.random.fold_in(rng, 6), dim), (shards_of,), jnp.float32, smallest / len(shards), largest / len(shards))
        gain = gain * jnp.repeat(jnp.exp(heights), shape[dim] // shards_of).reshape((-1,) + (1,) * (len(shape) - 1 - dim))
    return gain


def normal_values(rng, shape, spread, bound, shards=(), kind=jnp.bfloat16):
    level = levels(rng, shape, shards, -0.22, 0.18) if shards else 1.0
    drawn = jax.random.normal(rng, shape, jnp.float32) * spread * level
    return jnp.minimum(jnp.maximum(drawn, -bound), bound).astype(kind)


def setup_inputs(seed: int = 0) -> dict:
    splits = jax.random.split(jax.random.key(seed), 12)
    temp = normal_values(splits[0], (LEVELS, GRID_Y, GRID_X), 1.0, 6.0, ((1, 8), (2, 16)), jnp.float32)
    salt = jnp.clip(32.0 + 4.0 * jax.random.uniform(splits[1], (LEVELS, GRID_Y, GRID_X), jnp.float32) ** levels(splits[1], (LEVELS, GRID_Y, GRID_X), ((1, 8), (2, 16)), -0.2, 0.2), 32.0, 36.0)
    east_vel = jnp.clip(jax.random.uniform(splits[2], (LEVELS, GRID_Y, GRID_X), jnp.float32, -0.2, 0.2) * levels(splits[2], (LEVELS, GRID_Y, GRID_X), ((1, 8), (2, 16)), -0.4, 0.0), -0.2, 0.2)
    north_vel = jnp.clip(jax.random.uniform(splits[3], (LEVELS, GRID_Y, GRID_X), jnp.float32, -0.2, 0.2) * levels(splits[3], (LEVELS, GRID_Y, GRID_X), ((1, 8), (2, 16)), -0.4, 0.0), -0.2, 0.2)
    land_mask = place_ends((jax.random.randint(splits[4], (GRID_Y, GRID_X), 0, 16) < 15).astype(jnp.int32), jax.random.fold_in(splits[4], 1), 0, 1)
    ice_mask = place_ends((jax.random.randint(splits[5], (GRID_Y, GRID_X), 0, 16) < 15).astype(jnp.int32), jax.random.fold_in(splits[5], 1), 0, 1)
    ice_u = normal_values(splits[6], (GRID_Y, GRID_X), 0.5, 3.0, ((0, 8), (1, 16)), jnp.float32)
    ice_v = normal_values(splits[7], (GRID_Y, GRID_X), 0.5, 3.0, ((0, 8), (1, 16)), jnp.float32)
    ice_pressure_field = jnp.clip(jnp.exp(math.log(3.0) - 1.0986123 * jax.random.uniform(splits[8], (GRID_Y, GRID_X), jnp.float32) ** levels(splits[8], (GRID_Y, GRID_X), ((0, 8), (1, 16)), -0.2, 0.2)), 1.0, 3.0)
    wind_x = normal_values(splits[9], (GRID_Y, GRID_X), 0.5, 3.0, ((0, 8), (1, 16)), jnp.float32)
    wind_y = normal_values(splits[10], (GRID_Y, GRID_X), 0.5, 3.0, ((0, 8), (1, 16)), jnp.float32)
    return {"temp": temp, "salt": salt, "east_vel": east_vel, "north_vel": north_vel, "land_mask": land_mask, "ice_mask": ice_mask, "ice_u": ice_u, "ice_v": ice_v, "ice_pressure_field": ice_pressure_field, "wind_x": wind_x, "wind_y": wind_y}


TIME_STEP = 1.0
RELAX_RATE = 2.0
ELLIPSE_SQ = 4.0
DELTA_FLOOR = 0.25
MOMENTUM_STEP = 0.5
WATER_DRAG = 1.0
CORIOLIS_SCALE = 0.5
HEAT_RATE = 0.1
SALT_RATE = 0.5
FREEZE_SLOPE = 0.054

def advect(tracers, east_face, north_face, ocean_pad):
    face_x = ocean_pad[1:-1, :-1] * ocean_pad[1:-1, 1:]
    face_y = ocean_pad[:-1, 1:-1] * ocean_pad[1:, 1:-1]
    east_part = east_face[..., 1:-1, :-1]
    north_part = north_face[..., :-1, 1:-1]
    flux_x = east_part * jnp.where(east_part > 0, tracers[..., 1:-1, :-1], tracers[..., 1:-1, 1:]) * face_x
    flux_y = north_part * jnp.where(north_part > 0, tracers[..., :-1, 1:-1], tracers[..., 1:, 1:-1]) * face_y
    return tracers[..., 1:-1, 1:-1] - TIME_STEP * (flux_x[..., 1:] - flux_x[..., :-1] + (flux_y[..., 1:, :] - flux_y[..., :-1, :]))

def strain_rates(padded_eastward_velocity, padded_northward_velocity):
    dudx = (padded_eastward_velocity[1:-1, 2:] - padded_eastward_velocity[1:-1, :-2]) * 0.5
    dudy = (padded_eastward_velocity[2:, 1:-1] - padded_eastward_velocity[:-2, 1:-1]) * 0.5
    northward_velocity_xgrad = (padded_northward_velocity[1:-1, 2:] - padded_northward_velocity[1:-1, :-2]) * 0.5
    northward_velocity_ygrad = (padded_northward_velocity[2:, 1:-1] - padded_northward_velocity[:-2, 1:-1]) * 0.5
    return (dudx + northward_velocity_ygrad, dudx - northward_velocity_ygrad, dudy + northward_velocity_xgrad)

def stress_tensor(stress_old, strain, strength, covered_region):
    diverge, tension, shearing = strain
    delta = jnp.sqrt(diverge * diverge + (tension * tension + shearing * shearing) / ELLIPSE_SQ + DELTA_FLOOR)
    zeta = strength / (2.0 * delta)
    first = (stress_old[0] + RELAX_RATE * (2.0 * zeta * diverge - strength)) / (1.0 + RELAX_RATE) * covered_region
    second = (stress_old[1] + RELAX_RATE * (2.0 * zeta * tension / ELLIPSE_SQ)) / (1.0 + RELAX_RATE) * covered_region
    third = (stress_old[2] + RELAX_RATE * (zeta * shearing / ELLIPSE_SQ)) / (1.0 + RELAX_RATE) * covered_region
    return (first, second, third)

def momentum(ice_east, northward_ice_velocity, stress_pad, forcing, coriolis, covered_region):
    sxx = 0.5 * (stress_pad[0] + stress_pad[1])
    syy = 0.5 * (stress_pad[0] - stress_pad[1])
    sxy = stress_pad[2]
    force_x = (sxx[1:-1, 2:] - sxx[1:-1, :-2]) * 0.5 + (sxy[2:, 1:-1] - sxy[:-2, 1:-1]) * 0.5
    force_y = (sxy[1:-1, 2:] - sxy[1:-1, :-2]) * 0.5 + (syy[2:, 1:-1] - syy[:-2, 1:-1]) * 0.5
    wind_east, wind_north, ocean_u, ocean_v = forcing
    right_u = ice_east + MOMENTUM_STEP * (force_x + wind_east + WATER_DRAG * ocean_u)
    right_v = northward_ice_velocity + MOMENTUM_STEP * (force_y + wind_north + WATER_DRAG * ocean_v)
    diagonal = 1.0 + MOMENTUM_STEP * WATER_DRAG
    turning = MOMENTUM_STEP * coriolis
    determ = diagonal * diagonal + turning * turning
    new_east = (diagonal * right_u + turning * right_v) / determ * covered_region
    new_north = (diagonal * right_v - turning * right_u) / determ * covered_region
    return (new_east, new_north)

def wall_pad(values):
    padded = jnp.pad(values, [(0, 0)] * (values.ndim - 2) + [(1, 1), (0, 0)])
    return jnp.concatenate([padded[..., -1:], padded, padded[..., :1]], axis=-1)

def tripole_seam_padding(values, fold_sign, rim_depth):
    top_rows = fold_sign * values[GRID_Y - rim_depth:, :][::-1, ::-1]
    bottom = jnp.zeros((rim_depth, values.shape[1]), values.dtype)
    stacked = jnp.concatenate([bottom, values, top_rows], axis=0)
    return jnp.concatenate([stacked[:, -rim_depth:], stacked, stacked[:, :rim_depth]], axis=1)

def reference(temp, salt, east_vel, north_vel, land_mask, ice_mask, ice_u, ice_v, ice_pressure_field, wind_x, wind_y):
    ocean_cells = land_mask.astype(jnp.float32)
    covered_region = ocean_cells * ice_mask.astype(jnp.float32)
    ocean_pad = wall_pad(ocean_cells)
    moved_temp = []
    moved_salt = []
    for layer_index in range(LEVELS):
        tracers = wall_pad(jnp.stack([temp[layer_index], salt[layer_index]]))
        result = advect(tracers, wall_pad(east_vel[layer_index]), wall_pad(north_vel[layer_index]), ocean_pad)
        moved_temp.append(result[0])
        moved_salt.append(result[1])
    moved_temp = jnp.stack(moved_temp)
    moved_salt = jnp.stack(moved_salt)
    surface_t = moved_temp[0]
    surface_s = moved_salt[0]
    ocean_u = east_vel[0]
    ocean_v = north_vel[0]
    global_rows = jnp.arange(GRID_Y, dtype=jnp.int32)
    coriolis = CORIOLIS_SCALE * (2 * global_rows + 1 - GRID_Y).astype(jnp.float32)[:, None] / GRID_Y
    forcing = (wind_x, wind_y, ocean_u, ocean_v)
    ice_east = ice_u * covered_region
    northward_ice_velocity = ice_v * covered_region
    zero_field = jnp.zeros_like(ice_east)
    current_stress = (zero_field, zero_field, zero_field)
    for subcycle in range(SUBCYCLES):
        padded_eastward_velocity = tripole_seam_padding(ice_east, -1.0, 1)
        padded_northward_velocity = tripole_seam_padding(northward_ice_velocity, -1.0, 1)
        current_stress = stress_tensor(current_stress, strain_rates(padded_eastward_velocity, padded_northward_velocity), ice_pressure_field, covered_region)
        stress_pad = jnp.stack([tripole_seam_padding(member, 1.0, 1) for member in current_stress])
        ice_east, northward_ice_velocity = momentum(ice_east, northward_ice_velocity, stress_pad, forcing, coriolis, covered_region)
    slip_u = ice_east - ocean_u
    slip_v = northward_ice_velocity - ocean_v
    heat = HEAT_RATE * covered_region * (1.0 + WATER_DRAG * (slip_u * slip_u + slip_v * slip_v)) * (surface_t + FREEZE_SLOPE * surface_s)
    temp_out = moved_temp.at[0].set(surface_t - heat)
    salt_out = moved_salt.at[0].set(surface_s - SALT_RATE * heat)
    return (temp_out, salt_out, ice_east, northward_ice_velocity)
```

```python
import functools

import jax
import jax.numpy as jnp
from jax import lax
from jax.experimental import pallas as pl
from jax.experimental.pallas import tpu as pltpu
from jax.sharding import PartitionSpec as P

SUBCYCLES = 4
LANES = 128
HALO = 2 * SUBCYCLES
PAD = 16
MESH = pl.DeviceIdType.MESH
F32 = jnp.float32


def lane_iota():
    return lax.broadcasted_iota(jnp.int32, (8, LANES), 1)


def rows8(k, first=0):
    return pl.ds(pl.multiple_of(k * 8 + first, 8), 8)


def loop(count, body):
    def step(k, carry):
        body(k)
        return carry

    lax.fori_loop(0, count, step, 0)


def from_east(tiles, lane):
    rolled = [pltpu.roll(a, LANES - 1, 1) for a in tiles]
    n = len(tiles)
    return [jnp.where(lane == LANES - 1, rolled[(t + 1) % n], rolled[t]) for t in range(n)]


def from_west(tiles, lane):
    rolled = [pltpu.roll(a, 1, 1) for a in tiles]
    n = len(tiles)
    return [jnp.where(lane == 0, rolled[(t - 1) % n], rolled[t]) for t in range(n)]


def ocean_kernel(
    levels, rows, lat_count, lon_count,
    temp, salt, east, north, land, icem, ice_u, ice_v, press, wind_x, wind_y,
    moved, ext,
    tr, ev, nv, sea, icb, uvw, face_x, face_y,
    own_e, own_w, got_w, got_e, flux, ice_e, ice_w, igot_w, igot_e, fold,
    local_sem, send_sem, recv_sem,
):
    n_tiles = rows // 8
    lat = lax.axis_index("lat")
    lon = lax.axis_index("lon")
    lon_e = lax.rem(lon + 1, lon_count)
    lon_w = lax.rem(lon + lon_count - 1, lon_count)
    top = lat == lat_count - 1
    bottom = lat == 0
    mirror = lon_count - 1 - lon
    north_dev = (jnp.where(top, lat, lat + 1), jnp.where(top, mirror, lon))

    def dev(la, lo):
        return {"lat": la, "lon": lo}

    barrier = pltpu.get_barrier_semaphore()
    for lo in (lon_w, lon_e):
        pl.semaphore_signal(barrier, inc=1, device_id=dev(lat, lo), device_id_type=MESH)
    pl.semaphore_signal(barrier, inc=1, device_id=dev(*north_dev), device_id_type=MESH)

    @pl.when(jnp.logical_not(bottom))
    def _():
        pl.semaphore_signal(barrier, inc=1, device_id=dev(lat - 1, lon), device_id_type=MESH)

    started = []

    def load(src, dst):
        copy = pltpu.make_async_copy(src, dst, local_sem.at[len(started)])
        copy.start()
        started.append(copy)
        return copy

    def cols(t):
        return pl.ds(t * LANES, LANES)

    ice_loads = []
    for t in range(2):
        ice_loads += [
            load(land.at[:, cols(t)], sea.at[t, pl.ds(8, rows), :]),
            load(icem.at[:, cols(t)], icb.at[t]),
            load(ice_u.at[:, cols(t)], uvw.at[0, t]),
            load(ice_v.at[:, cols(t)], uvw.at[1, t]),
            load(wind_x.at[:, cols(t)], uvw.at[2, t]),
            load(wind_y.at[:, cols(t)], uvw.at[3, t]),
            load(press.at[:, cols(t)], ext.at[2, t, pl.ds(PAD, rows), :]),
        ]
    level_loads = []
    for l in range(levels):
        mine = []
        for t in range(2):
            mine += [
                load(east.at[l, :, cols(t)], ev.at[l, t]),
                load(north.at[l, :, cols(t)], nv.at[l, t, pl.ds(8, rows), :]),
                load(temp.at[l, :, cols(t)], tr.at[0, l, t, pl.ds(8, rows), :]),
                load(salt.at[l, :, cols(t)], tr.at[1, l, t, pl.ds(8, rows), :]),
            ]
        level_loads.append(mine)

    lane = lane_iota()
    zero = jnp.zeros((8, LANES), F32)

    @pl.when(bottom)
    def _():
        for t in range(2):
            sea[t, pl.ds(0, 8), :] = jnp.zeros((8, LANES), jnp.int32)
            for l in range(levels):
                nv[l, t, pl.ds(0, 8), :] = zero
                for c in range(2):
                    tr[c, l, t, pl.ds(0, 8), :] = zero
        for f in range(6):
            for t in range(3):
                ext[f, t, pl.ds(PAD - 8, 8), :] = zero

    @pl.when(top)
    def _():
        for t in range(2):
            sea[t, pl.ds(rows + 8, 8), :] = jnp.zeros((8, LANES), jnp.int32)
            for l in range(levels):
                for c in range(2):
                    tr[c, l, t, pl.ds(rows + 8, 8), :] = zero

    pl.semaphore_wait(barrier, jnp.where(bottom, 3, 4))

    def remote(i, src, dst, device, arrival=None):
        return pltpu.make_async_remote_copy(
            src_ref=src, dst_ref=dst, send_sem=send_sem.at[i],
            recv_sem=recv_sem.at[i if arrival is None else arrival],
            device_id=device, device_id_type=MESH,
        )

    last = pl.ds(rows - 8, 8)
    first = pl.ds(0, 8)
    above = pl.ds(rows + 8, 8)
    going_north, going_south = [], []
    index = 0
    for t in range(2):
        for src, dst in (
            (temp.at[:, last, cols(t)], tr.at[0, :, t, first, :]),
            (salt.at[:, last, cols(t)], tr.at[1, :, t, first, :]),
            (north.at[:, last, cols(t)], nv.at[:, t, first, :]),
            (land.at[last, cols(t)], sea.at[t, first, :]),
        ):
            going_north.append(remote(index, src, dst, dev(*north_dev)))
            index += 1
        for src, dst in (
            (temp.at[:, first, cols(t)], tr.at[0, :, t, above, :]),
            (salt.at[:, first, cols(t)], tr.at[1, :, t, above, :]),
            (land.at[first, cols(t)], sea.at[t, above, :]),
        ):
            going_south.append(
                remote(index, src, dst, dev(jnp.where(bottom, lat, lat - 1), lon))
            )
            index += 1

    @pl.when(jnp.logical_not(top))
    def _():
        for copy in going_north:
            copy.start()

    @pl.when(jnp.logical_not(bottom))
    def _():
        for copy in going_south:
            copy.start()

    for copy in ice_loads:
        copy.wait()
    for i in (0, 1, 4, 5):
        level_loads[0][i].wait()

    def ice_fields(k):
        here = rows8(k)
        out = rows8(k, PAD)
        fields = []
        for t in range(2):
            covered = (sea[t, rows8(k, 8), :] * icb[t, here, :]).astype(F32)
            u = uvw[0, t, here, :] * covered
            v = uvw[1, t, here, :] * covered
            fx = 0.5 * (uvw[2, t, here, :] + ev[0, t, here, :])
            fy = 0.5 * (uvw[3, t, here, :] + nv[0, t, rows8(k, 8), :])
            p = ext[2, t, out, :]
            ext[0, t, out, :] = u
            ext[1, t, out, :] = v
            ext[3, t, out, :] = fx
            ext[4, t, out, :] = fy
            ext[5, t, out, :] = covered
            fields.append((u, v, p, fx, fy, covered))
        return fields

    def pack_ice(k):
        pack_e, pack_w = zero, zero
        for h in range(2):
            fields = ice_fields(k + h * (n_tiles // 2))
            for f in range(6):
                base = h * 64 + f * 8
                here = (lane >= base) & (lane < base + 8)
                pack_e = jnp.where(
                    here, pltpu.roll(fields[1][f], (base - (LANES - 8)) % LANES, 1), pack_e
                )
                west = fields[0][f]
                pack_w = jnp.where(here, pltpu.roll(west, base, 1) if base else west, pack_w)
        ice_e[rows8(k), :] = pack_e
        ice_w[rows8(k), :] = pack_w

    loop(n_tiles // 2, pack_ice)
    send_ice_e = remote(index, ice_e, igot_w, dev(lat, lon_e))
    send_ice_w = remote(index + 1, ice_w, igot_e, dev(lat, lon_w))
    index += 2
    send_ice_e.start()
    send_ice_w.start()

    for l in range(levels):
        for i, copy in enumerate(level_loads[l]):
            if l or i not in (0, 1, 4, 5):
                copy.wait()

    def pack_edges(k):
        e0, e1, w0, w1 = zero, zero, zero, zero
        for q in range(4):
            kk = k + q * (n_tiles // 4)
            here, padded = rows8(kk), rows8(kk, 8)
            sea_e = sea[1, padded, pl.ds(LANES - 1, 1)].astype(F32)
            sea_w = sea[0, padded, pl.ds(0, 1)].astype(F32)
            w1 = jnp.where(lane >= 32 * q, jnp.broadcast_to(sea_w, (8, LANES)), w1)
            for l in range(levels):
                speed = jnp.broadcast_to(
                    ev[l, 1, here, pl.ds(LANES - 1, 1)] * sea_e, (8, LANES)
                )
                for c in range(2):
                    j = 32 * q + c * levels + l
                    e0 = jnp.where(
                        lane == j,
                        jnp.broadcast_to(tr[c, l, 1, padded, pl.ds(LANES - 1, 1)], (8, LANES)),
                        e0,
                    )
                    w0 = jnp.where(
                        lane == j,
                        jnp.broadcast_to(tr[c, l, 0, padded, pl.ds(0, 1)], (8, LANES)),
                        w0,
                    )
                    e1 = jnp.where(lane == j, speed, e1)
        own_e[0, rows8(k), :] = e0
        own_e[1, rows8(k), :] = e1
        own_w[0, rows8(k), :] = w0
        own_w[1, rows8(k), :] = w1

    loop(n_tiles // 4, pack_edges)
    send_edge_e = remote(index, own_e, got_w, dev(lat, lon_e))
    send_edge_w = remote(index + 1, own_w, got_e, dev(lat, lon_w))
    index += 2
    send_edge_e.start()
    send_edge_w.start()

    @pl.when(jnp.logical_not(bottom))
    def _():
        for copy in going_north:
            copy.wait_recv()

    @pl.when(jnp.logical_not(top))
    def _():
        for copy in going_south:
            copy.wait_recv()

    def faces(k):
        here = rows8(k)
        s = [sea[t, here, :].astype(F32) for t in range(2)]
        for t in range(2):
            up = sea[t, pl.ds(k * 8 + 1, 8), :].astype(F32)
            face_y[t, here, :] = s[t] * up
        se = from_east(s, lane)
        face_x[0, here, :] = s[0] * se[0]
        face_x[1, here, :] = jnp.where(lane == LANES - 1, 0.0, s[1] * se[1])

    loop(n_tiles + 1, faces)

    def advect(l):
        def body(k):
            here, mid = rows8(k), rows8(k, 8)
            below, over = pl.ds(k * 8 + 7, 8), pl.ds(k * 8 + 9, 8)
            ep, en, np_, nn, sp, sn = [], [], [], [], [], []
            for t in range(2):
                e = ev[l, t, here, :] * face_x[t, mid, :]
                n = nv[l, t, mid, :] * face_y[t, mid, :]
                s = nv[l, t, below, :] * face_y[t, below, :]
                for value, plus, minus in ((e, ep, en), (n, np_, nn), (s, sp, sn)):
                    plus.append(jnp.maximum(value, 0.0))
                    minus.append(jnp.minimum(value, 0.0))
            for c in range(2):
                x = [tr[c, l, t, mid, :] for t in range(2)]
                xe = from_east(x, lane)
                fe = [ep[t] * x[t] + en[t] * xe[t] for t in range(2)]
                fw = from_west(fe, lane)
                for t in range(2):
                    fn = np_[t] * x[t] + nn[t] * tr[c, l, t, over, :]
                    fs = sp[t] * tr[c, l, t, below, :] + sn[t] * x[t]
                    moved[c, l, t, here, :] = x[t] - ((fe[t] - fw[t]) + (fn - fs))

        loop(n_tiles, body)

    for l in range(levels // 2):
        advect(l)

    send_ice_e.wait_recv()
    send_ice_w.wait_recv()

    def unpack_ice(k):
        east_side, west_side = igot_e[rows8(k), :], igot_w[rows8(k), :]
        for h in range(2):
            for f in range(6):
                base = h * 64 + f * 8
                a = pltpu.roll(east_side, LANES - base, 1) if base else east_side
                b = pltpu.roll(west_side, (LANES - 8 - base) % LANES, 1)
                value = jnp.where(lane < 8, a, jnp.where(lane >= LANES - 8, b, 0.0))
                ext[f, 2, rows8(k + h * (n_tiles // 2), PAD), :] = value

    loop(n_tiles // 2, unpack_ice)

    top_rows = pl.ds(PAD + rows - HALO, HALO)
    low_rows = pl.ds(PAD, HALO)
    north_guard = pl.ds(PAD + rows, HALO)
    south_guard = pl.ds(PAD - HALO, HALO)
    send_n = remote(index, ext.at[:, :, top_rows, :], ext.at[:, :, south_guard, :], dev(*north_dev))
    send_s = remote(
        index + 1, ext.at[:, :, low_rows, :], ext.at[:, :, north_guard, :],
        dev(jnp.where(bottom, lat, lat - 1), lon),
    )
    send_fold = remote(
        index, fold, ext.at[:, :, north_guard, :], dev(*north_dev), arrival=index + 1
    )

    @pl.when(top)
    def _():
        back = LANES - 1 - lane
        for f in range(6):
            sign = -1.0 if f in (0, 1, 3, 4) else 1.0
            for t in range(3):
                block = ext[f, t, top_rows, :]
                turned = jnp.concatenate([block[r : r + 1] for r in range(HALO - 1, -1, -1)], axis=0)
                turned = jnp.take_along_axis(turned, back, axis=1)
                fold[f, (1, 0, 2)[t], :, :] = sign * turned
        send_fold.start()

    @pl.when(jnp.logical_not(top))
    def _():
        send_n.start()

    @pl.when(jnp.logical_not(bottom))
    def _():
        send_s.start()

    for l in range(levels // 2, levels):
        advect(l)

    send_edge_e.wait_recv()
    send_edge_w.wait_recv()

    def edge_flux(k):
        here = rows8(k)
        e = got_w[1, here, :] * own_w[1, here, :]
        flux[0, here, :] = e * jnp.where(e > 0, got_w[0, here, :], own_w[0, here, :])
        e = own_e[1, here, :] * got_e[1, here, :]
        flux[1, here, :] = e * jnp.where(e > 0, own_e[0, here, :], got_e[0, here, :])

    loop(n_tiles // 4, edge_flux)

    def edge_update(k):
        fw, fe = flux[0, rows8(k), :], flux[1, rows8(k), :]
        for q in range(4):
            here = rows8(k + q * (n_tiles // 4))
            for c in range(2):
                for l in range(levels):
                    j = 32 * q + c * levels + l
                    a = pltpu.roll(fw, LANES - j, 1) if j else fw
                    b = pltpu.roll(fe, LANES - 1 - j, 1)
                    moved[c, l, 0, here, :] += jnp.where(lane == 0, a, 0.0)
                    moved[c, l, 1, here, :] -= jnp.where(lane == LANES - 1, b, 0.0)

    loop(n_tiles // 4, edge_update)

    @pl.when(jnp.logical_not(bottom))
    def _():
        send_n.wait_recv()
        for copy in going_south:
            copy.wait_send()
        send_s.wait_send()

    @pl.when(jnp.logical_not(top))
    def _():
        for copy in going_north:
            copy.wait_send()
        send_n.wait_send()

    @pl.when(top)
    def _():
        send_fold.wait_send()

    send_s.wait_recv()
    for copy in (send_ice_e, send_ice_w, send_edge_e, send_edge_w):
        copy.wait_send()


N_REMOTE = 20
N_ICE_LOADS = 14


def ice_kernel(
    levels, rows, lat_count,
    moved, ext, east, north,
    temp_out, salt_out, u_out, v_out,
    vel, stress, turn, surf, water,
    load_sem, store_sem,
):
    n_ext = (rows + 2 * HALO) // 8
    n_tiles = rows // 8
    lat = lax.axis_index("lat")
    lane = lane_iota()
    grid_rows = rows * lat_count

    def cols(t):
        return pl.ds(t * LANES, LANES)

    loads, stores = [], []
    for i, src in enumerate((east, north)):
        for t in range(2):
            copy = pltpu.make_async_copy(
                src.at[0, :, cols(t)], water.at[i, t], load_sem.at[2 * i + t]
            )
            copy.start()
            loads.append(copy)

    def store(src, dst):
        copy = pltpu.make_async_copy(src, dst, store_sem.at[len(stores)])
        copy.start()
        stores.append(copy)

    for l in range(1, levels):
        for c, dst in enumerate((temp_out, salt_out)):
            for t in range(2):
                store(moved.at[c, l, t], dst.at[l, :, cols(t)])

    def turning(k):
        g = lat * rows - HALO + k * 8 + lax.broadcasted_iota(jnp.int32, (8, LANES), 0)
        g = jnp.where(g >= grid_rows, 2 * grid_rows - 1 - g, g)
        coriolis = 0.5 * (2 * g + 1 - grid_rows).astype(F32) / grid_rows
        b = 0.5 * coriolis
        inverse = 1.0 / (2.25 + b * b)
        turn[0, rows8(k), :] = 1.5 * inverse
        turn[1, rows8(k), :] = b * inverse

    loop(n_ext, turning)

    def stresses(src, fresh):
        def body(k):
            mid = rows8(k, 8)
            below, over = pl.ds(k * 8 + 7, 8), pl.ds(k * 8 + 9, 8)
            u = [src[0, t, mid, :] for t in range(3)]
            v = [src[1, t, mid, :] for t in range(3)]
            ue, uw = from_east(u, lane), from_west(u, lane)
            ve, vw = from_east(v, lane), from_west(v, lane)
            for t in range(3):
                dudx, dvdx = ue[t] - uw[t], ve[t] - vw[t]
                dudy = src[0, t, over, :] - src[0, t, below, :]
                dvdy = src[1, t, over, :] - src[1, t, below, :]
                div, ten, shr = dudx + dvdy, dudx - dvdy, dudy + dvdx
                p = ext[2, t, mid, :]
                third = ext[5, t, mid, :] * (1.0 / 3.0)
                zeta = p * lax.rsqrt(div * div + 0.25 * (ten * ten + shr * shr) + 1.0)
                quarter = 0.25 * zeta
                a = zeta * div - p
                b = quarter * ten
                sxx, syy, sxy = a + b, a - b, quarter * shr
                if not fresh:
                    sxx = stress[0, t, mid, :] + sxx
                    syy = stress[1, t, mid, :] + syy
                    sxy = stress[2, t, mid, :] + sxy
                stress[0, t, mid, :] = sxx * third
                stress[1, t, mid, :] = syy * third
                stress[2, t, mid, :] = sxy * third

        loop(n_ext, body)

    def momentum(src, k, first, tiles):
        mid = rows8(k, first)
        below, over = pl.ds(k * 8 + first - 1, 8), pl.ds(k * 8 + first + 1, 8)
        sxx = [stress[0, t, mid, :] for t in range(3)]
        sxy = [stress[2, t, mid, :] for t in range(3)]
        xxe, xxw = from_east(sxx, lane), from_west(sxx, lane)
        xye, xyw = from_east(sxy, lane), from_west(sxy, lane)
        a, b = turn[0, rows8(k, first - 8), :], turn[1, rows8(k, first - 8), :]
        out = []
        for t in range(tiles):
            fx = (xxe[t] - xxw[t]) + (stress[2, t, over, :] - stress[2, t, below, :])
            fy = (xye[t] - xyw[t]) + (stress[1, t, over, :] - stress[1, t, below, :])
            ru = src[0, t, mid, :] + (0.25 * fx + ext[3, t, mid, :])
            rv = src[1, t, mid, :] + (0.25 * fy + ext[4, t, mid, :])
            covered = ext[5, t, mid, :]
            out.append(((a * ru + b * rv) * covered, (a * rv - b * ru) * covered))
        return out

    src = ext
    for subcycle in range(SUBCYCLES - 1):
        stresses(src, subcycle == 0)

        def body(k, src=src):
            for t, (u, v) in enumerate(momentum(src, k, 8, 3)):
                vel[0, t, rows8(k, 8), :] = u
                vel[1, t, rows8(k, 8), :] = v

        loop(n_ext, body)
        src = vel
    stresses(src, False)
    for copy in loads:
        copy.wait()

    def final(k):
        here = rows8(k)
        for t, (u, v) in enumerate(momentum(vel, k, PAD, 2)):
            vel[0, t, rows8(k, PAD), :] = u
            vel[1, t, rows8(k, PAD), :] = v
            slip_u = u - water[0, t, here, :]
            slip_v = v - water[1, t, here, :]
            sst, sss = moved[0, 0, t, here, :], moved[1, 0, t, here, :]
            heat = (
                0.1 * ext[5, t, rows8(k, PAD), :]
                * (1.0 + (slip_u * slip_u + slip_v * slip_v))
                * (sst + 0.054 * sss)
            )
            surf[0, t, here, :] = sst - heat
            surf[1, t, here, :] = sss - 0.5 * heat

    loop(n_tiles, final)
    for t in range(2):
        store(vel.at[0, t, pl.ds(PAD, rows), :], u_out.at[:, cols(t)])
        store(vel.at[1, t, pl.ds(PAD, rows), :], v_out.at[:, cols(t)])
        store(surf.at[0, t], temp_out.at[0, :, cols(t)])
        store(surf.at[1, t], salt_out.at[0, :, cols(t)])
    for copy in stores:
        copy.wait()


def per_device(lat_count, lon_count, *args):
    temp = args[0]
    levels, rows, _ = temp.shape
    any_space = pl.BlockSpec(memory_space=pl.ANY)
    vmem_space = pl.BlockSpec(memory_space=pltpu.VMEM)
    deep = rows + 2 * PAD
    moved, ext = pl.pallas_call(
        functools.partial(ocean_kernel, levels, rows, lat_count, lon_count),
        out_shape=(
            pltpu.VMEM((2, levels, 2, rows, LANES), F32),
            pltpu.VMEM((6, 3, deep, LANES), F32),
        ),
        in_specs=[any_space] * 11,
        out_specs=(vmem_space, vmem_space),
        scratch_shapes=[
            pltpu.VMEM((2, levels, 2, rows + 16, LANES), F32),
            pltpu.VMEM((levels, 2, rows, LANES), F32),
            pltpu.VMEM((levels, 2, rows + 8, LANES), F32),
            pltpu.VMEM((2, rows + 16, LANES), jnp.int32),
            pltpu.VMEM((2, rows, LANES), jnp.int32),
            pltpu.VMEM((4, 2, rows, LANES), F32),
            pltpu.VMEM((2, rows + 8, LANES), F32),
            pltpu.VMEM((2, rows + 8, LANES), F32),
        ]
        + [pltpu.VMEM((2, rows // 4, LANES), F32)] * 5
        + [pltpu.VMEM((rows // 2, LANES), F32)] * 4
        + [
            pltpu.VMEM((6, 3, HALO, LANES), F32),
            pltpu.SemaphoreType.DMA((N_ICE_LOADS + 8 * levels,)),
            pltpu.SemaphoreType.DMA((N_REMOTE,)),
            pltpu.SemaphoreType.DMA((N_REMOTE,)),
        ],
        compiler_params=pltpu.CompilerParams(
            collective_id=0, has_side_effects=True, vmem_limit_bytes=48 * 1024 * 1024
        ),
        name="ocean",
    )(*args)
    moved = pltpu.with_memory_space_constraint(moved, pltpu.VMEM)
    ext = pltpu.with_memory_space_constraint(ext, pltpu.VMEM)
    shapes = (temp, temp, args[6], args[6])
    return pl.pallas_call(
        functools.partial(ice_kernel, levels, rows, lat_count),
        out_shape=tuple(jax.ShapeDtypeStruct(a.shape, a.dtype) for a in shapes),
        in_specs=[vmem_space, vmem_space, any_space, any_space],
        out_specs=(any_space,) * 4,
        scratch_shapes=[
            pltpu.VMEM((2, 3, deep, LANES), F32),
            pltpu.VMEM((3, 3, deep, LANES), F32),
            pltpu.VMEM((2, deep, LANES), F32),
            pltpu.VMEM((2, 2, rows, LANES), F32),
            pltpu.VMEM((2, 2, rows, LANES), F32),
            pltpu.SemaphoreType.DMA((4,)),
            pltpu.SemaphoreType.DMA((4 * (levels - 1) + 8,)),
        ],
        compiler_params=pltpu.CompilerParams(vmem_limit_bytes=48 * 1024 * 1024),
        name="ice",
    )(moved, ext, args[2], args[3])


def solution(mesh):
    deep, flat = P(None, "lat", "lon"), P("lat", "lon")
    return jax.shard_map(
        functools.partial(per_device, mesh.shape["lat"], mesh.shape["lon"]),
        mesh=mesh,
        in_specs=(deep,) * 4 + (flat,) * 7,
        out_specs=(deep, deep, flat, flat),
        check_vma=False,
    )
```

```python
import functools

import jax
import jax.numpy as jnp
from jax import lax
from jax.experimental import pallas as pl
from jax.experimental.pallas import tpu as pltpu
from jax.sharding import PartitionSpec as P

SUBCYCLES = 4
LANES = 128
HALO = 2 * SUBCYCLES
PAD = 16
MESH = pl.DeviceIdType.MESH
F32 = jnp.float32


def lane_iota(rows=8):
    return lax.broadcasted_iota(jnp.int32, (rows, LANES), 1)


ICE_ROWS = 400
LAST_ROWS = 384
PACK_ROWS = 384
FACE_ROWS = 392
EDGE_ROWS = 96
FLOW_ROWS = 384


def block(total, most):
    return max(n for n in range(8, most + 1, 8) if total % n == 0)


def rows8(k, first=0, count=8):
    return pl.ds(pl.multiple_of(k * count + first, 8), count)


def loop(count, body):
    def step(k, carry):
        body(k)
        return carry

    lax.fori_loop(0, count, step, 0)


def from_east(tiles):
    rolled = [pltpu.roll(a, LANES - 1, 1) for a in tiles]
    n = len(tiles)
    lane = lane_iota(tiles[0].shape[0])
    return [jnp.where(lane == LANES - 1, rolled[(t + 1) % n], rolled[t]) for t in range(n)]


def from_west(tiles):
    rolled = [pltpu.roll(a, 1, 1) for a in tiles]
    n = len(tiles)
    lane = lane_iota(tiles[0].shape[0])
    return [jnp.where(lane == 0, rolled[(t - 1) % n], rolled[t]) for t in range(n)]


def ocean_kernel(
    levels, rows, lat_count, lon_count,
    temp, salt, east, north, land, icem, ice_u, ice_v, press, wind_x, wind_y,
    moved, ext,
    tr, ev, nv, sea, icb, uvw, face_x, face_y,
    own, got_w, got_e, ice_own, ice_got_w, ice_got_e, fold,
    local_sem, send_sem, recv_sem,
):
    pack_rows, face_rows = block(rows, PACK_ROWS), block(rows + 8, FACE_ROWS)
    edge_rows, flow_rows = block(rows // 4, EDGE_ROWS), block(rows, FLOW_ROWS)
    lat = lax.axis_index("lat")
    lon = lax.axis_index("lon")
    lon_e = lax.rem(lon + 1, lon_count)
    lon_w = lax.rem(lon + lon_count - 1, lon_count)
    top = lat == lat_count - 1
    bottom = lat == 0
    mirror = lon_count - 1 - lon
    north_dev = (jnp.where(top, lat, lat + 1), jnp.where(top, mirror, lon))

    def dev(la, lo):
        return {"lat": la, "lon": lo}

    barrier = pltpu.get_barrier_semaphore()
    for lo in (lon_w, lon_e):
        pl.semaphore_signal(barrier, inc=1, device_id=dev(lat, lo), device_id_type=MESH)
    pl.semaphore_signal(barrier, inc=1, device_id=dev(*north_dev), device_id_type=MESH)

    @pl.when(jnp.logical_not(bottom))
    def _():
        pl.semaphore_signal(barrier, inc=1, device_id=dev(lat - 1, lon), device_id_type=MESH)

    started = []

    def load(src, dst):
        copy = pltpu.make_async_copy(src, dst, local_sem.at[len(started)])
        copy.start()
        started.append(copy)
        return copy

    def cols(t):
        return pl.ds(t * LANES, LANES)

    ice_loads = []
    for t in range(2):
        ice_loads += [
            load(land.at[:, cols(t)], sea.at[t, pl.ds(8, rows), :]),
            load(icem.at[:, cols(t)], icb.at[t]),
            load(ice_u.at[:, cols(t)], uvw.at[0, t]),
            load(ice_v.at[:, cols(t)], uvw.at[1, t]),
            load(wind_x.at[:, cols(t)], uvw.at[2, t]),
            load(wind_y.at[:, cols(t)], uvw.at[3, t]),
            load(press.at[:, cols(t)], ext.at[2, t, pl.ds(PAD, rows), :]),
        ]
    level_loads = []
    for l in range(levels):
        mine = []
        for t in range(2):
            mine += [
                load(east.at[l, :, cols(t)], ev.at[l, t]),
                load(north.at[l, :, cols(t)], nv.at[l, t, pl.ds(8, rows), :]),
                load(temp.at[l, :, cols(t)], tr.at[0, l, t, pl.ds(8, rows), :]),
                load(salt.at[l, :, cols(t)], tr.at[1, l, t, pl.ds(8, rows), :]),
            ]
        level_loads.append(mine)

    lane = lane_iota()
    zero = jnp.zeros((8, LANES), F32)

    @pl.when(bottom)
    def _():
        for t in range(2):
            sea[t, pl.ds(0, 8), :] = jnp.zeros((8, LANES), jnp.int32)
            for l in range(levels):
                nv[l, t, pl.ds(0, 8), :] = zero
                for c in range(2):
                    tr[c, l, t, pl.ds(0, 8), :] = zero
        for f in range(6):
            for t in range(3):
                ext[f, t, pl.ds(PAD - 8, 8), :] = zero

    @pl.when(top)
    def _():
        for t in range(2):
            sea[t, pl.ds(rows + 8, 8), :] = jnp.zeros((8, LANES), jnp.int32)
            for l in range(levels):
                for c in range(2):
                    tr[c, l, t, pl.ds(rows + 8, 8), :] = zero

    pl.semaphore_wait(barrier, jnp.where(bottom, 3, 4))

    def remote(i, src, dst, device, arrival=None):
        return pltpu.make_async_remote_copy(
            src_ref=src, dst_ref=dst, send_sem=send_sem.at[i],
            recv_sem=recv_sem.at[i if arrival is None else arrival],
            device_id=device, device_id_type=MESH,
        )

    last = pl.ds(rows - 8, 8)
    first = pl.ds(0, 8)
    above = pl.ds(rows + 8, 8)
    going_north, going_south = [], []
    index = 0
    for t in range(2):
        for src, dst in (
            (temp.at[:, last, cols(t)], tr.at[0, :, t, first, :]),
            (salt.at[:, last, cols(t)], tr.at[1, :, t, first, :]),
            (north.at[:, last, cols(t)], nv.at[:, t, first, :]),
            (land.at[last, cols(t)], sea.at[t, first, :]),
        ):
            going_north.append(remote(index, src, dst, dev(*north_dev)))
            index += 1
        for src, dst in (
            (temp.at[:, first, cols(t)], tr.at[0, :, t, above, :]),
            (salt.at[:, first, cols(t)], tr.at[1, :, t, above, :]),
            (land.at[first, cols(t)], sea.at[t, above, :]),
        ):
            going_south.append(
                remote(index, src, dst, dev(jnp.where(bottom, lat, lat - 1), lon))
            )
            index += 1

    @pl.when(jnp.logical_not(top))
    def _():
        for copy in going_north:
            copy.start()

    @pl.when(jnp.logical_not(bottom))
    def _():
        for copy in going_south:
            copy.start()

    for copy in ice_loads:
        copy.wait()
    for i in (0, 1, 4, 5):
        level_loads[0][i].wait()

    def pack_ice(k):
        n = pack_rows
        here, mid, out = rows8(k, 0, n), rows8(k, 8, n), rows8(k, PAD, n)
        lanes = lane_iota(n)
        fields = []
        for t in range(2):
            covered = (sea[t, mid, :] * icb[t, here, :]).astype(F32)
            mine = (
                uvw[0, t, here, :] * covered,
                uvw[1, t, here, :] * covered,
                ext[2, t, out, :],
                0.5 * (uvw[2, t, here, :] + ev[0, t, here, :]),
                0.5 * (uvw[3, t, here, :] + nv[0, t, mid, :]),
                covered,
            )
            for f in (0, 1, 3, 4, 5):
                ext[f, t, out, :] = mine[f]
            fields.append(mine)
        packed = jnp.zeros((n, LANES), F32)
        for f in range(6):
            both = jnp.where(lanes < HALO, fields[0][f], fields[1][f])
            both = pltpu.roll(both, 16 * f + 8, 1)
            packed = jnp.where((lanes >= 16 * f) & (lanes < 16 * f + 16), both, packed)
        ice_own[here, :] = packed

    loop(rows // pack_rows, pack_ice)
    send_ice_e = remote(index, ice_own, ice_got_w, dev(lat, lon_e))
    send_ice_w = remote(index + 1, ice_own, ice_got_e, dev(lat, lon_w))
    index += 2
    send_ice_e.start()
    send_ice_w.start()

    @pl.when(jnp.logical_not(bottom))
    def _():
        for copy in going_north:
            copy.wait_recv()

    @pl.when(jnp.logical_not(top))
    def _():
        for copy in going_south:
            copy.wait_recv()

    def faces(k):
        n = face_rows
        here = rows8(k, 0, n)
        s = [sea[t, here, :].astype(F32) for t in range(2)]
        for t in range(2):
            up = sea[t, pl.ds(k * n + 1, n), :].astype(F32)
            face_y[t, here, :] = s[t] * up
        se = from_east(s)
        face_x[0, here, :] = s[0] * se[0]
        face_x[1, here, :] = jnp.where(lane_iota(n) == LANES - 1, 0.0, s[1] * se[1])

    loop((rows + 8) // face_rows, faces)

    def wait_level(l):
        for i, copy in enumerate(level_loads[l]):
            if l or i not in (0, 1, 4, 5):
                copy.wait()

    def pack_edges(k):
        n = edge_rows
        lanes = lane_iota(n)
        value, speed = jnp.zeros((n, LANES), F32), jnp.zeros((n, LANES), F32)
        for q in range(4):
            first_row = q * (rows // 4)
            here, mid = rows8(k, first_row, n), rows8(k, first_row + 8, n)
            sea_e = sea[1, mid, :].astype(F32)
            sea_w = sea[0, mid, pl.ds(0, 1)].astype(F32)
            for l in range(levels):
                for c in range(2):
                    j = 32 * q + 2 * (c * levels + l)
                    both = jnp.where(lanes == 0, tr[c, l, 0, mid, :], tr[c, l, 1, mid, :])
                    both = pltpu.roll(both, j + 1, 1)
                    value = jnp.where((lanes == j) | (lanes == j + 1), both, value)
                j = 32 * q + 2 * l
                pushed = pltpu.roll(ev[l, 1, here, :] * sea_e, j + 1, 1)
                speed = jnp.where(lanes == j, pushed, speed)
            odd = (lanes >= 32 * q) & (lanes < 32 * q + 32) & (lanes % 2 == 1)
            speed = jnp.where(odd, jnp.broadcast_to(sea_w, (n, LANES)), speed)
        again = pltpu.roll(speed, 2 * levels, 1)
        place = lanes % 32
        again = (place >= 2 * levels) & (place < 4 * levels) & (place % 2 == 0), again
        out = rows8(k, 0, n)
        own[0, out, :] = value
        own[1, out, :] = jnp.where(again[0], again[1], speed)

    def advect(l):
        def body(k):
            n_rows = flow_rows
            here, mid = rows8(k, 0, n_rows), rows8(k, 8, n_rows)
            below, over = pl.ds(k * n_rows + 7, n_rows), pl.ds(k * n_rows + 9, n_rows)
            ep, en, np_, nn, sp, sn = [], [], [], [], [], []
            for t in range(2):
                e = ev[l, t, here, :] * face_x[t, mid, :]
                n = nv[l, t, mid, :] * face_y[t, mid, :]
                s = nv[l, t, below, :] * face_y[t, below, :]
                for value, plus, minus in ((e, ep, en), (n, np_, nn), (s, sp, sn)):
                    plus.append(jnp.maximum(value, 0.0))
                    minus.append(jnp.minimum(value, 0.0))
            for c in range(2):
                x = [tr[c, l, t, mid, :] for t in range(2)]
                xe = from_east(x)
                fe = [ep[t] * x[t] + en[t] * xe[t] for t in range(2)]
                fw = from_west(fe)
                for t in range(2):
                    fn = np_[t] * x[t] + nn[t] * tr[c, l, t, over, :]
                    fs = sp[t] * tr[c, l, t, below, :] + sn[t] * x[t]
                    moved[c, l, t, here, :] = x[t] - ((fe[t] - fw[t]) + (fn - fs))

        loop(rows // flow_rows, body)

    early = levels // 3
    for l in range(early):
        wait_level(l)
        advect(l)
    for l in range(early, levels):
        wait_level(l)
    loop(rows // 4 // edge_rows, pack_edges)
    send_edge_e = remote(index, own, got_w, dev(lat, lon_e))
    send_edge_w = remote(index + 1, own, got_e, dev(lat, lon_w))
    index += 2
    send_edge_e.start()
    send_edge_w.start()

    for l in range(early, levels - 2):
        advect(l)

    send_ice_e.wait_recv()
    send_ice_w.wait_recv()

    def unpack_ice(k):
        n = pack_rows
        here = rows8(k, 0, n)
        lanes = lane_iota(n)
        both = jnp.where(lanes % 16 < 8, ice_got_w[here, :], ice_got_e[here, :])
        side = (lanes < 8) | (lanes >= LANES - 8)
        for f in range(6):
            value = pltpu.roll(both, LANES - 16 * f - 8, 1)
            ext[f, 2, rows8(k, PAD, n), :] = jnp.where(side, value, 0.0)

    loop(rows // pack_rows, unpack_ice)

    top_rows = pl.ds(PAD + rows - HALO, HALO)
    low_rows = pl.ds(PAD, HALO)
    north_guard = pl.ds(PAD + rows, HALO)
    south_guard = pl.ds(PAD - HALO, HALO)
    send_n = remote(index, ext.at[:, :, top_rows, :], ext.at[:, :, south_guard, :], dev(*north_dev))
    send_s = remote(
        index + 1, ext.at[:, :, low_rows, :], ext.at[:, :, north_guard, :],
        dev(jnp.where(bottom, lat, lat - 1), lon),
    )
    send_fold = remote(
        index, fold, ext.at[:, :, north_guard, :], dev(*north_dev), arrival=index + 1
    )

    @pl.when(top)
    def _():
        back = LANES - 1 - lane
        for f in range(6):
            sign = -1.0 if f in (0, 1, 3, 4) else 1.0
            for t in range(3):
                block = ext[f, t, top_rows, :]
                turned = jnp.concatenate([block[r : r + 1] for r in range(HALO - 1, -1, -1)], axis=0)
                turned = jnp.take_along_axis(turned, back, axis=1)
                fold[f, (1, 0, 2)[t], :, :] = sign * turned
        send_fold.start()

    @pl.when(jnp.logical_not(top))
    def _():
        send_n.start()

    @pl.when(jnp.logical_not(bottom))
    def _():
        send_s.start()

    for l in range(levels - 2, levels):
        advect(l)

    send_edge_e.wait_recv()
    send_edge_w.wait_recv()

    def edge_update(k):
        n = edge_rows
        lanes = lane_iota(n)
        here = rows8(k, 0, n)
        x_own, s_own = own[0, here, :], own[1, here, :]
        e = got_w[1, here, :] * pltpu.roll(s_own, LANES - 1, 1)
        west = e * jnp.where(e > 0, got_w[0, here, :], pltpu.roll(x_own, LANES - 1, 1))
        e = s_own * pltpu.roll(got_e[1, here, :], LANES - 1, 1)
        east_flux = e * jnp.where(e > 0, x_own, pltpu.roll(got_e[0, here, :], LANES - 1, 1))
        both = jnp.where(lanes % 2 == 0, -east_flux, pltpu.roll(west, 1, 1))
        for q in range(4):
            at = rows8(k, q * (rows // 4), n)
            for c in range(2):
                for l in range(levels):
                    j = 32 * q + 2 * (c * levels + l)
                    value = pltpu.roll(both, LANES - 1 - j, 1)
                    moved[c, l, 0, at, :] += jnp.where(lanes == 0, value, 0.0)
                    moved[c, l, 1, at, :] += jnp.where(lanes == LANES - 1, value, 0.0)

    loop(rows // 4 // edge_rows, edge_update)

    @pl.when(jnp.logical_not(bottom))
    def _():
        send_n.wait_recv()
        for copy in going_south:
            copy.wait_send()
        send_s.wait_send()

    @pl.when(jnp.logical_not(top))
    def _():
        for copy in going_north:
            copy.wait_send()
        send_n.wait_send()

    @pl.when(top)
    def _():
        send_fold.wait_send()

    send_s.wait_recv()
    for copy in (send_ice_e, send_ice_w, send_edge_e, send_edge_w):
        copy.wait_send()


N_REMOTE = 20
N_ICE_LOADS = 14


def ice_kernel(
    levels, rows, lat_count,
    moved, ext, east, north,
    temp_out, salt_out, u_out, v_out,
    vel, stress, turn, surf, water,
    load_sem, store_sem,
):
    n_ext = (rows + 2 * HALO) // 8
    ice_rows, last_rows = block(8 * n_ext, ICE_ROWS), block(rows, LAST_ROWS)
    lat = lax.axis_index("lat")
    grid_rows = rows * lat_count

    def cols(t):
        return pl.ds(t * LANES, LANES)

    loads, stores = [], []
    for i, src in enumerate((east, north)):
        for t in range(2):
            copy = pltpu.make_async_copy(
                src.at[0, :, cols(t)], water.at[i, t], load_sem.at[2 * i + t]
            )
            copy.start()
            loads.append(copy)

    def store(src, dst):
        copy = pltpu.make_async_copy(src, dst, store_sem.at[len(stores)])
        copy.start()
        stores.append(copy)

    for l in range(1, levels):
        for c, dst in enumerate((temp_out, salt_out)):
            for t in range(2):
                store(moved.at[c, l, t], dst.at[l, :, cols(t)])

    def turning(k):
        g = lat * rows - HALO + k * 8 + lax.broadcasted_iota(jnp.int32, (8, LANES), 0)
        g = jnp.where(g >= grid_rows, 2 * grid_rows - 1 - g, g)
        coriolis = 0.5 * (2 * g + 1 - grid_rows).astype(F32) / grid_rows
        b = 0.5 * coriolis
        inverse = 1.0 / (2.25 + b * b)
        turn[0, rows8(k), :] = 1.5 * inverse
        turn[1, rows8(k), :] = b * inverse

    loop(n_ext, turning)

    def stresses(src, fresh):
        def body(k):
            mid = rows8(k, 8, ice_rows)
            below, over = pl.ds(k * ice_rows + 7, ice_rows), pl.ds(k * ice_rows + 9, ice_rows)
            u = [src[0, t, mid, :] for t in range(3)]
            v = [src[1, t, mid, :] for t in range(3)]
            ue, uw = from_east(u), from_west(u)
            ve, vw = from_east(v), from_west(v)
            for t in range(3):
                dudx, dvdx = ue[t] - uw[t], ve[t] - vw[t]
                dudy = src[0, t, over, :] - src[0, t, below, :]
                dvdy = src[1, t, over, :] - src[1, t, below, :]
                div, ten, shr = dudx + dvdy, dudx - dvdy, dudy + dvdx
                p = ext[2, t, mid, :]
                third = ext[5, t, mid, :] * (1.0 / 3.0)
                zeta = p * lax.rsqrt(div * div + 0.25 * (ten * ten + shr * shr) + 1.0)
                quarter = 0.25 * zeta
                a = zeta * div - p
                b = quarter * ten
                sxx, syy, sxy = a + b, a - b, quarter * shr
                if not fresh:
                    sxx = stress[0, t, mid, :] + sxx
                    syy = stress[1, t, mid, :] + syy
                    sxy = stress[2, t, mid, :] + sxy
                stress[0, t, mid, :] = sxx * third
                stress[1, t, mid, :] = syy * third
                stress[2, t, mid, :] = sxy * third

        loop(8 * n_ext // ice_rows, body)

    def momentum(src, k, first, tiles, count):
        mid = rows8(k, first, count)
        below, over = pl.ds(k * count + first - 1, count), pl.ds(k * count + first + 1, count)
        sxx = [stress[0, t, mid, :] for t in range(3)]
        sxy = [stress[2, t, mid, :] for t in range(3)]
        xxe, xxw = from_east(sxx), from_west(sxx)
        xye, xyw = from_east(sxy), from_west(sxy)
        a, b = (turn[i, rows8(k, first - 8, count), :] for i in range(2))
        out = []
        for t in range(tiles):
            fx = (xxe[t] - xxw[t]) + (stress[2, t, over, :] - stress[2, t, below, :])
            fy = (xye[t] - xyw[t]) + (stress[1, t, over, :] - stress[1, t, below, :])
            ru = src[0, t, mid, :] + (0.25 * fx + ext[3, t, mid, :])
            rv = src[1, t, mid, :] + (0.25 * fy + ext[4, t, mid, :])
            covered = ext[5, t, mid, :]
            out.append(((a * ru + b * rv) * covered, (a * rv - b * ru) * covered))
        return out

    src = ext
    for subcycle in range(SUBCYCLES - 1):
        stresses(src, subcycle == 0)

        def body(k, src=src):
            for t, (u, v) in enumerate(momentum(src, k, 8, 3, ice_rows)):
                vel[0, t, rows8(k, 8, ice_rows), :] = u
                vel[1, t, rows8(k, 8, ice_rows), :] = v

        loop(8 * n_ext // ice_rows, body)
        src = vel
    stresses(src, False)
    for copy in loads:
        copy.wait()

    def final(k):
        here, mid = rows8(k, 0, last_rows), rows8(k, PAD, last_rows)
        for t, (u, v) in enumerate(momentum(vel, k, PAD, 2, last_rows)):
            vel[0, t, mid, :] = u
            vel[1, t, mid, :] = v
            slip_u = u - water[0, t, here, :]
            slip_v = v - water[1, t, here, :]
            sst, sss = moved[0, 0, t, here, :], moved[1, 0, t, here, :]
            heat = (
                0.1 * ext[5, t, mid, :]
                * (1.0 + (slip_u * slip_u + slip_v * slip_v))
                * (sst + 0.054 * sss)
            )
            surf[0, t, here, :] = sst - heat
            surf[1, t, here, :] = sss - 0.5 * heat

    loop(rows // last_rows, final)
    for t in range(2):
        store(vel.at[0, t, pl.ds(PAD, rows), :], u_out.at[:, cols(t)])
        store(vel.at[1, t, pl.ds(PAD, rows), :], v_out.at[:, cols(t)])
        store(surf.at[0, t], temp_out.at[0, :, cols(t)])
        store(surf.at[1, t], salt_out.at[0, :, cols(t)])
    for copy in stores:
        copy.wait()


def per_device(lat_count, lon_count, *args):
    temp = args[0]
    levels, rows, _ = temp.shape
    any_space = pl.BlockSpec(memory_space=pl.ANY)
    vmem_space = pl.BlockSpec(memory_space=pltpu.VMEM)
    deep = rows + 2 * PAD
    moved, ext = pl.pallas_call(
        functools.partial(ocean_kernel, levels, rows, lat_count, lon_count),
        out_shape=(
            pltpu.VMEM((2, levels, 2, rows, LANES), F32),
            pltpu.VMEM((6, 3, deep, LANES), F32),
        ),
        in_specs=[any_space] * 11,
        out_specs=(vmem_space, vmem_space),
        scratch_shapes=[
            pltpu.VMEM((2, levels, 2, rows + 16, LANES), F32),
            pltpu.VMEM((levels, 2, rows, LANES), F32),
            pltpu.VMEM((levels, 2, rows + 8, LANES), F32),
            pltpu.VMEM((2, rows + 16, LANES), jnp.int32),
            pltpu.VMEM((2, rows, LANES), jnp.int32),
            pltpu.VMEM((4, 2, rows, LANES), F32),
            pltpu.VMEM((2, rows + 8, LANES), F32),
            pltpu.VMEM((2, rows + 8, LANES), F32),
        ]
        + [pltpu.VMEM((2, rows // 4, LANES), F32)] * 3
        + [pltpu.VMEM((rows, LANES), F32)] * 3
        + [
            pltpu.VMEM((6, 3, HALO, LANES), F32),
            pltpu.SemaphoreType.DMA((N_ICE_LOADS + 8 * levels,)),
            pltpu.SemaphoreType.DMA((N_REMOTE,)),
            pltpu.SemaphoreType.DMA((N_REMOTE,)),
        ],
        compiler_params=pltpu.CompilerParams(
            collective_id=0, has_side_effects=True, vmem_limit_bytes=48 * 1024 * 1024
        ),
        name="ocean",
    )(*args)
    moved = pltpu.with_memory_space_constraint(moved, pltpu.VMEM)
    ext = pltpu.with_memory_space_constraint(ext, pltpu.VMEM)
    shapes = (temp, temp, args[6], args[6])
    return pl.pallas_call(
        functools.partial(ice_kernel, levels, rows, lat_count),
        out_shape=tuple(jax.ShapeDtypeStruct(a.shape, a.dtype) for a in shapes),
        in_specs=[vmem_space, vmem_space, any_space, any_space],
        out_specs=(any_space,) * 4,
        scratch_shapes=[
            pltpu.VMEM((2, 3, deep, LANES), F32),
            pltpu.VMEM((3, 3, deep, LANES), F32),
            pltpu.VMEM((2, deep, LANES), F32),
            pltpu.VMEM((2, 2, rows, LANES), F32),
            pltpu.VMEM((2, 2, rows, LANES), F32),
            pltpu.SemaphoreType.DMA((4,)),
            pltpu.SemaphoreType.DMA((4 * (levels - 1) + 8,)),
        ],
        compiler_params=pltpu.CompilerParams(vmem_limit_bytes=48 * 1024 * 1024),
        name="ice",
    )(moved, ext, args[2], args[3])


def solution(mesh):
    deep, flat = P(None, "lat", "lon"), P("lat", "lon")
    return jax.shard_map(
        functools.partial(per_device, mesh.shape["lat"], mesh.shape["lon"]),
        mesh=mesh,
        in_specs=(deep,) * 4 + (flat,) * 7,
        out_specs=(deep, deep, flat, flat),
        check_vma=False,
    )
```

```python
import functools

import jax
import jax.numpy as jnp
from jax import lax
from jax.experimental import pallas as pl
from jax.experimental.pallas import tpu as pltpu
from jax.sharding import PartitionSpec as P

SUBCYCLES = 4
LANES = 128
HALO = 2 * SUBCYCLES
PAD = 16
MESH = pl.DeviceIdType.MESH
F32 = jnp.float32


def lane_iota(rows=8):
    return lax.broadcasted_iota(jnp.int32, (rows, LANES), 1)


ICE_ROWS = 400
LAST_ROWS = 384
PACK_ROWS = 384
FACE_ROWS = 392
EDGE_ROWS = 96
FLOW_ROWS = 384


def block(total, most):
    return max(n for n in range(8, most + 1, 8) if total % n == 0)


def rows8(k, first=0, count=8):
    return pl.ds(pl.multiple_of(k * count + first, 8), count)


def loop(count, body):
    def step(k, carry):
        body(k)
        return carry

    lax.fori_loop(0, count, step, 0)


def from_east(tiles):
    rolled = [pltpu.roll(a, LANES - 1, 1) for a in tiles]
    n = len(tiles)
    lane = lane_iota(tiles[0].shape[0])
    return [jnp.where(lane == LANES - 1, rolled[(t + 1) % n], rolled[t]) for t in range(n)]


def from_west(tiles):
    rolled = [pltpu.roll(a, 1, 1) for a in tiles]
    n = len(tiles)
    lane = lane_iota(tiles[0].shape[0])
    return [jnp.where(lane == 0, rolled[(t - 1) % n], rolled[t]) for t in range(n)]


def ocean_kernel(
    levels, rows, lat_count, lon_count,
    temp, salt, east, north, land, icem, ice_u, ice_v, press, wind_x, wind_y,
    moved, ext,
    tr, ev, nv, sea, icb, uvw, face_x, face_y, rim_s, rim_n, sea_s, sea_n, corners,
    own, got_w, got_e, ice_own, ice_got_w, ice_got_e, fold,
    local_sem, send_sem, recv_sem,
):
    pack_rows, face_rows = block(rows, PACK_ROWS), block(rows + 8, FACE_ROWS)
    edge_rows, flow_rows = block(rows // 4, EDGE_ROWS), block(rows, FLOW_ROWS)
    lat = lax.axis_index("lat")
    lon = lax.axis_index("lon")
    lon_e = lax.rem(lon + 1, lon_count)
    lon_w = lax.rem(lon + lon_count - 1, lon_count)
    top = lat == lat_count - 1
    bottom = lat == 0
    inner_top, inner_bottom = jnp.logical_not(top), jnp.logical_not(bottom)
    mirror = lon_count - 1 - lon
    fold_w = lax.rem(2 * lon_count - 2 - lon, lon_count)
    fold_e = lax.rem(lon_count - lon, lon_count)
    fold_w_far = top & (fold_w != lon)
    fold_e_far = top & (fold_e != lon)

    def dev(la, lo):
        return {"lat": la, "lon": lo}

    upper, lower = jnp.where(top, lat, lat + 1), jnp.where(bottom, lat, lat - 1)
    north_dev = dev(upper, jnp.where(top, mirror, lon))
    south_dev = dev(lower, lon)

    barrier = pltpu.get_barrier_semaphore()

    def greet(device):
        pl.semaphore_signal(barrier, inc=1, device_id=device, device_id_type=MESH)

    greet(dev(lat, lon_w))
    greet(dev(lat, lon_e))
    greet(north_dev)

    @pl.when(inner_top)
    def _():
        greet(dev(upper, lon_w))
        greet(dev(upper, lon_e))

    @pl.when(fold_w_far)
    def _():
        greet(dev(lat, fold_w))

    @pl.when(fold_e_far)
    def _():
        greet(dev(lat, fold_e))

    @pl.when(inner_bottom)
    def _():
        greet(south_dev)
        greet(dev(lower, lon_w))
        greet(dev(lower, lon_e))

    greeted = (
        3
        + 3 * inner_bottom.astype(jnp.int32)
        + 2 * inner_top.astype(jnp.int32)
        + fold_w_far.astype(jnp.int32)
        + fold_e_far.astype(jnp.int32)
    )

    started = []

    def load(src, dst):
        copy = pltpu.make_async_copy(src, dst, local_sem.at[len(started)])
        copy.start()
        started.append(copy)
        return copy

    def cols(t):
        return pl.ds(t * LANES, LANES)

    ice_loads = []
    for t in range(2):
        ice_loads += [
            load(land.at[:, cols(t)], sea.at[t, pl.ds(8, rows), :]),
            load(icem.at[:, cols(t)], icb.at[t]),
            load(ice_u.at[:, cols(t)], uvw.at[0, t]),
            load(ice_v.at[:, cols(t)], uvw.at[1, t]),
            load(wind_x.at[:, cols(t)], uvw.at[2, t]),
            load(wind_y.at[:, cols(t)], uvw.at[3, t]),
            load(press.at[:, cols(t)], ext.at[2, t, pl.ds(PAD, rows), :]),
        ]
    level_loads = []
    for l in range(levels):
        mine = []
        for t in range(2):
            mine += [
                load(east.at[l, :, cols(t)], ev.at[l, t]),
                load(north.at[l, :, cols(t)], nv.at[l, t, pl.ds(8, rows), :]),
                load(temp.at[l, :, cols(t)], tr.at[0, l, t, pl.ds(8, rows), :]),
                load(salt.at[l, :, cols(t)], tr.at[1, l, t, pl.ds(8, rows), :]),
            ]
        level_loads.append(mine)

    zero = jnp.zeros((8, LANES), F32)
    for t in range(2):
        for edge in (0, rows + 8):
            sea[t, pl.ds(edge, 8), :] = jnp.zeros((8, LANES), jnp.int32)
            for l in range(levels):
                for c in range(2):
                    tr[c, l, t, pl.ds(edge, 8), :] = zero
        for l in range(levels):
            nv[l, t, pl.ds(0, 8), :] = zero

    def remote(i, src, dst, device, arrival=None):
        return pltpu.make_async_remote_copy(
            src_ref=src, dst_ref=dst, send_sem=send_sem.at[i],
            recv_sem=recv_sem.at[i if arrival is None else arrival],
            device_id=device, device_id_type=MESH,
        )

    for copy in ice_loads:
        copy.wait()
    for i in (0, 1, 4, 5):
        level_loads[0][i].wait()

    def pack_ice(k):
        n = pack_rows
        here, mid, out = rows8(k, 0, n), rows8(k, 8, n), rows8(k, PAD, n)
        lanes = lane_iota(n)
        fields = []
        for t in range(2):
            covered = (sea[t, mid, :] * icb[t, here, :]).astype(F32)
            mine = (
                uvw[0, t, here, :] * covered,
                uvw[1, t, here, :] * covered,
                ext[2, t, out, :],
                0.5 * (uvw[2, t, here, :] + ev[0, t, here, :]),
                0.5 * (uvw[3, t, here, :] + nv[0, t, mid, :]),
                covered,
            )
            for f in (0, 1, 3, 4, 5):
                ext[f, t, out, :] = mine[f]
            fields.append(mine)
        packed = jnp.zeros((n, LANES), F32)
        for f in range(6):
            both = jnp.where(lanes < HALO, fields[0][f], fields[1][f])
            both = pltpu.roll(both, 16 * f + 8, 1)
            packed = jnp.where((lanes >= 16 * f) & (lanes < 16 * f + 16), both, packed)
        ice_own[here, :] = packed

    loop(rows // pack_rows, pack_ice)

    top_rows = pl.ds(PAD + rows - HALO, HALO)
    low_rows = pl.ds(PAD, HALO)
    north_guard = pl.ds(PAD + rows, HALO)
    south_guard = pl.ds(PAD - HALO, HALO)

    def turned(f, value):
        value = jnp.concatenate([value[r : r + 1] for r in range(HALO - 1, -1, -1)], axis=0)
        value = jnp.take_along_axis(value, LANES - 1 - lane_iota(), axis=1)
        return -value if f in (0, 1, 3, 4) else value

    @pl.when(top)
    def _():
        for f in range(6):
            for t in range(2):
                fold[f, 1 - t, :, :] = turned(f, ext[f, t, top_rows, :])

    pl.semaphore_wait(barrier, greeted)

    send_e = remote(0, ice_own, ice_got_w, dev(lat, lon_e))
    send_w = remote(1, ice_own, ice_got_e, dev(lat, lon_w))
    send_e.start()
    send_w.start()
    wide = pl.ds(0, 2)
    send_n = remote(
        2, ext.at[:, wide, top_rows, :], ext.at[:, wide, south_guard, :], north_dev
    )
    send_s = remote(
        3, ext.at[:, wide, low_rows, :], ext.at[:, wide, north_guard, :], south_dev
    )
    send_fold = remote(2, fold, ext.at[:, wide, north_guard, :], north_dev, arrival=3)
    slab_top, slab_low = ice_own.at[pl.ds(rows - HALO, HALO)], ice_own.at[pl.ds(0, HALO)]
    send_ne = remote(4, slab_top, corners.at[0], dev(upper, lon_e))
    send_nw = remote(5, slab_top, corners.at[1], dev(upper, lon_w))
    send_se = remote(6, slab_low, corners.at[2], dev(lower, lon_e))
    send_sw = remote(7, slab_low, corners.at[3], dev(lower, lon_w))
    send_fold_w = remote(4, slab_top, corners.at[2], dev(lat, fold_w), arrival=6)
    send_fold_e = remote(5, slab_top, corners.at[3], dev(lat, fold_e), arrival=7)

    last, first = pl.ds(rows - 8, 8), pl.ds(0, 8)
    rims_n = [
        remote(8 + i, src, dst, north_dev)
        for i, (src, dst) in enumerate((
            (temp.at[:, last, :], rim_s.at[0]),
            (salt.at[:, last, :], rim_s.at[1]),
            (north.at[:, last, :], rim_s.at[2]),
            (land.at[last, :], sea_s),
        ))
    ]
    rims_s = [
        remote(12 + i, src, dst, south_dev)
        for i, (src, dst) in enumerate((
            (temp.at[:, first, :], rim_n.at[0]),
            (salt.at[:, first, :], rim_n.at[1]),
            (land.at[first, :], sea_n),
        ))
    ]

    @pl.when(inner_top)
    def _():
        for copy in [send_n, send_ne, send_nw] + rims_n:
            copy.start()

    @pl.when(inner_bottom)
    def _():
        for copy in [send_s, send_se, send_sw] + rims_s:
            copy.start()

    @pl.when(top)
    def _():
        send_fold.start()

    @pl.when(fold_w_far)
    def _():
        send_fold_w.start()

    @pl.when(fold_e_far)
    def _():
        send_fold_e.start()

    @pl.when(top & (fold_w == lon))
    def _():
        corners[2, :, :] = ice_own[pl.ds(rows - HALO, HALO), :]

    @pl.when(top & (fold_e == lon))
    def _():
        corners[3, :, :] = ice_own[pl.ds(rows - HALO, HALO), :]

    def faces(k):
        n = face_rows
        here = rows8(k, 0, n)
        s = [sea[t, here, :].astype(F32) for t in range(2)]
        for t in range(2):
            up = sea[t, pl.ds(k * n + 1, n), :].astype(F32)
            face_y[t, here, :] = s[t] * up
        se = from_east(s)
        face_x[0, here, :] = s[0] * se[0]
        face_x[1, here, :] = jnp.where(lane_iota(n) == LANES - 1, 0.0, s[1] * se[1])

    loop((rows + 8) // face_rows, faces)

    def wait_level(l):
        for i, copy in enumerate(level_loads[l]):
            if l or i not in (0, 1, 4, 5):
                copy.wait()

    def pack_edges(k):
        n = edge_rows
        lanes = lane_iota(n)
        value, speed = jnp.zeros((n, LANES), F32), jnp.zeros((n, LANES), F32)
        for q in range(4):
            first_row = q * (rows // 4)
            here, mid = rows8(k, first_row, n), rows8(k, first_row + 8, n)
            sea_e = sea[1, mid, :].astype(F32)
            sea_w = sea[0, mid, pl.ds(0, 1)].astype(F32)
            for l in range(levels):
                for c in range(2):
                    j = 32 * q + 2 * (c * levels + l)
                    both = jnp.where(lanes == 0, tr[c, l, 0, mid, :], tr[c, l, 1, mid, :])
                    both = pltpu.roll(both, j + 1, 1)
                    value = jnp.where((lanes == j) | (lanes == j + 1), both, value)
                j = 32 * q + 2 * l
                pushed = pltpu.roll(ev[l, 1, here, :] * sea_e, j + 1, 1)
                speed = jnp.where(lanes == j, pushed, speed)
            odd = (lanes >= 32 * q) & (lanes < 32 * q + 32) & (lanes % 2 == 1)
            speed = jnp.where(odd, jnp.broadcast_to(sea_w, (n, LANES)), speed)
        again = pltpu.roll(speed, 2 * levels, 1)
        place = lanes % 32
        again = (place >= 2 * levels) & (place < 4 * levels) & (place % 2 == 0), again
        out = rows8(k, 0, n)
        own[0, out, :] = value
        own[1, out, :] = jnp.where(again[0], again[1], speed)

    def advect(l):
        def body(k):
            n_rows = flow_rows
            here, mid = rows8(k, 0, n_rows), rows8(k, 8, n_rows)
            below, over = pl.ds(k * n_rows + 7, n_rows), pl.ds(k * n_rows + 9, n_rows)
            ep, en, np_, nn, sp, sn = [], [], [], [], [], []
            for t in range(2):
                e = ev[l, t, here, :] * face_x[t, mid, :]
                n = nv[l, t, mid, :] * face_y[t, mid, :]
                s = nv[l, t, below, :] * face_y[t, below, :]
                for value, plus, minus in ((e, ep, en), (n, np_, nn), (s, sp, sn)):
                    plus.append(jnp.maximum(value, 0.0))
                    minus.append(jnp.minimum(value, 0.0))
            for c in range(2):
                x = [tr[c, l, t, mid, :] for t in range(2)]
                xe = from_east(x)
                fe = [ep[t] * x[t] + en[t] * xe[t] for t in range(2)]
                fw = from_west(fe)
                for t in range(2):
                    fn = np_[t] * x[t] + nn[t] * tr[c, l, t, over, :]
                    fs = sp[t] * tr[c, l, t, below, :] + sn[t] * x[t]
                    moved[c, l, t, here, :] = x[t] - ((fe[t] - fw[t]) + (fn - fs))

        loop(rows // flow_rows, body)

    early = levels // 3
    for l in range(early):
        wait_level(l)
        advect(l)
    for l in range(early, levels):
        wait_level(l)
    loop(rows // 4 // edge_rows, pack_edges)
    send_edge_e = remote(15, own, got_w, dev(lat, lon_e))
    send_edge_w = remote(16, own, got_e, dev(lat, lon_w))
    send_edge_e.start()
    send_edge_w.start()

    for l in range(early, levels):
        advect(l)

    def unpack(value_w, value_e, n):
        lanes = lane_iota(n)
        both = jnp.where(lanes % 16 < 8, value_w, value_e)
        side = (lanes < 8) | (lanes >= LANES - 8)
        return [
            jnp.where(side, pltpu.roll(both, LANES - 16 * f - 8, 1), 0.0) for f in range(6)
        ]

    send_e.wait_recv()
    send_w.wait_recv()

    def unpack_ice(k):
        here = rows8(k, 0, pack_rows)
        for f, value in enumerate(unpack(ice_got_w[here, :], ice_got_e[here, :], pack_rows)):
            ext[f, 2, rows8(k, PAD, pack_rows), :] = value

    loop(rows // pack_rows, unpack_ice)

    @pl.when(inner_bottom)
    def _():
        send_ne.wait_recv()
        send_nw.wait_recv()
        for f, value in enumerate(unpack(corners[0], corners[1], HALO)):
            ext[f, 2, south_guard, :] = value

    @pl.when(bottom)
    def _():
        for f in range(6):
            for t in range(3):
                ext[f, t, south_guard, :] = zero

    @pl.when(inner_top | fold_w_far)
    def _():
        send_se.wait_recv()

    @pl.when(inner_top | fold_e_far)
    def _():
        send_sw.wait_recv()

    @pl.when(inner_top)
    def _():
        for f, value in enumerate(unpack(corners[2], corners[3], HALO)):
            ext[f, 2, north_guard, :] = value

    @pl.when(top)
    def _():
        for f, value in enumerate(unpack(corners[2], corners[3], HALO)):
            ext[f, 2, north_guard, :] = turned(f, value)

    send_edge_e.wait_recv()
    send_edge_w.wait_recv()

    def edge_update(k):
        n = edge_rows
        lanes = lane_iota(n)
        here = rows8(k, 0, n)
        x_own, s_own = own[0, here, :], own[1, here, :]
        e = got_w[1, here, :] * pltpu.roll(s_own, LANES - 1, 1)
        west = e * jnp.where(e > 0, got_w[0, here, :], pltpu.roll(x_own, LANES - 1, 1))
        e = s_own * pltpu.roll(got_e[1, here, :], LANES - 1, 1)
        east_flux = e * jnp.where(e > 0, x_own, pltpu.roll(got_e[0, here, :], LANES - 1, 1))
        both = jnp.where(lanes % 2 == 0, -east_flux, pltpu.roll(west, 1, 1))
        for q in range(4):
            at = rows8(k, q * (rows // 4), n)
            for c in range(2):
                for l in range(levels):
                    j = 32 * q + 2 * (c * levels + l)
                    value = pltpu.roll(both, LANES - 1 - j, 1)
                    moved[c, l, 0, at, :] += jnp.where(lanes == 0, value, 0.0)
                    moved[c, l, 1, at, :] += jnp.where(lanes == LANES - 1, value, 0.0)

    loop(rows // 4 // edge_rows, edge_update)

    def row(t, r):
        return pl.ds(r, 1), pl.ds(t * LANES, LANES)

    @pl.when(inner_bottom)
    def _():
        for copy in rims_n:
            copy.wait_recv()
        for t in range(2):
            rim = row(t, 7)
            face = (sea_s[rim] * sea[t, pl.ds(8, 1), :]).astype(F32)
            for l in range(levels):
                speed = rim_s[(2, l) + rim] * face
                for c in range(2):
                    value = jnp.where(speed > 0, rim_s[(c, l) + rim], tr[c, l, t, pl.ds(8, 1), :])
                    moved[c, l, t, pl.ds(0, 1), :] += speed * value

    @pl.when(inner_top)
    def _():
        for copy in rims_s:
            copy.wait_recv()
        mine = pl.ds(rows + 7, 1)
        for t in range(2):
            rim = row(t, 0)
            face = (sea[t, mine, :] * sea_n[rim]).astype(F32)
            for l in range(levels):
                speed = nv[l, t, mine, :] * face
                for c in range(2):
                    value = jnp.where(speed > 0, tr[c, l, t, mine, :], rim_n[(c, l) + rim])
                    moved[c, l, t, pl.ds(rows - 1, 1), :] -= speed * value

    @pl.when(inner_bottom)
    def _():
        send_n.wait_recv()
        for copy in [send_s, send_se, send_sw] + rims_s:
            copy.wait_send()

    @pl.when(inner_top)
    def _():
        for copy in [send_n, send_ne, send_nw] + rims_n:
            copy.wait_send()

    @pl.when(top)
    def _():
        send_fold.wait_send()

    @pl.when(fold_w_far)
    def _():
        send_fold_w.wait_send()

    @pl.when(fold_e_far)
    def _():
        send_fold_e.wait_send()

    send_s.wait_recv()
    for copy in (send_e, send_w, send_edge_e, send_edge_w):
        copy.wait_send()


N_REMOTE = 17
N_ICE_LOADS = 14


def ice_kernel(
    levels, rows, lat_count,
    moved, ext, east, north,
    temp_out, salt_out, u_out, v_out,
    vel, stress, turn, surf, water,
    load_sem, store_sem,
):
    n_ext = (rows + 2 * HALO) // 8
    ice_rows, last_rows = block(8 * n_ext, ICE_ROWS), block(rows, LAST_ROWS)
    lat = lax.axis_index("lat")
    grid_rows = rows * lat_count

    def cols(t):
        return pl.ds(t * LANES, LANES)

    loads, stores = [], []
    for i, src in enumerate((east, north)):
        for t in range(2):
            copy = pltpu.make_async_copy(
                src.at[0, :, cols(t)], water.at[i, t], load_sem.at[2 * i + t]
            )
            copy.start()
            loads.append(copy)

    def store(src, dst):
        copy = pltpu.make_async_copy(src, dst, store_sem.at[len(stores)])
        copy.start()
        stores.append(copy)

    for l in range(1, levels):
        for c, dst in enumerate((temp_out, salt_out)):
            for t in range(2):
                store(moved.at[c, l, t], dst.at[l, :, cols(t)])

    def turning(k):
        g = lat * rows - HALO + k * 8 + lax.broadcasted_iota(jnp.int32, (8, LANES), 0)
        g = jnp.where(g >= grid_rows, 2 * grid_rows - 1 - g, g)
        coriolis = 0.5 * (2 * g + 1 - grid_rows).astype(F32) / grid_rows
        b = 0.5 * coriolis
        inverse = 1.0 / (2.25 + b * b)
        turn[0, rows8(k), :] = 1.5 * inverse
        turn[1, rows8(k), :] = b * inverse

    loop(n_ext, turning)

    def stresses(src, fresh):
        def body(k):
            mid = rows8(k, 8, ice_rows)
            below, over = pl.ds(k * ice_rows + 7, ice_rows), pl.ds(k * ice_rows + 9, ice_rows)
            u = [src[0, t, mid, :] for t in range(3)]
            v = [src[1, t, mid, :] for t in range(3)]
            ue, uw = from_east(u), from_west(u)
            ve, vw = from_east(v), from_west(v)
            for t in range(3):
                dudx, dvdx = ue[t] - uw[t], ve[t] - vw[t]
                dudy = src[0, t, over, :] - src[0, t, below, :]
                dvdy = src[1, t, over, :] - src[1, t, below, :]
                div, ten, shr = dudx + dvdy, dudx - dvdy, dudy + dvdx
                p = ext[2, t, mid, :]
                third = ext[5, t, mid, :] * (1.0 / 3.0)
                zeta = p * lax.rsqrt(div * div + 0.25 * (ten * ten + shr * shr) + 1.0)
                quarter = 0.25 * zeta
                a = zeta * div - p
                b = quarter * ten
                sxx, syy, sxy = a + b, a - b, quarter * shr
                if not fresh:
                    sxx = stress[0, t, mid, :] + sxx
                    syy = stress[1, t, mid, :] + syy
                    sxy = stress[2, t, mid, :] + sxy
                stress[0, t, mid, :] = sxx * third
                stress[1, t, mid, :] = syy * third
                stress[2, t, mid, :] = sxy * third

        loop(8 * n_ext // ice_rows, body)

    def momentum(src, k, first, tiles, count):
        mid = rows8(k, first, count)
        below, over = pl.ds(k * count + first - 1, count), pl.ds(k * count + first + 1, count)
        sxx = [stress[0, t, mid, :] for t in range(3)]
        sxy = [stress[2, t, mid, :] for t in range(3)]
        xxe, xxw = from_east(sxx), from_west(sxx)
        xye, xyw = from_east(sxy), from_west(sxy)
        a, b = (turn[i, rows8(k, first - 8, count), :] for i in range(2))
        out = []
        for t in range(tiles):
            fx = (xxe[t] - xxw[t]) + (stress[2, t, over, :] - stress[2, t, below, :])
            fy = (xye[t] - xyw[t]) + (stress[1, t, over, :] - stress[1, t, below, :])
            ru = src[0, t, mid, :] + (0.25 * fx + ext[3, t, mid, :])
            rv = src[1, t, mid, :] + (0.25 * fy + ext[4, t, mid, :])
            covered = ext[5, t, mid, :]
            out.append(((a * ru + b * rv) * covered, (a * rv - b * ru) * covered))
        return out

    src = ext
    for subcycle in range(SUBCYCLES - 1):
        stresses(src, subcycle == 0)

        def body(k, src=src):
            for t, (u, v) in enumerate(momentum(src, k, 8, 3, ice_rows)):
                vel[0, t, rows8(k, 8, ice_rows), :] = u
                vel[1, t, rows8(k, 8, ice_rows), :] = v

        loop(8 * n_ext // ice_rows, body)
        src = vel
    stresses(src, False)
    for copy in loads:
        copy.wait()

    def final(k):
        here, mid = rows8(k, 0, last_rows), rows8(k, PAD, last_rows)
        for t, (u, v) in enumerate(momentum(vel, k, PAD, 2, last_rows)):
            vel[0, t, mid, :] = u
            vel[1, t, mid, :] = v
            slip_u = u - water[0, t, here, :]
            slip_v = v - water[1, t, here, :]
            sst, sss = moved[0, 0, t, here, :], moved[1, 0, t, here, :]
            heat = (
                0.1 * ext[5, t, mid, :]
                * (1.0 + (slip_u * slip_u + slip_v * slip_v))
                * (sst + 0.054 * sss)
            )
            surf[0, t, here, :] = sst - heat
            surf[1, t, here, :] = sss - 0.5 * heat

    loop(rows // last_rows, final)
    for t in range(2):
        store(vel.at[0, t, pl.ds(PAD, rows), :], u_out.at[:, cols(t)])
        store(vel.at[1, t, pl.ds(PAD, rows), :], v_out.at[:, cols(t)])
        store(surf.at[0, t], temp_out.at[0, :, cols(t)])
        store(surf.at[1, t], salt_out.at[0, :, cols(t)])
    for copy in stores:
        copy.wait()


def per_device(lat_count, lon_count, *args):
    temp = args[0]
    levels, rows, _ = temp.shape
    any_space = pl.BlockSpec(memory_space=pl.ANY)
    vmem_space = pl.BlockSpec(memory_space=pltpu.VMEM)
    deep = rows + 2 * PAD
    moved, ext = pl.pallas_call(
        functools.partial(ocean_kernel, levels, rows, lat_count, lon_count),
        out_shape=(
            pltpu.VMEM((2, levels, 2, rows, LANES), F32),
            pltpu.VMEM((6, 3, deep, LANES), F32),
        ),
        in_specs=[any_space] * 11,
        out_specs=(vmem_space, vmem_space),
        scratch_shapes=[
            pltpu.VMEM((2, levels, 2, rows + 16, LANES), F32),
            pltpu.VMEM((levels, 2, rows, LANES), F32),
            pltpu.VMEM((levels, 2, rows + 8, LANES), F32),
            pltpu.VMEM((2, rows + 16, LANES), jnp.int32),
            pltpu.VMEM((2, rows, LANES), jnp.int32),
            pltpu.VMEM((4, 2, rows, LANES), F32),
            pltpu.VMEM((2, rows + 8, LANES), F32),
            pltpu.VMEM((2, rows + 8, LANES), F32),
            pltpu.VMEM((3, levels, 8, 2 * LANES), F32),
            pltpu.VMEM((2, levels, 8, 2 * LANES), F32),
            pltpu.VMEM((8, 2 * LANES), jnp.int32),
            pltpu.VMEM((8, 2 * LANES), jnp.int32),
            pltpu.VMEM((4, HALO, LANES), F32),
        ]
        + [pltpu.VMEM((2, rows // 4, LANES), F32)] * 3
        + [pltpu.VMEM((rows, LANES), F32)] * 3
        + [
            pltpu.VMEM((6, 2, HALO, LANES), F32),
            pltpu.SemaphoreType.DMA((N_ICE_LOADS + 8 * levels,)),
            pltpu.SemaphoreType.DMA((N_REMOTE,)),
            pltpu.SemaphoreType.DMA((N_REMOTE,)),
        ],
        compiler_params=pltpu.CompilerParams(
            collective_id=0, has_side_effects=True, vmem_limit_bytes=48 * 1024 * 1024
        ),
        name="ocean",
    )(*args)
    moved = pltpu.with_memory_space_constraint(moved, pltpu.VMEM)
    ext = pltpu.with_memory_space_constraint(ext, pltpu.VMEM)
    shapes = (temp, temp, args[6], args[6])
    return pl.pallas_call(
        functools.partial(ice_kernel, levels, rows, lat_count),
        out_shape=tuple(jax.ShapeDtypeStruct(a.shape, a.dtype) for a in shapes),
        in_specs=[vmem_space, vmem_space, any_space, any_space],
        out_specs=(any_space,) * 4,
        scratch_shapes=[
            pltpu.VMEM((2, 3, deep, LANES), F32),
            pltpu.VMEM((3, 3, deep, LANES), F32),
            pltpu.VMEM((2, deep, LANES), F32),
            pltpu.VMEM((2, 2, rows, LANES), F32),
            pltpu.VMEM((2, 2, rows, LANES), F32),
            pltpu.SemaphoreType.DMA((4,)),
            pltpu.SemaphoreType.DMA((4 * (levels - 1) + 8,)),
        ],
        compiler_params=pltpu.CompilerParams(vmem_limit_bytes=48 * 1024 * 1024),
        name="ice",
    )(moved, ext, args[2], args[3])


def solution(mesh):
    deep, flat = P(None, "lat", "lon"), P("lat", "lon")
    return jax.shard_map(
        functools.partial(per_device, mesh.shape["lat"], mesh.shape["lon"]),
        mesh=mesh,
        in_specs=(deep,) * 4 + (flat,) * 7,
        out_specs=(deep, deep, flat, flat),
        check_vma=False,
    )
```

```python
import functools

import jax
import jax.numpy as jnp
from jax import lax
from jax.experimental import pallas as pl
from jax.experimental.pallas import tpu as pltpu
from jax.sharding import PartitionSpec as P

SUBCYCLES = 4
LANES = 128
HALO = 2 * SUBCYCLES
PAD = 16
MESH = pl.DeviceIdType.MESH
F32 = jnp.float32


def lane_iota(rows=8):
    return lax.broadcasted_iota(jnp.int32, (rows, LANES), 1)


ICE_ROWS = 8
LAST_ROWS = 8
PACK_ROWS = 384
FACE_ROWS = 392
EDGE_ROWS = 96
AHEAD = 8


def block(total, most):
    return max(n for n in range(8, most + 1, 8) if total % n == 0)


def rows8(k, first=0, count=8):
    start = k * count + first
    return pl.ds(start if isinstance(start, int) else pl.multiple_of(start, 8), count)


def loop(count, body):
    def step(k, carry):
        body(k)
        return carry

    lax.fori_loop(0, count, step, 0, unroll=count)


def from_east(tiles):
    rolled = [pltpu.roll(a, LANES - 1, 1) for a in tiles]
    n = len(tiles)
    lane = lane_iota(tiles[0].shape[0])
    return [jnp.where(lane == LANES - 1, rolled[(t + 1) % n], rolled[t]) for t in range(n)]


def from_west(tiles):
    rolled = [pltpu.roll(a, 1, 1) for a in tiles]
    n = len(tiles)
    lane = lane_iota(tiles[0].shape[0])
    return [jnp.where(lane == 0, rolled[(t - 1) % n], rolled[t]) for t in range(n)]


def ocean_kernel(
    levels, rows, lat_count, lon_count,
    temp, salt, east, north, land, icem, ice_u, ice_v, press, wind_x, wind_y,
    moved, ext,
    tr, ev, nv, sea, icb, uvw, face_x, face_y, rim_s, rim_n, sea_s, sea_n, corners,
    own, got_w, got_e, ice_own, ice_got_w, ice_got_e, fold,
    local_sem, send_sem, recv_sem,
):
    pack_rows, face_rows = block(rows, PACK_ROWS), block(rows + 8, FACE_ROWS)
    edge_rows = block(rows // 4, EDGE_ROWS)
    lat = lax.axis_index("lat")
    lon = lax.axis_index("lon")
    lon_e = lax.rem(lon + 1, lon_count)
    lon_w = lax.rem(lon + lon_count - 1, lon_count)
    top = lat == lat_count - 1
    bottom = lat == 0
    inner_top, inner_bottom = jnp.logical_not(top), jnp.logical_not(bottom)
    mirror = lon_count - 1 - lon
    fold_w = lax.rem(2 * lon_count - 2 - lon, lon_count)
    fold_e = lax.rem(lon_count - lon, lon_count)
    fold_w_far = top & (fold_w != lon)
    fold_e_far = top & (fold_e != lon)

    def dev(la, lo):
        return {"lat": la, "lon": lo}

    upper, lower = jnp.where(top, lat, lat + 1), jnp.where(bottom, lat, lat - 1)
    north_dev = dev(upper, jnp.where(top, mirror, lon))
    south_dev = dev(lower, lon)

    barrier = pltpu.get_barrier_semaphore()

    def greet(device):
        pl.semaphore_signal(barrier, inc=1, device_id=device, device_id_type=MESH)

    greet(dev(lat, lon_w))
    greet(dev(lat, lon_e))
    greet(north_dev)

    @pl.when(inner_top)
    def _():
        greet(dev(upper, lon_w))
        greet(dev(upper, lon_e))

    @pl.when(fold_w_far)
    def _():
        greet(dev(lat, fold_w))

    @pl.when(fold_e_far)
    def _():
        greet(dev(lat, fold_e))

    @pl.when(inner_bottom)
    def _():
        greet(south_dev)
        greet(dev(lower, lon_w))
        greet(dev(lower, lon_e))

    greeted = (
        3
        + 3 * inner_bottom.astype(jnp.int32)
        + 2 * inner_top.astype(jnp.int32)
        + fold_w_far.astype(jnp.int32)
        + fold_e_far.astype(jnp.int32)
    )

    started = []

    def load(src, dst):
        copy = pltpu.make_async_copy(src, dst, local_sem.at[len(started)])
        copy.start()
        started.append(copy)
        return copy

    def cols(t):
        return pl.ds(t * LANES, LANES)

    ice_loads = []
    for t in range(2):
        ice_loads += [
            load(land.at[:, cols(t)], sea.at[t, pl.ds(8, rows), :]),
            load(icem.at[:, cols(t)], icb.at[t]),
            load(ice_u.at[:, cols(t)], uvw.at[0, t]),
            load(ice_v.at[:, cols(t)], uvw.at[1, t]),
            load(wind_x.at[:, cols(t)], uvw.at[2, t]),
            load(wind_y.at[:, cols(t)], uvw.at[3, t]),
            load(press.at[:, cols(t)], ext.at[2, t, pl.ds(PAD, rows), :]),
        ]
    level_loads = []
    for l in range(levels):
        mine = []
        for t in range(2):
            mine += [
                load(east.at[l, :, cols(t)], ev.at[l, t]),
                load(north.at[l, :, cols(t)], nv.at[l, t, pl.ds(8, rows), :]),
                load(temp.at[l, :, cols(t)], tr.at[0, l, t, pl.ds(8, rows), :]),
                load(salt.at[l, :, cols(t)], tr.at[1, l, t, pl.ds(8, rows), :]),
            ]
        level_loads.append(mine)

    zero = jnp.zeros((8, LANES), F32)
    for t in range(2):
        for edge in (0, rows + 8):
            sea[t, pl.ds(edge, 8), :] = jnp.zeros((8, LANES), jnp.int32)
            for l in range(levels):
                for c in range(2):
                    tr[c, l, t, pl.ds(edge, 8), :] = zero
        for l in range(levels):
            nv[l, t, pl.ds(0, 8), :] = zero

    def remote(i, src, dst, device, arrival=None):
        return pltpu.make_async_remote_copy(
            src_ref=src, dst_ref=dst, send_sem=send_sem.at[i],
            recv_sem=recv_sem.at[i if arrival is None else arrival],
            device_id=device, device_id_type=MESH,
        )

    for copy in ice_loads:
        copy.wait()
    for i in (0, 1, 4, 5):
        level_loads[0][i].wait()

    def pack_ice(k):
        n = pack_rows
        here, mid, out = rows8(k, 0, n), rows8(k, 8, n), rows8(k, PAD, n)
        lanes = lane_iota(n)
        fields = []
        for t in range(2):
            covered = (sea[t, mid, :] * icb[t, here, :]).astype(F32)
            mine = (
                uvw[0, t, here, :] * covered,
                uvw[1, t, here, :] * covered,
                ext[2, t, out, :],
                0.5 * (uvw[2, t, here, :] + ev[0, t, here, :]),
                0.5 * (uvw[3, t, here, :] + nv[0, t, mid, :]),
                covered,
            )
            for f in (0, 1, 3, 4, 5):
                ext[f, t, out, :] = mine[f]
            fields.append(mine)
        packed = jnp.zeros((n, LANES), F32)
        for f in range(6):
            both = jnp.where(lanes < HALO, fields[0][f], fields[1][f])
            both = pltpu.roll(both, 16 * f + 8, 1)
            packed = jnp.where((lanes >= 16 * f) & (lanes < 16 * f + 16), both, packed)
        ice_own[here, :] = packed

    loop(rows // pack_rows, pack_ice)

    top_rows = pl.ds(PAD + rows - HALO, HALO)
    low_rows = pl.ds(PAD, HALO)
    north_guard = pl.ds(PAD + rows, HALO)
    south_guard = pl.ds(PAD - HALO, HALO)

    def turned(f, value):
        value = jnp.concatenate([value[r : r + 1] for r in range(HALO - 1, -1, -1)], axis=0)
        value = jnp.take_along_axis(value, LANES - 1 - lane_iota(), axis=1)
        return -value if f in (0, 1, 3, 4) else value

    @pl.when(top)
    def _():
        for f in range(6):
            for t in range(2):
                fold[f, 1 - t, :, :] = turned(f, ext[f, t, top_rows, :])

    pl.semaphore_wait(barrier, greeted)

    send_e = remote(0, ice_own, ice_got_w, dev(lat, lon_e))
    send_w = remote(1, ice_own, ice_got_e, dev(lat, lon_w))
    send_e.start()
    send_w.start()
    wide = pl.ds(0, 2)
    send_n = remote(
        2, ext.at[:, wide, top_rows, :], ext.at[:, wide, south_guard, :], north_dev
    )
    send_s = remote(
        3, ext.at[:, wide, low_rows, :], ext.at[:, wide, north_guard, :], south_dev
    )
    send_fold = remote(2, fold, ext.at[:, wide, north_guard, :], north_dev, arrival=3)
    slab_top, slab_low = ice_own.at[pl.ds(rows - HALO, HALO)], ice_own.at[pl.ds(0, HALO)]
    send_ne = remote(4, slab_top, corners.at[0], dev(upper, lon_e))
    send_nw = remote(5, slab_top, corners.at[1], dev(upper, lon_w))
    send_se = remote(6, slab_low, corners.at[2], dev(lower, lon_e))
    send_sw = remote(7, slab_low, corners.at[3], dev(lower, lon_w))
    send_fold_w = remote(4, slab_top, corners.at[2], dev(lat, fold_w), arrival=6)
    send_fold_e = remote(5, slab_top, corners.at[3], dev(lat, fold_e), arrival=7)

    last, first = pl.ds(rows - 8, 8), pl.ds(0, 8)
    rims_n = [
        remote(8 + i, src, dst, north_dev)
        for i, (src, dst) in enumerate((
            (temp.at[:, last, :], rim_s.at[0]),
            (salt.at[:, last, :], rim_s.at[1]),
            (north.at[:, last, :], rim_s.at[2]),
            (land.at[last, :], sea_s),
        ))
    ]
    rims_s = [
        remote(12 + i, src, dst, south_dev)
        for i, (src, dst) in enumerate((
            (temp.at[:, first, :], rim_n.at[0]),
            (salt.at[:, first, :], rim_n.at[1]),
            (land.at[first, :], sea_n),
        ))
    ]

    @pl.when(inner_top)
    def _():
        for copy in [send_n, send_ne, send_nw] + rims_n:
            copy.start()

    @pl.when(inner_bottom)
    def _():
        for copy in [send_s, send_se, send_sw] + rims_s:
            copy.start()

    @pl.when(top)
    def _():
        send_fold.start()

    @pl.when(fold_w_far)
    def _():
        send_fold_w.start()

    @pl.when(fold_e_far)
    def _():
        send_fold_e.start()

    @pl.when(top & (fold_w == lon))
    def _():
        corners[2, :, :] = ice_own[pl.ds(rows - HALO, HALO), :]

    @pl.when(top & (fold_e == lon))
    def _():
        corners[3, :, :] = ice_own[pl.ds(rows - HALO, HALO), :]

    def faces(k):
        n = face_rows
        here = rows8(k, 0, n)
        s = [sea[t, here, :].astype(F32) for t in range(2)]
        for t in range(2):
            up = sea[t, pl.ds(k * n + 1, n), :].astype(F32)
            face_y[t, here, :] = s[t] * up
        se = from_east(s)
        face_x[0, here, :] = s[0] * se[0]
        face_x[1, here, :] = jnp.where(lane_iota(n) == LANES - 1, 0.0, s[1] * se[1])

    loop((rows + 8) // face_rows, faces)

    def wait_level(l):
        for i, copy in enumerate(level_loads[l]):
            if l or i not in (0, 1, 4, 5):
                copy.wait()

    def pack_edges(k):
        n = edge_rows
        lanes = lane_iota(n)
        value, speed = jnp.zeros((n, LANES), F32), jnp.zeros((n, LANES), F32)
        for q in range(4):
            first_row = q * (rows // 4)
            here, mid = rows8(k, first_row, n), rows8(k, first_row + 8, n)
            sea_e = sea[1, mid, :].astype(F32)
            sea_w = sea[0, mid, pl.ds(0, 1)].astype(F32)
            for l in range(levels):
                for c in range(2):
                    j = 32 * q + 2 * (c * levels + l)
                    both = jnp.where(lanes == 0, tr[c, l, 0, mid, :], tr[c, l, 1, mid, :])
                    both = pltpu.roll(both, j + 1, 1)
                    value = jnp.where((lanes == j) | (lanes == j + 1), both, value)
                j = 32 * q + 2 * l
                pushed = pltpu.roll(ev[l, 1, here, :] * sea_e, j + 1, 1)
                speed = jnp.where(lanes == j, pushed, speed)
            odd = (lanes >= 32 * q) & (lanes < 32 * q + 32) & (lanes % 2 == 1)
            speed = jnp.where(odd, jnp.broadcast_to(sea_w, (n, LANES)), speed)
        again = pltpu.roll(speed, 2 * levels, 1)
        place = lanes % 32
        again = (place >= 2 * levels) & (place < 4 * levels) & (place % 2 == 0), again
        out = rows8(k, 0, n)
        own[0, out, :] = value
        own[1, out, :] = jnp.where(again[0], again[1], speed)

    both = [(c, t) for c in range(2) for t in range(2)]

    def advect(l):
        def ahead(k):
            return [pltpu.roll(tr[c, l, t, rows8(k, 8), :], LANES - 1, 1) for c, t in both]

        def east_flux(k, rolled):
            lanes = lane_iota()
            flux = []
            for c in range(2):
                a, b = rolled[2 * c], rolled[2 * c + 1]
                for t, xe in enumerate(
                    (jnp.where(lanes == LANES - 1, b, a), jnp.where(lanes == LANES - 1, a, b))
                ):
                    e = ev[l, t, rows8(k), :] * face_x[t, rows8(k, 8), :]
                    x = tr[c, l, t, rows8(k, 8), :]
                    flux.append(jnp.maximum(e, 0.0) * x + jnp.minimum(e, 0.0) * xe)
            return flux + [pltpu.roll(f, 1, 1) for f in flux]

        def finish(k, fluxes):
            lanes = lane_iota()
            mid, below, over = rows8(k, 8), pl.ds(k * 8 + 7, 8), pl.ds(k * 8 + 9, 8)
            for t in range(2):
                n = nv[l, t, mid, :] * face_y[t, mid, :]
                s = nv[l, t, below, :] * face_y[t, below, :]
                n_plus, n_minus = jnp.maximum(n, 0.0), jnp.minimum(n, 0.0)
                s_plus, s_minus = jnp.maximum(s, 0.0), jnp.minimum(s, 0.0)
                for c in range(2):
                    x = tr[c, l, t, mid, :]
                    fe = fluxes[2 * c + t]
                    fw = jnp.where(lanes == 0, fluxes[4 + 2 * c + 1 - t], fluxes[4 + 2 * c + t])
                    fn = n_plus * x + n_minus * tr[c, l, t, over, :]
                    fs = s_plus * tr[c, l, t, below, :] + s_minus * x
                    moved[c, l, t, rows8(k), :] = x - ((fe - fw) + (fn - fs))

        first, second = [], []
        n_blocks = rows // 8
        depth = min(AHEAD, n_blocks // 4)
        for k in range(depth):
            first.append(ahead(k))
        for k in range(depth):
            first.append(ahead(k + depth))
            second.append(east_flux(k, first.pop(0)))

        def step(k, carry):
            first, second = list(carry[0]), list(carry[1])
            first.append(ahead(k))
            second.append(east_flux(k - depth, first.pop(0)))
            finish(k - 2 * depth, second.pop(0))
            return first, second

        first, second = lax.fori_loop(
            2 * depth, n_blocks, step, (first, second), unroll=n_blocks - 2 * depth
        )
        for k in range(n_blocks, n_blocks + depth):
            second.append(east_flux(k - depth, first.pop(0)))
            finish(k - 2 * depth, second.pop(0))
        for k in range(n_blocks + depth, n_blocks + 2 * depth):
            finish(k - 2 * depth, second.pop(0))

    early = levels // 3
    for l in range(early):
        wait_level(l)
        advect(l)
    for l in range(early, levels):
        wait_level(l)
    loop(rows // 4 // edge_rows, pack_edges)
    send_edge_e = remote(15, own, got_w, dev(lat, lon_e))
    send_edge_w = remote(16, own, got_e, dev(lat, lon_w))
    send_edge_e.start()
    send_edge_w.start()

    for l in range(early, levels):
        advect(l)

    def unpack(value_w, value_e, n):
        lanes = lane_iota(n)
        both = jnp.where(lanes % 16 < 8, value_w, value_e)
        side = (lanes < 8) | (lanes >= LANES - 8)
        return [
            jnp.where(side, pltpu.roll(both, LANES - 16 * f - 8, 1), 0.0) for f in range(6)
        ]

    send_e.wait_recv()
    send_w.wait_recv()

    def unpack_ice(k):
        here = rows8(k, 0, pack_rows)
        for f, value in enumerate(unpack(ice_got_w[here, :], ice_got_e[here, :], pack_rows)):
            ext[f, 2, rows8(k, PAD, pack_rows), :] = value

    loop(rows // pack_rows, unpack_ice)

    @pl.when(inner_bottom)
    def _():
        send_ne.wait_recv()
        send_nw.wait_recv()
        for f, value in enumerate(unpack(corners[0], corners[1], HALO)):
            ext[f, 2, south_guard, :] = value

    @pl.when(bottom)
    def _():
        for f in range(6):
            for t in range(3):
                ext[f, t, south_guard, :] = zero

    @pl.when(inner_top | fold_w_far)
    def _():
        send_se.wait_recv()

    @pl.when(inner_top | fold_e_far)
    def _():
        send_sw.wait_recv()

    @pl.when(inner_top)
    def _():
        for f, value in enumerate(unpack(corners[2], corners[3], HALO)):
            ext[f, 2, north_guard, :] = value

    @pl.when(top)
    def _():
        for f, value in enumerate(unpack(corners[2], corners[3], HALO)):
            ext[f, 2, north_guard, :] = turned(f, value)

    send_edge_e.wait_recv()
    send_edge_w.wait_recv()

    def edge_update(k):
        n = edge_rows
        lanes = lane_iota(n)
        here = rows8(k, 0, n)
        x_own, s_own = own[0, here, :], own[1, here, :]
        e = got_w[1, here, :] * pltpu.roll(s_own, LANES - 1, 1)
        west = e * jnp.where(e > 0, got_w[0, here, :], pltpu.roll(x_own, LANES - 1, 1))
        e = s_own * pltpu.roll(got_e[1, here, :], LANES - 1, 1)
        east_flux = e * jnp.where(e > 0, x_own, pltpu.roll(got_e[0, here, :], LANES - 1, 1))
        both = jnp.where(lanes % 2 == 0, -east_flux, pltpu.roll(west, 1, 1))
        for q in range(4):
            at = rows8(k, q * (rows // 4), n)
            for c in range(2):
                for l in range(levels):
                    j = 32 * q + 2 * (c * levels + l)
                    value = pltpu.roll(both, LANES - 1 - j, 1)
                    moved[c, l, 0, at, :] += jnp.where(lanes == 0, value, 0.0)
                    moved[c, l, 1, at, :] += jnp.where(lanes == LANES - 1, value, 0.0)

    loop(rows // 4 // edge_rows, edge_update)

    def row(t, r):
        return pl.ds(r, 1), pl.ds(t * LANES, LANES)

    @pl.when(inner_bottom)
    def _():
        for copy in rims_n:
            copy.wait_recv()
        for t in range(2):
            rim = row(t, 7)
            face = (sea_s[rim] * sea[t, pl.ds(8, 1), :]).astype(F32)
            for l in range(levels):
                speed = rim_s[(2, l) + rim] * face
                for c in range(2):
                    value = jnp.where(speed > 0, rim_s[(c, l) + rim], tr[c, l, t, pl.ds(8, 1), :])
                    moved[c, l, t, pl.ds(0, 1), :] += speed * value

    @pl.when(inner_top)
    def _():
        for copy in rims_s:
            copy.wait_recv()
        mine = pl.ds(rows + 7, 1)
        for t in range(2):
            rim = row(t, 0)
            face = (sea[t, mine, :] * sea_n[rim]).astype(F32)
            for l in range(levels):
                speed = nv[l, t, mine, :] * face
                for c in range(2):
                    value = jnp.where(speed > 0, tr[c, l, t, mine, :], rim_n[(c, l) + rim])
                    moved[c, l, t, pl.ds(rows - 1, 1), :] -= speed * value

    @pl.when(inner_bottom)
    def _():
        send_n.wait_recv()
        for copy in [send_s, send_se, send_sw] + rims_s:
            copy.wait_send()

    @pl.when(inner_top)
    def _():
        for copy in [send_n, send_ne, send_nw] + rims_n:
            copy.wait_send()

    @pl.when(top)
    def _():
        send_fold.wait_send()

    @pl.when(fold_w_far)
    def _():
        send_fold_w.wait_send()

    @pl.when(fold_e_far)
    def _():
        send_fold_e.wait_send()

    send_s.wait_recv()
    for copy in (send_e, send_w, send_edge_e, send_edge_w):
        copy.wait_send()


N_REMOTE = 17
N_ICE_LOADS = 14


def ice_kernel(
    levels, rows, lat_count,
    moved, ext, east, north,
    temp_out, salt_out, u_out, v_out,
    vel, stress, turn, surf, water,
    load_sem, store_sem,
):
    n_ext = (rows + 2 * HALO) // 8
    ice_rows, last_rows = block(8 * n_ext, ICE_ROWS), block(rows, LAST_ROWS)
    lat = lax.axis_index("lat")
    grid_rows = rows * lat_count

    def cols(t):
        return pl.ds(t * LANES, LANES)

    loads, stores = [], []
    for i, src in enumerate((east, north)):
        for t in range(2):
            copy = pltpu.make_async_copy(
                src.at[0, :, cols(t)], water.at[i, t], load_sem.at[2 * i + t]
            )
            copy.start()
            loads.append(copy)

    def store(src, dst):
        copy = pltpu.make_async_copy(src, dst, store_sem.at[len(stores)])
        copy.start()
        stores.append(copy)

    for l in range(1, levels):
        for c, dst in enumerate((temp_out, salt_out)):
            for t in range(2):
                store(moved.at[c, l, t], dst.at[l, :, cols(t)])

    def turning(k):
        g = lat * rows - HALO + k * 8 + lax.broadcasted_iota(jnp.int32, (8, LANES), 0)
        g = jnp.where(g >= grid_rows, 2 * grid_rows - 1 - g, g)
        coriolis = 0.5 * (2 * g + 1 - grid_rows).astype(F32) / grid_rows
        b = 0.5 * coriolis
        inverse = 1.0 / (2.25 + b * b)
        turn[0, rows8(k), :] = 1.5 * inverse
        turn[1, rows8(k), :] = b * inverse

    loop(n_ext, turning)

    def stresses(src, fresh):
        def body(k):
            mid = rows8(k, 8, ice_rows)
            below, over = pl.ds(k * ice_rows + 7, ice_rows), pl.ds(k * ice_rows + 9, ice_rows)
            u = [src[0, t, mid, :] for t in range(3)]
            v = [src[1, t, mid, :] for t in range(3)]
            ue, uw = from_east(u), from_west(u)
            ve, vw = from_east(v), from_west(v)
            for t in range(3):
                dudx, dvdx = ue[t] - uw[t], ve[t] - vw[t]
                dudy = src[0, t, over, :] - src[0, t, below, :]
                dvdy = src[1, t, over, :] - src[1, t, below, :]
                div, ten, shr = dudx + dvdy, dudx - dvdy, dudy + dvdx
                p = ext[2, t, mid, :]
                third = ext[5, t, mid, :] * (1.0 / 3.0)
                zeta = p * lax.rsqrt(div * div + 0.25 * (ten * ten + shr * shr) + 1.0)
                quarter = 0.25 * zeta
                a = zeta * div - p
                b = quarter * ten
                sxx, syy, sxy = a + b, a - b, quarter * shr
                if not fresh:
                    sxx = stress[0, t, mid, :] + sxx
                    syy = stress[1, t, mid, :] + syy
                    sxy = stress[2, t, mid, :] + sxy
                stress[0, t, mid, :] = sxx * third
                stress[1, t, mid, :] = syy * third
                stress[2, t, mid, :] = sxy * third

        loop(8 * n_ext // ice_rows, body)

    def momentum(src, k, first, tiles, count):
        mid = rows8(k, first, count)
        below, over = pl.ds(k * count + first - 1, count), pl.ds(k * count + first + 1, count)
        sxx = [stress[0, t, mid, :] for t in range(3)]
        sxy = [stress[2, t, mid, :] for t in range(3)]
        xxe, xxw = from_east(sxx), from_west(sxx)
        xye, xyw = from_east(sxy), from_west(sxy)
        a, b = (turn[i, rows8(k, first - 8, count), :] for i in range(2))
        out = []
        for t in range(tiles):
            fx = (xxe[t] - xxw[t]) + (stress[2, t, over, :] - stress[2, t, below, :])
            fy = (xye[t] - xyw[t]) + (stress[1, t, over, :] - stress[1, t, below, :])
            ru = src[0, t, mid, :] + (0.25 * fx + ext[3, t, mid, :])
            rv = src[1, t, mid, :] + (0.25 * fy + ext[4, t, mid, :])
            covered = ext[5, t, mid, :]
            out.append(((a * ru + b * rv) * covered, (a * rv - b * ru) * covered))
        return out

    src = ext
    for subcycle in range(SUBCYCLES - 1):
        stresses(src, subcycle == 0)

        def body(k, src=src):
            for t, (u, v) in enumerate(momentum(src, k, 8, 3, ice_rows)):
                vel[0, t, rows8(k, 8, ice_rows), :] = u
                vel[1, t, rows8(k, 8, ice_rows), :] = v

        loop(8 * n_ext // ice_rows, body)
        src = vel
    stresses(src, False)
    for copy in loads:
        copy.wait()

    def final(k):
        here, mid = rows8(k, 0, last_rows), rows8(k, PAD, last_rows)
        for t, (u, v) in enumerate(momentum(vel, k, PAD, 2, last_rows)):
            vel[0, t, mid, :] = u
            vel[1, t, mid, :] = v
            slip_u = u - water[0, t, here, :]
            slip_v = v - water[1, t, here, :]
            sst, sss = moved[0, 0, t, here, :], moved[1, 0, t, here, :]
            heat = (
                0.1 * ext[5, t, mid, :]
                * (1.0 + (slip_u * slip_u + slip_v * slip_v))
                * (sst + 0.054 * sss)
            )
            surf[0, t, here, :] = sst - heat
            surf[1, t, here, :] = sss - 0.5 * heat

    loop(rows // last_rows, final)
    for t in range(2):
        store(vel.at[0, t, pl.ds(PAD, rows), :], u_out.at[:, cols(t)])
        store(vel.at[1, t, pl.ds(PAD, rows), :], v_out.at[:, cols(t)])
        store(surf.at[0, t], temp_out.at[0, :, cols(t)])
        store(surf.at[1, t], salt_out.at[0, :, cols(t)])
    for copy in stores:
        copy.wait()


def per_device(lat_count, lon_count, *args):
    temp = args[0]
    levels, rows, _ = temp.shape
    any_space = pl.BlockSpec(memory_space=pl.ANY)
    vmem_space = pl.BlockSpec(memory_space=pltpu.VMEM)
    deep = rows + 2 * PAD
    moved, ext = pl.pallas_call(
        functools.partial(ocean_kernel, levels, rows, lat_count, lon_count),
        out_shape=(
            pltpu.VMEM((2, levels, 2, rows, LANES), F32),
            pltpu.VMEM((6, 3, deep, LANES), F32),
        ),
        in_specs=[any_space] * 11,
        out_specs=(vmem_space, vmem_space),
        scratch_shapes=[
            pltpu.VMEM((2, levels, 2, rows + 16, LANES), F32),
            pltpu.VMEM((levels, 2, rows, LANES), F32),
            pltpu.VMEM((levels, 2, rows + 8, LANES), F32),
            pltpu.VMEM((2, rows + 16, LANES), jnp.int32),
            pltpu.VMEM((2, rows, LANES), jnp.int32),
            pltpu.VMEM((4, 2, rows, LANES), F32),
            pltpu.VMEM((2, rows + 8, LANES), F32),
            pltpu.VMEM((2, rows + 8, LANES), F32),
            pltpu.VMEM((3, levels, 8, 2 * LANES), F32),
            pltpu.VMEM((2, levels, 8, 2 * LANES), F32),
            pltpu.VMEM((8, 2 * LANES), jnp.int32),
            pltpu.VMEM((8, 2 * LANES), jnp.int32),
            pltpu.VMEM((4, HALO, LANES), F32),
        ]
        + [pltpu.VMEM((2, rows // 4, LANES), F32)] * 3
        + [pltpu.VMEM((rows, LANES), F32)] * 3
        + [
            pltpu.VMEM((6, 2, HALO, LANES), F32),
            pltpu.SemaphoreType.DMA((N_ICE_LOADS + 8 * levels,)),
            pltpu.SemaphoreType.DMA((N_REMOTE,)),
            pltpu.SemaphoreType.DMA((N_REMOTE,)),
        ],
        compiler_params=pltpu.CompilerParams(
            collective_id=0, has_side_effects=True, vmem_limit_bytes=48 * 1024 * 1024
        ),
        name="ocean",
    )(*args)
    moved = pltpu.with_memory_space_constraint(moved, pltpu.VMEM)
    ext = pltpu.with_memory_space_constraint(ext, pltpu.VMEM)
    shapes = (temp, temp, args[6], args[6])
    return pl.pallas_call(
        functools.partial(ice_kernel, levels, rows, lat_count),
        out_shape=tuple(jax.ShapeDtypeStruct(a.shape, a.dtype) for a in shapes),
        in_specs=[vmem_space, vmem_space, any_space, any_space],
        out_specs=(any_space,) * 4,
        scratch_shapes=[
            pltpu.VMEM((2, 3, deep, LANES), F32),
            pltpu.VMEM((3, 3, deep, LANES), F32),
            pltpu.VMEM((2, deep, LANES), F32),
            pltpu.VMEM((2, 2, rows, LANES), F32),
            pltpu.VMEM((2, 2, rows, LANES), F32),
            pltpu.SemaphoreType.DMA((4,)),
            pltpu.SemaphoreType.DMA((4 * (levels - 1) + 8,)),
        ],
        compiler_params=pltpu.CompilerParams(vmem_limit_bytes=48 * 1024 * 1024),
        name="ice",
    )(moved, ext, args[2], args[3])


def solution(mesh):
    deep, flat = P(None, "lat", "lon"), P("lat", "lon")
    return jax.shard_map(
        functools.partial(per_device, mesh.shape["lat"], mesh.shape["lon"]),
        mesh=mesh,
        in_specs=(deep,) * 4 + (flat,) * 7,
        out_specs=(deep, deep, flat, flat),
        check_vma=False,
    )
```

```python
import functools

import jax
import jax.numpy as jnp
from jax import lax
from jax.experimental import pallas as pl
from jax.experimental.pallas import tpu as pltpu
from jax.sharding import PartitionSpec as P

SUBCYCLES = 4
LANES = 128
HALO = 2 * SUBCYCLES
PAD = 16
MESH = pl.DeviceIdType.MESH
F32 = jnp.float32


def lane_iota(rows=8):
    return lax.broadcasted_iota(jnp.int32, (rows, LANES), 1)


ICE_ROWS = 8
LAST_ROWS = 8
PACK_ROWS = 48
FACE_ROWS = 8
EDGE_ROWS = 96
AHEAD = 8
EARLY = 1


def block(total, most):
    return max(n for n in range(8, most + 1, 8) if total % n == 0)


def rows8(k, first=0, count=8):
    start = k * count + first
    return pl.ds(start if isinstance(start, int) else pl.multiple_of(start, 8), count)


def loop(count, body):
    def step(k, carry):
        body(k)
        return carry

    lax.fori_loop(0, count, step, 0, unroll=count)


def from_east(tiles):
    rolled = [pltpu.roll(a, LANES - 1, 1) for a in tiles]
    n = len(tiles)
    lane = lane_iota(tiles[0].shape[0])
    return [jnp.where(lane == LANES - 1, rolled[(t + 1) % n], rolled[t]) for t in range(n)]


def from_west(tiles):
    rolled = [pltpu.roll(a, 1, 1) for a in tiles]
    n = len(tiles)
    lane = lane_iota(tiles[0].shape[0])
    return [jnp.where(lane == 0, rolled[(t - 1) % n], rolled[t]) for t in range(n)]


def ocean_kernel(
    levels, rows, lat_count, lon_count,
    temp, salt, east, north, land, icem, ice_u, ice_v, press, wind_x, wind_y,
    moved, ext,
    tr, ev, nv, sea, icb, uvw, face_x, face_y, rim_s, rim_n, rim_up, rim_down, corners,
    own, got_w, got_e, ice_own, ice_got_w, ice_got_e, fold,
    local_sem, send_sem, recv_sem,
):
    pack_rows, face_rows = block(rows, PACK_ROWS), block(rows + 8, FACE_ROWS)
    edge_rows = block(rows // 4, EDGE_ROWS)
    lat = lax.axis_index("lat")
    lon = lax.axis_index("lon")
    lon_e = lax.rem(lon + 1, lon_count)
    lon_w = lax.rem(lon + lon_count - 1, lon_count)
    top = lat == lat_count - 1
    bottom = lat == 0
    inner_top, inner_bottom = jnp.logical_not(top), jnp.logical_not(bottom)
    mirror = lon_count - 1 - lon
    fold_w = lax.rem(2 * lon_count - 2 - lon, lon_count)
    fold_e = lax.rem(lon_count - lon, lon_count)
    fold_w_far = top & (fold_w != lon)
    fold_e_far = top & (fold_e != lon)

    def dev(la, lo):
        return {"lat": la, "lon": lo}

    upper, lower = jnp.where(top, lat, lat + 1), jnp.where(bottom, lat, lat - 1)
    north_dev = dev(upper, jnp.where(top, mirror, lon))
    south_dev = dev(lower, lon)

    barrier = pltpu.get_barrier_semaphore()

    def greet(device):
        pl.semaphore_signal(barrier, inc=1, device_id=device, device_id_type=MESH)

    greet(dev(lat, lon_w))
    greet(dev(lat, lon_e))
    greet(north_dev)

    @pl.when(inner_top)
    def _():
        greet(dev(upper, lon_w))
        greet(dev(upper, lon_e))

    @pl.when(fold_w_far)
    def _():
        greet(dev(lat, fold_w))

    @pl.when(fold_e_far)
    def _():
        greet(dev(lat, fold_e))

    @pl.when(inner_bottom)
    def _():
        greet(south_dev)
        greet(dev(lower, lon_w))
        greet(dev(lower, lon_e))

    greeted = (
        3
        + 3 * inner_bottom.astype(jnp.int32)
        + 2 * inner_top.astype(jnp.int32)
        + fold_w_far.astype(jnp.int32)
        + fold_e_far.astype(jnp.int32)
    )

    started = []

    def load(src, dst):
        copy = pltpu.make_async_copy(src, dst, local_sem.at[len(started)])
        copy.start()
        started.append(copy)
        return copy

    def cols(t):
        return pl.ds(t * LANES, LANES)

    ice_loads = []
    for t in range(2):
        ice_loads += [
            load(land.at[:, cols(t)], sea.at[t, pl.ds(8, rows), :]),
            load(icem.at[:, cols(t)], icb.at[t]),
            load(ice_u.at[:, cols(t)], uvw.at[0, t]),
            load(ice_v.at[:, cols(t)], uvw.at[1, t]),
            load(wind_x.at[:, cols(t)], uvw.at[2, t]),
            load(wind_y.at[:, cols(t)], uvw.at[3, t]),
            load(press.at[:, cols(t)], ext.at[2, t, pl.ds(PAD, rows), :]),
        ]
    side_loads, north_loads = [], []

    def load_north(l):
        north_loads.append(
            [load(north.at[l, :, cols(t)], nv.at[l, t, pl.ds(8, rows), :]) for t in range(2)]
        )

    for l in range(levels):
        speeds = [load(east.at[l, :, cols(t)], ev.at[l, t]) for t in range(2)]
        if l < EARLY:
            load_north(l)
        for t in range(2):
            speeds += [
                load(temp.at[l, :, cols(t)], tr.at[0, l, t, pl.ds(8, rows), :]),
                load(salt.at[l, :, cols(t)], tr.at[1, l, t, pl.ds(8, rows), :]),
            ]
        side_loads.append(speeds)
    for l in range(EARLY, levels):
        load_north(l)

    zero = jnp.zeros((8, LANES), F32)
    for t in range(2):
        for edge in (0, rows + 8):
            sea[t, pl.ds(edge, 8), :] = jnp.zeros((8, LANES), jnp.int32)
            for l in range(levels):
                for c in range(2):
                    tr[c, l, t, pl.ds(edge, 8), :] = zero
        for l in range(levels):
            nv[l, t, pl.ds(0, 8), :] = zero

    def remote(i, src, dst, device, arrival=None):
        return pltpu.make_async_remote_copy(
            src_ref=src, dst_ref=dst, send_sem=send_sem.at[i],
            recv_sem=recv_sem.at[i if arrival is None else arrival],
            device_id=device, device_id_type=MESH,
        )

    for copy in ice_loads:
        copy.wait()
    for copy in side_loads[0][:2] + north_loads[0]:
        copy.wait()

    def pack_ice(k):
        n = pack_rows
        here, mid, out = rows8(k, 0, n), rows8(k, 8, n), rows8(k, PAD, n)
        lanes = lane_iota(n)
        fields = []
        for t in range(2):
            covered = (sea[t, mid, :] * icb[t, here, :]).astype(F32)
            third = covered * (1.0 / 3.0)
            mine = (
                uvw[0, t, here, :] * covered,
                uvw[1, t, here, :] * covered,
                ext[2, t, out, :],
                0.5 * (uvw[2, t, here, :] + ev[0, t, here, :]),
                0.5 * (uvw[3, t, here, :] + nv[0, t, mid, :]),
                third,
            )
            for f in (0, 1, 3, 4, 5):
                ext[f, t, out, :] = mine[f]
            fields.append(mine)
        packed = jnp.zeros((n, LANES), F32)
        for f in range(6):
            both = jnp.where(lanes < HALO, fields[0][f], fields[1][f])
            both = pltpu.roll(both, 16 * f + 8, 1)
            packed = jnp.where((lanes >= 16 * f) & (lanes < 16 * f + 16), both, packed)
        ice_own[here, :] = packed

    loop(rows // pack_rows, pack_ice)

    top_rows = pl.ds(PAD + rows - HALO, HALO)
    low_rows = pl.ds(PAD, HALO)
    north_guard = pl.ds(PAD + rows, HALO)
    south_guard = pl.ds(PAD - HALO, HALO)

    def turned(f, value):
        value = jnp.concatenate([value[r : r + 1] for r in range(HALO - 1, -1, -1)], axis=0)
        value = jnp.take_along_axis(value, LANES - 1 - lane_iota(), axis=1)
        return -value if f in (0, 1, 3, 4) else value

    @pl.when(top)
    def _():
        for f in range(6):
            for t in range(2):
                fold[f, 1 - t, :, :] = turned(f, ext[f, t, top_rows, :])

    def faces(k):
        n = face_rows
        here = rows8(k, 0, n)
        s = [sea[t, here, :].astype(F32) for t in range(2)]
        for t in range(2):
            up = sea[t, pl.ds(k * n + 1, n), :].astype(F32)
            face_y[t, here, :] = s[t] * up
        se = from_east(s)
        face_x[0, here, :] = s[0] * se[0]
        face_x[1, here, :] = jnp.where(lane_iota(n) == LANES - 1, 0.0, s[1] * se[1])

    loop((rows + 8) // face_rows, faces)

    pl.semaphore_wait(barrier, greeted)

    send_e = remote(0, ice_own, ice_got_w, dev(lat, lon_e))
    send_w = remote(1, ice_own, ice_got_e, dev(lat, lon_w))
    send_e.start()
    send_w.start()
    wide = pl.ds(0, 2)
    send_n = remote(
        2, ext.at[:, wide, top_rows, :], ext.at[:, wide, south_guard, :], north_dev
    )
    send_s = remote(
        3, ext.at[:, wide, low_rows, :], ext.at[:, wide, north_guard, :], south_dev
    )
    send_fold = remote(2, fold, ext.at[:, wide, north_guard, :], north_dev, arrival=3)
    slab_top, slab_low = ice_own.at[pl.ds(rows - HALO, HALO)], ice_own.at[pl.ds(0, HALO)]
    send_ne = remote(4, slab_top, corners.at[0], dev(upper, lon_e))
    send_nw = remote(5, slab_top, corners.at[1], dev(upper, lon_w))
    send_se = remote(6, slab_low, corners.at[2], dev(lower, lon_e))
    send_sw = remote(7, slab_low, corners.at[3], dev(lower, lon_w))
    send_fold_w = remote(4, slab_top, corners.at[2], dev(lat, fold_w), arrival=6)
    send_fold_e = remote(5, slab_top, corners.at[3], dev(lat, fold_e), arrival=7)

    @pl.when(inner_top)
    def _():
        for copy in (send_n, send_ne, send_nw):
            copy.start()

    @pl.when(inner_bottom)
    def _():
        for copy in (send_s, send_se, send_sw):
            copy.start()

    @pl.when(top)
    def _():
        send_fold.start()

    @pl.when(fold_w_far)
    def _():
        send_fold_w.start()

    @pl.when(fold_e_far)
    def _():
        send_fold_e.start()

    @pl.when(top & (fold_w == lon))
    def _():
        corners[2, :, :] = ice_own[pl.ds(rows - HALO, HALO), :]

    @pl.when(top & (fold_e == lon))
    def _():
        corners[3, :, :] = ice_own[pl.ds(rows - HALO, HALO), :]

    def pack_edges(l):
        def body(k):
            n = edge_rows
            lanes = lane_iota(n)
            place = lanes % 32
            out = rows8(k, 0, n)
            if l:
                value, speed = own[0, out, :], own[1, out, :]
            else:
                value = speed = jnp.zeros((n, LANES), F32)
            for q in range(4):
                first_row = q * (rows // 4)
                here, mid = rows8(k, first_row, n), rows8(k, first_row + 8, n)
                for c in range(2):
                    j = 32 * q + 2 * (c * levels + l)
                    both = jnp.where(lanes == 0, tr[c, l, 0, mid, :], tr[c, l, 1, mid, :])
                    both = pltpu.roll(both, j + 1, 1)
                    value = jnp.where((lanes == j) | (lanes == j + 1), both, value)
                sea_e = sea[1, mid, :].astype(F32)
                j = 32 * q + 2 * l
                pushed = pltpu.roll(ev[l, 1, here, :] * sea_e, j + 1, 1)
                speed = jnp.where(lanes == j, pushed, speed)
                if not l:
                    sea_w = sea[0, mid, pl.ds(0, 1)].astype(F32)
                    odd = (lanes >= 32 * q) & (lanes < 32 * q + 32) & (lanes % 2 == 1)
                    speed = jnp.where(odd, jnp.broadcast_to(sea_w, (n, LANES)), speed)
            if l == levels - 1:
                again = (place >= 2 * levels) & (place < 4 * levels) & (place % 2 == 0)
                speed = jnp.where(again, pltpu.roll(speed, 2 * levels, 1), speed)
            own[0, out, :] = value
            own[1, out, :] = speed

        loop(rows // 4 // edge_rows, body)

    def pack_rim(out, row, with_speed):
        out[pl.ds(out.shape[0] - 8, 8), :] = jnp.zeros((8, 2 * LANES), F32)
        for t in range(2):
            at = pl.ds(t * LANES, LANES)
            for l in range(levels):
                for c in range(2):
                    out[pl.ds(c * levels + l, 1), at] = tr[c, l, t, row, :]
                if with_speed:
                    out[pl.ds(2 * levels + l, 1), at] = nv[l, t, row, :]
            out[pl.ds(3 * levels, 1), at] = sea[t, row, :].astype(F32)

    both = [(c, t) for c in range(2) for t in range(2)]

    def advect(l):
        def ahead(k):
            return [pltpu.roll(tr[c, l, t, rows8(k, 8), :], LANES - 1, 1) for c, t in both]

        def east_flux(k, rolled):
            lanes = lane_iota()
            flux = []
            for c in range(2):
                a, b = rolled[2 * c], rolled[2 * c + 1]
                for t, xe in enumerate(
                    (jnp.where(lanes == LANES - 1, b, a), jnp.where(lanes == LANES - 1, a, b))
                ):
                    e = ev[l, t, rows8(k), :] * face_x[t, rows8(k, 8), :]
                    x = tr[c, l, t, rows8(k, 8), :]
                    flux.append(jnp.maximum(e, 0.0) * x + jnp.minimum(e, 0.0) * xe)
            return flux + [pltpu.roll(f, 1, 1) for f in flux]

        def finish(k, fluxes):
            lanes = lane_iota()
            mid, below, over = rows8(k, 8), pl.ds(k * 8 + 7, 8), pl.ds(k * 8 + 9, 8)
            for t in range(2):
                n = nv[l, t, mid, :] * face_y[t, mid, :]
                s = nv[l, t, below, :] * face_y[t, below, :]
                n_plus, n_minus = jnp.maximum(n, 0.0), jnp.minimum(n, 0.0)
                s_plus, s_minus = jnp.maximum(s, 0.0), jnp.minimum(s, 0.0)
                for c in range(2):
                    x = tr[c, l, t, mid, :]
                    fe = fluxes[2 * c + t]
                    fw = jnp.where(lanes == 0, fluxes[4 + 2 * c + 1 - t], fluxes[4 + 2 * c + t])
                    fn = n_plus * x + n_minus * tr[c, l, t, over, :]
                    fs = s_plus * tr[c, l, t, below, :] + s_minus * x
                    moved[c, l, t, rows8(k), :] = x - ((fe - fw) + (fn - fs))

        first, second = [], []
        n_blocks = rows // 8
        depth = min(AHEAD, n_blocks // 4)
        for k in range(depth):
            first.append(ahead(k))
        for k in range(depth):
            first.append(ahead(k + depth))
            second.append(east_flux(k, first.pop(0)))

        def step(k, carry):
            first, second = list(carry[0]), list(carry[1])
            first.append(ahead(k))
            second.append(east_flux(k - depth, first.pop(0)))
            finish(k - 2 * depth, second.pop(0))
            return first, second

        first, second = lax.fori_loop(
            2 * depth, n_blocks, step, (first, second), unroll=n_blocks - 2 * depth
        )
        for k in range(n_blocks, n_blocks + depth):
            second.append(east_flux(k - depth, first.pop(0)))
            finish(k - 2 * depth, second.pop(0))
        for k in range(n_blocks + depth, n_blocks + 2 * depth):
            finish(k - 2 * depth, second.pop(0))

    for l in range(levels):
        for copy in side_loads[l][2 if l == 0 else 0 :]:
            copy.wait()
        pack_edges(l)
        if l < EARLY:
            if l:
                for copy in north_loads[l]:
                    copy.wait()
            advect(l)
    send_edge_e = remote(8, own, got_w, dev(lat, lon_e))
    send_edge_w = remote(9, own, got_e, dev(lat, lon_w))
    send_edge_e.start()
    send_edge_w.start()
    for l in range(EARLY, levels):
        for copy in north_loads[l]:
            copy.wait()
    send_rim_n = remote(10, rim_up, rim_s, north_dev)
    send_rim_s = remote(11, rim_down, rim_n, south_dev)

    @pl.when(inner_top)
    def _():
        pack_rim(rim_up, pl.ds(rows + 7, 1), True)
        send_rim_n.start()

    @pl.when(inner_bottom)
    def _():
        pack_rim(rim_down, pl.ds(8, 1), False)
        send_rim_s.start()

    for l in range(EARLY, levels):
        advect(l)

    def unpack(value_w, value_e, n):
        lanes = lane_iota(n)
        both = jnp.where(lanes % 16 < 8, value_w, value_e)
        side = (lanes < 8) | (lanes >= LANES - 8)
        return [
            jnp.where(side, pltpu.roll(both, LANES - 16 * f - 8, 1), 0.0) for f in range(6)
        ]

    send_e.wait_recv()
    send_w.wait_recv()

    def unpack_ice(k):
        here = rows8(k, 0, pack_rows)
        for f, value in enumerate(unpack(ice_got_w[here, :], ice_got_e[here, :], pack_rows)):
            ext[f, 2, rows8(k, PAD, pack_rows), :] = value

    loop(rows // pack_rows, unpack_ice)

    @pl.when(inner_bottom)
    def _():
        send_ne.wait_recv()
        send_nw.wait_recv()
        for f, value in enumerate(unpack(corners[0], corners[1], HALO)):
            ext[f, 2, south_guard, :] = value

    @pl.when(bottom)
    def _():
        for f in range(6):
            for t in range(3):
                ext[f, t, south_guard, :] = zero

    @pl.when(inner_top | fold_w_far)
    def _():
        send_se.wait_recv()

    @pl.when(inner_top | fold_e_far)
    def _():
        send_sw.wait_recv()

    @pl.when(inner_top)
    def _():
        for f, value in enumerate(unpack(corners[2], corners[3], HALO)):
            ext[f, 2, north_guard, :] = value

    @pl.when(top)
    def _():
        for f, value in enumerate(unpack(corners[2], corners[3], HALO)):
            ext[f, 2, north_guard, :] = turned(f, value)

    def rim_row(i, t):
        return pl.ds(i, 1), pl.ds(t * LANES, LANES)

    @pl.when(inner_bottom)
    def _():
        send_rim_n.wait_recv()
        mine = pl.ds(8, 1)
        for t in range(2):
            face = rim_s[rim_row(3 * levels, t)] * sea[t, mine, :].astype(F32)
            for l in range(levels):
                speed = rim_s[rim_row(2 * levels + l, t)] * face
                for c in range(2):
                    there = rim_s[rim_row(c * levels + l, t)]
                    value = jnp.where(speed > 0, there, tr[c, l, t, mine, :])
                    moved[c, l, t, pl.ds(0, 1), :] += speed * value

    @pl.when(inner_top)
    def _():
        send_rim_s.wait_recv()
        mine = pl.ds(rows + 7, 1)
        for t in range(2):
            face = sea[t, mine, :].astype(F32) * rim_n[rim_row(3 * levels, t)]
            for l in range(levels):
                speed = nv[l, t, mine, :] * face
                for c in range(2):
                    there = rim_n[rim_row(c * levels + l, t)]
                    value = jnp.where(speed > 0, tr[c, l, t, mine, :], there)
                    moved[c, l, t, pl.ds(rows - 1, 1), :] -= speed * value

    send_edge_e.wait_recv()
    send_edge_w.wait_recv()

    def edge_update(k):
        n = edge_rows
        lanes = lane_iota(n)
        here = rows8(k, 0, n)
        x_own, s_own = own[0, here, :], own[1, here, :]
        e = got_w[1, here, :] * pltpu.roll(s_own, LANES - 1, 1)
        west = e * jnp.where(e > 0, got_w[0, here, :], pltpu.roll(x_own, LANES - 1, 1))
        e = s_own * pltpu.roll(got_e[1, here, :], LANES - 1, 1)
        east_flux = e * jnp.where(e > 0, x_own, pltpu.roll(got_e[0, here, :], LANES - 1, 1))
        both = jnp.where(lanes % 2 == 0, -east_flux, pltpu.roll(west, 1, 1))
        for q in range(4):
            at = rows8(k, q * (rows // 4), n)
            for c in range(2):
                for l in range(levels):
                    j = 32 * q + 2 * (c * levels + l)
                    value = pltpu.roll(both, LANES - 1 - j, 1)
                    moved[c, l, 0, at, :] += jnp.where(lanes == 0, value, 0.0)
                    moved[c, l, 1, at, :] += jnp.where(lanes == LANES - 1, value, 0.0)

    loop(rows // 4 // edge_rows, edge_update)

    @pl.when(inner_bottom)
    def _():
        send_n.wait_recv()
        for copy in (send_s, send_se, send_sw, send_rim_s):
            copy.wait_send()

    @pl.when(inner_top)
    def _():
        for copy in (send_n, send_ne, send_nw, send_rim_n):
            copy.wait_send()

    @pl.when(top)
    def _():
        send_fold.wait_send()

    @pl.when(fold_w_far)
    def _():
        send_fold_w.wait_send()

    @pl.when(fold_e_far)
    def _():
        send_fold_e.wait_send()

    send_s.wait_recv()
    for copy in (send_e, send_w, send_edge_e, send_edge_w):
        copy.wait_send()


N_REMOTE = 12
N_ICE_LOADS = 14


def ice_kernel(
    levels, rows, lat_count,
    moved, ext, east, north,
    temp_out, salt_out, u_out, v_out,
    vel, stress, turn, surf, water,
    load_sem, store_sem,
):
    n_ext = (rows + 2 * HALO) // 8
    ice_rows, last_rows = block(8 * n_ext, ICE_ROWS), block(rows, LAST_ROWS)
    lat = lax.axis_index("lat")
    grid_rows = rows * lat_count

    def cols(t):
        return pl.ds(t * LANES, LANES)

    loads, stores = [], []
    for i, src in enumerate((east, north)):
        for t in range(2):
            copy = pltpu.make_async_copy(
                src.at[0, :, cols(t)], water.at[i, t], load_sem.at[2 * i + t]
            )
            copy.start()
            loads.append(copy)

    def store(src, dst):
        copy = pltpu.make_async_copy(src, dst, store_sem.at[len(stores)])
        copy.start()
        stores.append(copy)

    for l in range(1, levels):
        for c, dst in enumerate((temp_out, salt_out)):
            for t in range(2):
                store(moved.at[c, l, t], dst.at[l, :, cols(t)])

    def turning(k):
        g = lat * rows - HALO + k * 8 + lax.broadcasted_iota(jnp.int32, (8, LANES), 0)
        g = jnp.where(g >= grid_rows, 2 * grid_rows - 1 - g, g)
        coriolis = 0.5 * (2 * g + 1 - grid_rows).astype(F32) / grid_rows
        b = 0.5 * coriolis
        inverse = 1.0 / (2.25 + b * b)
        turn[0, rows8(k), :] = 4.5 * inverse
        turn[1, rows8(k), :] = 3.0 * b * inverse

    loop(n_ext, turning)

    def stresses(src, fresh):
        def body(k):
            mid = rows8(k, 8, ice_rows)
            below, over = pl.ds(k * ice_rows + 7, ice_rows), pl.ds(k * ice_rows + 9, ice_rows)
            u = [src[0, t, mid, :] for t in range(3)]
            v = [src[1, t, mid, :] for t in range(3)]
            ue, uw = from_east(u), from_west(u)
            ve, vw = from_east(v), from_west(v)
            for t in range(3):
                dudx, dvdx = ue[t] - uw[t], ve[t] - vw[t]
                dudy = src[0, t, over, :] - src[0, t, below, :]
                dvdy = src[1, t, over, :] - src[1, t, below, :]
                div, ten, shr = dudx + dvdy, dudx - dvdy, dudy + dvdx
                p = ext[2, t, mid, :]
                third = ext[5, t, mid, :]
                zeta = p * lax.rsqrt(div * div + 0.25 * (ten * ten + shr * shr) + 1.0)
                quarter = 0.25 * zeta
                a = zeta * div - p
                b = quarter * ten
                sxx, syy, sxy = a + b, a - b, quarter * shr
                if not fresh:
                    sxx = stress[0, t, mid, :] + sxx
                    syy = stress[1, t, mid, :] + syy
                    sxy = stress[2, t, mid, :] + sxy
                stress[0, t, mid, :] = sxx * third
                stress[1, t, mid, :] = syy * third
                stress[2, t, mid, :] = sxy * third

        loop(8 * n_ext // ice_rows, body)

    def momentum(src, k, first, tiles, count):
        mid = rows8(k, first, count)
        below, over = pl.ds(k * count + first - 1, count), pl.ds(k * count + first + 1, count)
        sxx = [stress[0, t, mid, :] for t in range(3)]
        sxy = [stress[2, t, mid, :] for t in range(3)]
        xxe, xxw = from_east(sxx), from_west(sxx)
        xye, xyw = from_east(sxy), from_west(sxy)
        a, b = (turn[i, rows8(k, first - 8, count), :] for i in range(2))
        out = []
        for t in range(tiles):
            fx = (xxe[t] - xxw[t]) + (stress[2, t, over, :] - stress[2, t, below, :])
            fy = (xye[t] - xyw[t]) + (stress[1, t, over, :] - stress[1, t, below, :])
            ru = src[0, t, mid, :] + (0.25 * fx + ext[3, t, mid, :])
            rv = src[1, t, mid, :] + (0.25 * fy + ext[4, t, mid, :])
            third = ext[5, t, mid, :]
            out.append(((a * ru + b * rv) * third, (a * rv - b * ru) * third))
        return out

    src = ext
    for subcycle in range(SUBCYCLES - 1):
        stresses(src, subcycle == 0)

        def body(k, src=src):
            for t, (u, v) in enumerate(momentum(src, k, 8, 3, ice_rows)):
                vel[0, t, rows8(k, 8, ice_rows), :] = u
                vel[1, t, rows8(k, 8, ice_rows), :] = v

        loop(8 * n_ext // ice_rows, body)
        src = vel
    stresses(src, False)
    for copy in loads:
        copy.wait()

    def final(k):
        here, mid = rows8(k, 0, last_rows), rows8(k, PAD, last_rows)
        for t, (u, v) in enumerate(momentum(vel, k, PAD, 2, last_rows)):
            vel[0, t, mid, :] = u
            vel[1, t, mid, :] = v
            slip_u = u - water[0, t, here, :]
            slip_v = v - water[1, t, here, :]
            sst, sss = moved[0, 0, t, here, :], moved[1, 0, t, here, :]
            heat = (
                0.3 * ext[5, t, mid, :]
                * (1.0 + (slip_u * slip_u + slip_v * slip_v))
                * (sst + 0.054 * sss)
            )
            surf[0, t, here, :] = sst - heat
            surf[1, t, here, :] = sss - 0.5 * heat

    loop(rows // last_rows, final)
    for t in range(2):
        store(vel.at[0, t, pl.ds(PAD, rows), :], u_out.at[:, cols(t)])
        store(vel.at[1, t, pl.ds(PAD, rows), :], v_out.at[:, cols(t)])
        store(surf.at[0, t], temp_out.at[0, :, cols(t)])
        store(surf.at[1, t], salt_out.at[0, :, cols(t)])
    for copy in stores:
        copy.wait()


def per_device(lat_count, lon_count, *args):
    temp = args[0]
    levels, rows, _ = temp.shape
    any_space = pl.BlockSpec(memory_space=pl.ANY)
    vmem_space = pl.BlockSpec(memory_space=pltpu.VMEM)
    deep = rows + 2 * PAD
    moved, ext = pl.pallas_call(
        functools.partial(ocean_kernel, levels, rows, lat_count, lon_count),
        out_shape=(
            pltpu.VMEM((2, levels, 2, rows, LANES), F32),
            pltpu.VMEM((6, 3, deep, LANES), F32),
        ),
        in_specs=[any_space] * 11,
        out_specs=(vmem_space, vmem_space),
        scratch_shapes=[
            pltpu.VMEM((2, levels, 2, rows + 16, LANES), F32),
            pltpu.VMEM((levels, 2, rows, LANES), F32),
            pltpu.VMEM((levels, 2, rows + 8, LANES), F32),
            pltpu.VMEM((2, rows + 16, LANES), jnp.int32),
            pltpu.VMEM((2, rows, LANES), jnp.int32),
            pltpu.VMEM((4, 2, rows, LANES), F32),
            pltpu.VMEM((2, rows + 8, LANES), F32),
            pltpu.VMEM((2, rows + 8, LANES), F32),
        ]
        + [pltpu.VMEM((8 * pl.cdiv(3 * levels + 1, 8), 2 * LANES), F32)] * 4
        + [
            pltpu.VMEM((4, HALO, LANES), F32),
        ]
        + [pltpu.VMEM((2, rows // 4, LANES), F32)] * 3
        + [pltpu.VMEM((rows, LANES), F32)] * 3
        + [
            pltpu.VMEM((6, 2, HALO, LANES), F32),
            pltpu.SemaphoreType.DMA((N_ICE_LOADS + 8 * levels,)),
            pltpu.SemaphoreType.DMA((N_REMOTE,)),
            pltpu.SemaphoreType.DMA((N_REMOTE,)),
        ],
        compiler_params=pltpu.CompilerParams(
            collective_id=0, has_side_effects=True, vmem_limit_bytes=48 * 1024 * 1024
        ),
        name="ocean",
    )(*args)
    moved = pltpu.with_memory_space_constraint(moved, pltpu.VMEM)
    ext = pltpu.with_memory_space_constraint(ext, pltpu.VMEM)
    shapes = (temp, temp, args[6], args[6])
    return pl.pallas_call(
        functools.partial(ice_kernel, levels, rows, lat_count),
        out_shape=tuple(jax.ShapeDtypeStruct(a.shape, a.dtype) for a in shapes),
        in_specs=[vmem_space, vmem_space, any_space, any_space],
        out_specs=(any_space,) * 4,
        scratch_shapes=[
            pltpu.VMEM((2, 3, deep, LANES), F32),
            pltpu.VMEM((3, 3, deep, LANES), F32),
            pltpu.VMEM((2, deep, LANES), F32),
            pltpu.VMEM((2, 2, rows, LANES), F32),
            pltpu.VMEM((2, 2, rows, LANES), F32),
            pltpu.SemaphoreType.DMA((4,)),
            pltpu.SemaphoreType.DMA((4 * (levels - 1) + 8,)),
        ],
        compiler_params=pltpu.CompilerParams(vmem_limit_bytes=48 * 1024 * 1024),
        name="ice",
    )(moved, ext, args[2], args[3])


def solution(mesh):
    deep, flat = P(None, "lat", "lon"), P("lat", "lon")
    return jax.shard_map(
        functools.partial(per_device, mesh.shape["lat"], mesh.shape["lon"]),
        mesh=mesh,
        in_specs=(deep,) * 4 + (flat,) * 7,
        out_specs=(deep, deep, flat, flat),
        check_vma=False,
    )
```

```python
import functools

import jax
import jax.numpy as jnp
from jax import lax
from jax.experimental import pallas as pl
from jax.experimental.pallas import tpu as pltpu
from jax.sharding import PartitionSpec as P

SUBCYCLES = 4
LANES = 128
HALO = 2 * SUBCYCLES
PAD = 16
MESH = pl.DeviceIdType.MESH
F32 = jnp.float32


def lane_iota(rows=8):
    return lax.broadcasted_iota(jnp.int32, (rows, LANES), 1)


ICE_ROWS = 8
LAST_ROWS = 8
GROUPS = 2
PACK_ROWS = 96
FACE_ROWS = 8
EDGE_ROWS = 96
AHEAD = 8
EARLY = 1


def block(total, most):
    return max(n for n in range(8, most + 1, 8) if total % n == 0)


def rows8(k, first=0, count=8):
    start = k * count + first
    return pl.ds(start if isinstance(start, int) else pl.multiple_of(start, 8), count)


def loop(count, body):
    def step(k, carry):
        body(k)
        return carry

    lax.fori_loop(0, count, step, 0, unroll=count)


def from_east(tiles):
    rolled = [pltpu.roll(a, LANES - 1, 1) for a in tiles]
    n = len(tiles)
    lane = lane_iota(tiles[0].shape[0])
    return [jnp.where(lane == LANES - 1, rolled[(t + 1) % n], rolled[t]) for t in range(n)]


def from_west(tiles):
    rolled = [pltpu.roll(a, 1, 1) for a in tiles]
    n = len(tiles)
    lane = lane_iota(tiles[0].shape[0])
    return [jnp.where(lane == 0, rolled[(t - 1) % n], rolled[t]) for t in range(n)]


def ocean_kernel(
    levels, rows, lat_count, lon_count,
    temp, salt, east, north, land, icem, ice_u, ice_v, press, wind_x, wind_y,
    moved, ext, turn,
    tr, ev, nv, sea, icb, uvw, face_x, face_y, rim_s, rim_n, rim_up, rim_down, corners,
    own, own_e, own_w, got_w, got_e, ice_own, ice_e, ice_w, ice_got_w, ice_got_e, fold,
    local_sem, send_sem, recv_sem,
):
    pack_rows, face_rows = block(rows, PACK_ROWS), block(rows + 8, FACE_ROWS)
    edge_rows, half_rows = block(rows // 4, EDGE_ROWS), block(rows // 2, PACK_ROWS)
    lat = lax.axis_index("lat")
    lon = lax.axis_index("lon")
    lon_e = lax.rem(lon + 1, lon_count)
    lon_w = lax.rem(lon + lon_count - 1, lon_count)
    top = lat == lat_count - 1
    bottom = lat == 0
    inner_top, inner_bottom = jnp.logical_not(top), jnp.logical_not(bottom)
    mirror = lon_count - 1 - lon
    fold_w = lax.rem(2 * lon_count - 2 - lon, lon_count)
    fold_e = lax.rem(lon_count - lon, lon_count)
    fold_w_far = top & (fold_w != lon)
    fold_e_far = top & (fold_e != lon)

    def dev(la, lo):
        return {"lat": la, "lon": lo}

    upper, lower = jnp.where(top, lat, lat + 1), jnp.where(bottom, lat, lat - 1)
    north_dev = dev(upper, jnp.where(top, mirror, lon))
    south_dev = dev(lower, lon)

    barrier = pltpu.get_barrier_semaphore()

    def greet(device):
        pl.semaphore_signal(barrier, inc=1, device_id=device, device_id_type=MESH)

    greet(dev(lat, lon_w))
    greet(dev(lat, lon_e))
    greet(north_dev)

    @pl.when(inner_top)
    def _():
        greet(dev(upper, lon_w))
        greet(dev(upper, lon_e))

    @pl.when(fold_w_far)
    def _():
        greet(dev(lat, fold_w))

    @pl.when(fold_e_far)
    def _():
        greet(dev(lat, fold_e))

    @pl.when(inner_bottom)
    def _():
        greet(south_dev)
        greet(dev(lower, lon_w))
        greet(dev(lower, lon_e))

    greeted = (
        3
        + 3 * inner_bottom.astype(jnp.int32)
        + 2 * inner_top.astype(jnp.int32)
        + fold_w_far.astype(jnp.int32)
        + fold_e_far.astype(jnp.int32)
    )

    started = []

    def load(src, dst):
        copy = pltpu.make_async_copy(src, dst, local_sem.at[len(started)])
        copy.start()
        started.append(copy)
        return copy

    def cols(t):
        return pl.ds(t * LANES, LANES)

    ice_loads = []
    for t in range(2):
        ice_loads += [
            load(land.at[:, cols(t)], sea.at[t, pl.ds(8, rows), :]),
            load(icem.at[:, cols(t)], icb.at[t]),
            load(ice_u.at[:, cols(t)], uvw.at[0, t]),
            load(ice_v.at[:, cols(t)], uvw.at[1, t]),
            load(wind_x.at[:, cols(t)], uvw.at[2, t]),
            load(wind_y.at[:, cols(t)], uvw.at[3, t]),
            load(press.at[:, cols(t)], ext.at[2, t, pl.ds(PAD, rows), :]),
        ]
    side_loads, north_loads = [], []

    def load_north(l):
        north_loads.append(
            [load(north.at[l, :, cols(t)], nv.at[l, t, pl.ds(8, rows), :]) for t in range(2)]
        )

    for l in range(levels):
        speeds = [load(east.at[l, :, cols(t)], ev.at[l, t]) for t in range(2)]
        if l < EARLY:
            load_north(l)
        for t in range(2):
            speeds += [
                load(temp.at[l, :, cols(t)], tr.at[0, l, t, pl.ds(8, rows), :]),
                load(salt.at[l, :, cols(t)], tr.at[1, l, t, pl.ds(8, rows), :]),
            ]
        side_loads.append(speeds)
    for l in range(EARLY, levels):
        load_north(l)

    def turning(k):
        g = lat * rows - HALO + k * 8 + lax.broadcasted_iota(jnp.int32, (8, LANES), 0)
        g = jnp.where(g >= grid_rows, 2 * grid_rows - 1 - g, g)
        coriolis = 0.5 * (2 * g + 1 - grid_rows).astype(F32) / grid_rows
        b = 0.5 * coriolis
        inverse = 1.0 / (2.25 + b * b)
        turn[0, rows8(k), :] = 4.5 * inverse
        turn[1, rows8(k), :] = 3.0 * b * inverse

    grid_rows = rows * lat_count
    loop((rows + 2 * HALO) // 8, turning)

    zero = jnp.zeros((8, LANES), F32)
    for t in range(2):
        for edge in (0, rows + 8):
            sea[t, pl.ds(edge, 8), :] = jnp.zeros((8, LANES), jnp.int32)
            for l in range(levels):
                for c in range(2):
                    tr[c, l, t, pl.ds(edge, 8), :] = zero
        for l in range(levels):
            nv[l, t, pl.ds(0, 8), :] = zero

    def remote(i, src, dst, device, arrival=None):
        return pltpu.make_async_remote_copy(
            src_ref=src, dst_ref=dst, send_sem=send_sem.at[i],
            recv_sem=recv_sem.at[i if arrival is None else arrival],
            device_id=device, device_id_type=MESH,
        )

    for copy in ice_loads:
        copy.wait()
    for copy in side_loads[0][:2] + north_loads[0]:
        copy.wait()

    def pack_ice(k):
        n = pack_rows
        here, mid, out = rows8(k, 0, n), rows8(k, 8, n), rows8(k, PAD, n)
        lanes = lane_iota(n)
        fields = []
        for t in range(2):
            covered = (sea[t, mid, :] * icb[t, here, :]).astype(F32)
            third = covered * (1.0 / 3.0)
            mine = (
                uvw[0, t, here, :] * covered,
                uvw[1, t, here, :] * covered,
                ext[2, t, out, :],
                0.5 * (uvw[2, t, here, :] + ev[0, t, here, :]),
                0.5 * (uvw[3, t, here, :] + nv[0, t, mid, :]),
                third,
            )
            for f in (0, 1, 3, 4, 5):
                ext[f, t, out, :] = mine[f]
            fields.append(mine)
        packed = jnp.zeros((n, LANES), F32)
        for f in range(6):
            both = jnp.where(lanes < HALO, fields[0][f], fields[1][f])
            both = pltpu.roll(both, 16 * f + 8, 1)
            packed = jnp.where((lanes >= 16 * f) & (lanes < 16 * f + 16), both, packed)
        ice_own[here, :] = packed

    loop(rows // pack_rows, pack_ice)

    def halve(k):
        upper = ice_own[rows8(k, 0, half_rows), :]
        lower = ice_own[rows8(k, rows // 2, half_rows), :]
        left = lane_iota(half_rows) % 16 < 8
        out = rows8(k, 0, half_rows)
        ice_e[out, :] = jnp.where(left, upper, pltpu.roll(lower, 8, 1))
        ice_w[out, :] = jnp.where(left, pltpu.roll(lower, LANES - 8, 1), upper)

    loop(rows // 2 // half_rows, halve)

    top_rows = pl.ds(PAD + rows - HALO, HALO)
    low_rows = pl.ds(PAD, HALO)
    north_guard = pl.ds(PAD + rows, HALO)
    south_guard = pl.ds(PAD - HALO, HALO)

    def turned(f, value):
        value = jnp.concatenate([value[r : r + 1] for r in range(HALO - 1, -1, -1)], axis=0)
        value = jnp.take_along_axis(value, LANES - 1 - lane_iota(), axis=1)
        return -value if f in (0, 1, 3, 4) else value

    @pl.when(top)
    def _():
        for f in range(6):
            for t in range(2):
                fold[f, 1 - t, :, :] = turned(f, ext[f, t, top_rows, :])

    def faces(k):
        n = face_rows
        here = rows8(k, 0, n)
        s = [sea[t, here, :].astype(F32) for t in range(2)]
        for t in range(2):
            up = sea[t, pl.ds(k * n + 1, n), :].astype(F32)
            face_y[t, here, :] = s[t] * up
        se = from_east(s)
        face_x[0, here, :] = s[0] * se[0]
        face_x[1, here, :] = jnp.where(lane_iota(n) == LANES - 1, 0.0, s[1] * se[1])

    loop((rows + 8) // face_rows, faces)

    pl.semaphore_wait(barrier, greeted)

    send_e = remote(0, ice_e, ice_got_w, dev(lat, lon_e))
    send_w = remote(1, ice_w, ice_got_e, dev(lat, lon_w))
    send_e.start()
    send_w.start()
    wide = pl.ds(0, 2)
    send_n = remote(
        2, ext.at[:, wide, top_rows, :], ext.at[:, wide, south_guard, :], north_dev
    )
    send_s = remote(
        3, ext.at[:, wide, low_rows, :], ext.at[:, wide, north_guard, :], south_dev
    )
    send_fold = remote(2, fold, ext.at[:, wide, north_guard, :], north_dev, arrival=3)
    slab_top, slab_low = ice_own.at[pl.ds(rows - HALO, HALO)], ice_own.at[pl.ds(0, HALO)]
    send_ne = remote(4, slab_top, corners.at[0], dev(upper, lon_e))
    send_nw = remote(5, slab_top, corners.at[1], dev(upper, lon_w))
    send_se = remote(6, slab_low, corners.at[2], dev(lower, lon_e))
    send_sw = remote(7, slab_low, corners.at[3], dev(lower, lon_w))
    send_fold_w = remote(4, slab_top, corners.at[2], dev(lat, fold_w), arrival=6)
    send_fold_e = remote(5, slab_top, corners.at[3], dev(lat, fold_e), arrival=7)

    @pl.when(inner_top)
    def _():
        for copy in (send_n, send_ne, send_nw):
            copy.start()

    @pl.when(inner_bottom)
    def _():
        for copy in (send_s, send_se, send_sw):
            copy.start()

    @pl.when(top)
    def _():
        send_fold.start()

    @pl.when(fold_w_far)
    def _():
        send_fold_w.start()

    @pl.when(fold_e_far)
    def _():
        send_fold_e.start()

    @pl.when(top & (fold_w == lon))
    def _():
        corners[2, :, :] = ice_own[pl.ds(rows - HALO, HALO), :]

    @pl.when(top & (fold_e == lon))
    def _():
        corners[3, :, :] = ice_own[pl.ds(rows - HALO, HALO), :]

    def pack_edges(l):
        def body(k):
            n = edge_rows
            lanes = lane_iota(n)
            place = lanes % 32
            out = rows8(k, 0, n)
            if l:
                value, speed = own[0, out, :], own[1, out, :]
            else:
                value = speed = jnp.zeros((n, LANES), F32)
            for q in range(4):
                first_row = q * (rows // 4)
                here, mid = rows8(k, first_row, n), rows8(k, first_row + 8, n)
                for c in range(2):
                    j = 32 * q + 2 * (c * levels + l)
                    both = jnp.where(lanes == 0, tr[c, l, 0, mid, :], tr[c, l, 1, mid, :])
                    both = pltpu.roll(both, j + 1, 1)
                    value = jnp.where((lanes == j) | (lanes == j + 1), both, value)
                sea_e = sea[1, mid, :].astype(F32)
                j = 32 * q + 2 * l
                pushed = pltpu.roll(ev[l, 1, here, :] * sea_e, j + 1, 1)
                speed = jnp.where(lanes == j, pushed, speed)
                if not l:
                    sea_w = sea[0, mid, pl.ds(0, 1)].astype(F32)
                    odd = (lanes >= 32 * q) & (lanes < 32 * q + 32) & (lanes % 2 == 1)
                    speed = jnp.where(odd, jnp.broadcast_to(sea_w, (n, LANES)), speed)
            if l == levels - 1:
                again = (place >= 2 * levels) & (place < 4 * levels) & (place % 2 == 0)
                speed = jnp.where(again, pltpu.roll(speed, 2 * levels, 1), speed)
            own[0, out, :] = value
            own[1, out, :] = speed
            if l == levels - 1:
                even = lanes % 2 == 0
                own_e[out, :] = jnp.where(even, value, pltpu.roll(speed, 1, 1))
                own_w[out, :] = jnp.where(even, pltpu.roll(speed, LANES - 1, 1), value)

        loop(rows // 4 // edge_rows, body)

    def pack_rim(out, row, with_speed):
        out[pl.ds(out.shape[0] - 8, 8), :] = jnp.zeros((8, 2 * LANES), F32)
        for t in range(2):
            at = pl.ds(t * LANES, LANES)
            for l in range(levels):
                for c in range(2):
                    out[pl.ds(c * levels + l, 1), at] = tr[c, l, t, row, :]
                if with_speed:
                    out[pl.ds(2 * levels + l, 1), at] = nv[l, t, row, :]
            out[pl.ds(3 * levels, 1), at] = sea[t, row, :].astype(F32)

    both = [(c, t) for c in range(2) for t in range(2)]

    def advect(l):
        def ahead(k):
            return [pltpu.roll(tr[c, l, t, rows8(k, 8), :], LANES - 1, 1) for c, t in both]

        def east_flux(k, rolled):
            lanes = lane_iota()
            flux = []
            for c in range(2):
                a, b = rolled[2 * c], rolled[2 * c + 1]
                for t, xe in enumerate(
                    (jnp.where(lanes == LANES - 1, b, a), jnp.where(lanes == LANES - 1, a, b))
                ):
                    e = ev[l, t, rows8(k), :] * face_x[t, rows8(k, 8), :]
                    x = tr[c, l, t, rows8(k, 8), :]
                    flux.append(jnp.maximum(e, 0.0) * x + jnp.minimum(e, 0.0) * xe)
            return flux + [pltpu.roll(f, 1, 1) for f in flux]

        def finish(k, fluxes):
            lanes = lane_iota()
            mid, below, over = rows8(k, 8), pl.ds(k * 8 + 7, 8), pl.ds(k * 8 + 9, 8)
            for t in range(2):
                n = nv[l, t, mid, :] * face_y[t, mid, :]
                s = nv[l, t, below, :] * face_y[t, below, :]
                n_plus, n_minus = jnp.maximum(n, 0.0), jnp.minimum(n, 0.0)
                s_plus, s_minus = jnp.maximum(s, 0.0), jnp.minimum(s, 0.0)
                for c in range(2):
                    x = tr[c, l, t, mid, :]
                    fe = fluxes[2 * c + t]
                    fw = jnp.where(lanes == 0, fluxes[4 + 2 * c + 1 - t], fluxes[4 + 2 * c + t])
                    fn = n_plus * x + n_minus * tr[c, l, t, over, :]
                    fs = s_plus * tr[c, l, t, below, :] + s_minus * x
                    moved[c, l, t, rows8(k), :] = x - ((fe - fw) + (fn - fs))

        first, second = [], []
        n_blocks = rows // 8
        depth = min(AHEAD, n_blocks // 4)
        for k in range(depth):
            first.append(ahead(k))
        for k in range(depth):
            first.append(ahead(k + depth))
            second.append(east_flux(k, first.pop(0)))

        def step(k, carry):
            first, second = list(carry[0]), list(carry[1])
            first.append(ahead(k))
            second.append(east_flux(k - depth, first.pop(0)))
            finish(k - 2 * depth, second.pop(0))
            return first, second

        first, second = lax.fori_loop(
            2 * depth, n_blocks, step, (first, second), unroll=n_blocks - 2 * depth
        )
        for k in range(n_blocks, n_blocks + depth):
            second.append(east_flux(k - depth, first.pop(0)))
            finish(k - 2 * depth, second.pop(0))
        for k in range(n_blocks + depth, n_blocks + 2 * depth):
            finish(k - 2 * depth, second.pop(0))

    for l in range(levels):
        for copy in side_loads[l][2 if l == 0 else 0 :]:
            copy.wait()
        pack_edges(l)
        if l < EARLY:
            if l:
                for copy in north_loads[l]:
                    copy.wait()
            advect(l)
    send_edge_e = remote(8, own_e, got_w, dev(lat, lon_e))
    send_edge_w = remote(9, own_w, got_e, dev(lat, lon_w))
    send_edge_e.start()
    send_edge_w.start()
    for l in range(EARLY, levels):
        for copy in north_loads[l]:
            copy.wait()
    send_rim_n = remote(10, rim_up, rim_s, north_dev)
    send_rim_s = remote(11, rim_down, rim_n, south_dev)

    @pl.when(inner_top)
    def _():
        pack_rim(rim_up, pl.ds(rows + 7, 1), True)
        send_rim_n.start()

    @pl.when(inner_bottom)
    def _():
        pack_rim(rim_down, pl.ds(8, 1), False)
        send_rim_s.start()

    for l in range(EARLY, levels):
        advect(l)

    def unpack(value_w, value_e, n):
        lanes = lane_iota(n)
        both = jnp.where(lanes % 16 < 8, value_w, value_e)
        side = (lanes < 8) | (lanes >= LANES - 8)
        return [
            jnp.where(side, pltpu.roll(both, LANES - 16 * f - 8, 1), 0.0) for f in range(6)
        ]

    send_e.wait_recv()
    send_w.wait_recv()

    def unpack_ice(k):
        here = rows8(k, 0, half_rows)
        from_w, from_e = ice_got_w[here, :], ice_got_e[here, :]
        halves = (
            (from_w, from_e),
            (pltpu.roll(from_w, LANES - 8, 1), pltpu.roll(from_e, 8, 1)),
        )
        for h, (w, e) in enumerate(halves):
            for f, value in enumerate(unpack(w, e, half_rows)):
                ext[f, 2, rows8(k, PAD + h * (rows // 2), half_rows), :] = value

    loop(rows // 2 // half_rows, unpack_ice)

    @pl.when(inner_bottom)
    def _():
        send_ne.wait_recv()
        send_nw.wait_recv()
        for f, value in enumerate(unpack(corners[0], corners[1], HALO)):
            ext[f, 2, south_guard, :] = value

    @pl.when(bottom)
    def _():
        for f in range(6):
            for t in range(3):
                ext[f, t, south_guard, :] = zero

    @pl.when(inner_top | fold_w_far)
    def _():
        send_se.wait_recv()

    @pl.when(inner_top | fold_e_far)
    def _():
        send_sw.wait_recv()

    @pl.when(inner_top)
    def _():
        for f, value in enumerate(unpack(corners[2], corners[3], HALO)):
            ext[f, 2, north_guard, :] = value

    @pl.when(top)
    def _():
        for f, value in enumerate(unpack(corners[2], corners[3], HALO)):
            ext[f, 2, north_guard, :] = turned(f, value)

    def rim_row(i, t):
        return pl.ds(i, 1), pl.ds(t * LANES, LANES)

    @pl.when(inner_bottom)
    def _():
        send_rim_n.wait_recv()
        mine = pl.ds(8, 1)
        for t in range(2):
            face = rim_s[rim_row(3 * levels, t)] * sea[t, mine, :].astype(F32)
            for l in range(levels):
                speed = rim_s[rim_row(2 * levels + l, t)] * face
                for c in range(2):
                    there = rim_s[rim_row(c * levels + l, t)]
                    value = jnp.where(speed > 0, there, tr[c, l, t, mine, :])
                    moved[c, l, t, pl.ds(0, 1), :] += speed * value

    @pl.when(inner_top)
    def _():
        send_rim_s.wait_recv()
        mine = pl.ds(rows + 7, 1)
        for t in range(2):
            face = sea[t, mine, :].astype(F32) * rim_n[rim_row(3 * levels, t)]
            for l in range(levels):
                speed = nv[l, t, mine, :] * face
                for c in range(2):
                    there = rim_n[rim_row(c * levels + l, t)]
                    value = jnp.where(speed > 0, tr[c, l, t, mine, :], there)
                    moved[c, l, t, pl.ds(rows - 1, 1), :] -= speed * value

    send_edge_e.wait_recv()
    send_edge_w.wait_recv()

    def edge_update(k):
        n = edge_rows
        lanes = lane_iota(n)
        here = rows8(k, 0, n)
        x_own, s_own = own[0, here, :], own[1, here, :]
        x_w, x_e = got_w[here, :], got_e[here, :]
        e = pltpu.roll(x_w, LANES - 1, 1) * pltpu.roll(s_own, LANES - 1, 1)
        west = e * jnp.where(e > 0, x_w, pltpu.roll(x_own, LANES - 1, 1))
        e = s_own * x_e
        east_flux = e * jnp.where(e > 0, x_own, pltpu.roll(x_e, LANES - 1, 1))
        both = jnp.where(lanes % 2 == 0, -east_flux, pltpu.roll(west, 1, 1))
        for q in range(4):
            at = rows8(k, q * (rows // 4), n)
            for c in range(2):
                for l in range(levels):
                    j = 32 * q + 2 * (c * levels + l)
                    value = pltpu.roll(both, LANES - 1 - j, 1)
                    moved[c, l, 0, at, :] += jnp.where(lanes == 0, value, 0.0)
                    moved[c, l, 1, at, :] += jnp.where(lanes == LANES - 1, value, 0.0)

    loop(rows // 4 // edge_rows, edge_update)

    @pl.when(inner_bottom)
    def _():
        send_n.wait_recv()
        for copy in (send_s, send_se, send_sw, send_rim_s):
            copy.wait_send()

    @pl.when(inner_top)
    def _():
        for copy in (send_n, send_ne, send_nw, send_rim_n):
            copy.wait_send()

    @pl.when(top)
    def _():
        send_fold.wait_send()

    @pl.when(fold_w_far)
    def _():
        send_fold_w.wait_send()

    @pl.when(fold_e_far)
    def _():
        send_fold_e.wait_send()

    send_s.wait_recv()
    for copy in (send_e, send_w, send_edge_e, send_edge_w):
        copy.wait_send()


N_REMOTE = 12
N_ICE_LOADS = 14


def ice_kernel(
    levels, rows,
    moved, ext, turn, east, north,
    temp_out, salt_out, u_out, v_out,
    vel, stress, surf, water,
    load_sem, store_sem,
):
    n_ext = (rows + 2 * HALO) // 8
    ice_rows, last_rows = block(8 * n_ext, ICE_ROWS), block(rows, LAST_ROWS)

    def cols(t):
        return pl.ds(t * LANES, LANES)

    loads, stores = [], []
    for i, src in enumerate((east, north)):
        for t in range(2):
            copy = pltpu.make_async_copy(
                src.at[0, :, cols(t)], water.at[i, t], load_sem.at[2 * i + t]
            )
            copy.start()
            loads.append(copy)

    def store(src, dst):
        copy = pltpu.make_async_copy(src, dst, store_sem.at[len(stores)])
        copy.start()
        stores.append(copy)

    for l in range(1, levels):
        for c, dst in enumerate((temp_out, salt_out)):
            for t in range(2):
                store(moved.at[c, l, t], dst.at[l, :, cols(t)])

    def stresses(src, fresh):
        def body(k):
            mid = rows8(k, 8, ice_rows)
            below, over = pl.ds(k * ice_rows + 7, ice_rows), pl.ds(k * ice_rows + 9, ice_rows)
            u = [src[0, t, mid, :] for t in range(3)]
            v = [src[1, t, mid, :] for t in range(3)]
            ue, uw = from_east(u), from_west(u)
            ve, vw = from_east(v), from_west(v)
            for t in range(3):
                dudx, dvdx = ue[t] - uw[t], ve[t] - vw[t]
                dudy = src[0, t, over, :] - src[0, t, below, :]
                dvdy = src[1, t, over, :] - src[1, t, below, :]
                div, ten, shr = dudx + dvdy, dudx - dvdy, dudy + dvdx
                p = ext[2, t, mid, :]
                third = ext[5, t, mid, :]
                zeta = p * lax.rsqrt(div * div + 0.25 * (ten * ten + shr * shr) + 1.0)
                quarter = 0.25 * zeta
                a = zeta * div - p
                b = quarter * ten
                sxx, syy, sxy = a + b, a - b, quarter * shr
                if not fresh:
                    sxx = stress[0, t, mid, :] + sxx
                    syy = stress[1, t, mid, :] + syy
                    sxy = stress[2, t, mid, :] + sxy
                stress[0, t, mid, :] = sxx * third
                stress[1, t, mid, :] = syy * third
                stress[2, t, mid, :] = sxy * third

        loop(8 * n_ext // ice_rows, body)

    def momentum(src, k, first, tiles, count):
        mid = rows8(k, first, count)
        below, over = pl.ds(k * count + first - 1, count), pl.ds(k * count + first + 1, count)
        sxx = [stress[0, t, mid, :] for t in range(3)]
        sxy = [stress[2, t, mid, :] for t in range(3)]
        xxe, xxw = from_east(sxx), from_west(sxx)
        xye, xyw = from_east(sxy), from_west(sxy)
        a, b = (turn[i, rows8(k, first - 8, count), :] for i in range(2))
        out = []
        for t in range(tiles):
            fx = (xxe[t] - xxw[t]) + (stress[2, t, over, :] - stress[2, t, below, :])
            fy = (xye[t] - xyw[t]) + (stress[1, t, over, :] - stress[1, t, below, :])
            ru = src[0, t, mid, :] + (0.25 * fx + ext[3, t, mid, :])
            rv = src[1, t, mid, :] + (0.25 * fy + ext[4, t, mid, :])
            third = ext[5, t, mid, :]
            out.append(((a * ru + b * rv) * third, (a * rv - b * ru) * third))
        return out

    src = ext
    for subcycle in range(SUBCYCLES - 1):
        stresses(src, subcycle == 0)

        def body(k, src=src):
            for t, (u, v) in enumerate(momentum(src, k, 8, 3, ice_rows)):
                vel[0, t, rows8(k, 8, ice_rows), :] = u
                vel[1, t, rows8(k, 8, ice_rows), :] = v

        loop(8 * n_ext // ice_rows, body)
        src = vel
    stresses(src, False)
    for copy in loads:
        copy.wait()

    def final(k):
        here, mid = rows8(k, 0, last_rows), rows8(k, PAD, last_rows)
        for t, (u, v) in enumerate(momentum(vel, k, PAD, 2, last_rows)):
            vel[0, t, mid, :] = u
            vel[1, t, mid, :] = v
            slip_u = u - water[0, t, here, :]
            slip_v = v - water[1, t, here, :]
            sst, sss = moved[0, 0, t, here, :], moved[1, 0, t, here, :]
            heat = (
                0.3 * ext[5, t, mid, :]
                * (1.0 + (slip_u * slip_u + slip_v * slip_v))
                * (sst + 0.054 * sss)
            )
            surf[0, t, here, :] = sst - heat
            surf[1, t, here, :] = sss - 0.5 * heat

    steps = rows // last_rows
    for group in range(GROUPS):
        begin, end = steps * group // GROUPS, steps * (group + 1) // GROUPS
        loop(end - begin, lambda k, begin=begin: final(k + begin))
        at, count = begin * last_rows, (end - begin) * last_rows
        for t in range(2):
            here = pl.ds(at, count)
            store(vel.at[0, t, pl.ds(PAD + at, count), :], u_out.at[here, cols(t)])
            store(vel.at[1, t, pl.ds(PAD + at, count), :], v_out.at[here, cols(t)])
            store(surf.at[0, t, here, :], temp_out.at[0, here, cols(t)])
            store(surf.at[1, t, here, :], salt_out.at[0, here, cols(t)])
    for copy in stores:
        copy.wait()


def per_device(lat_count, lon_count, *args):
    temp = args[0]
    levels, rows, _ = temp.shape
    any_space = pl.BlockSpec(memory_space=pl.ANY)
    vmem_space = pl.BlockSpec(memory_space=pltpu.VMEM)
    deep = rows + 2 * PAD
    moved, ext, turn = pl.pallas_call(
        functools.partial(ocean_kernel, levels, rows, lat_count, lon_count),
        out_shape=(
            pltpu.VMEM((2, levels, 2, rows, LANES), F32),
            pltpu.VMEM((6, 3, deep, LANES), F32),
            pltpu.VMEM((2, rows + 2 * HALO, LANES), F32),
        ),
        in_specs=[any_space] * 11,
        out_specs=(vmem_space,) * 3,
        scratch_shapes=[
            pltpu.VMEM((2, levels, 2, rows + 16, LANES), F32),
            pltpu.VMEM((levels, 2, rows, LANES), F32),
            pltpu.VMEM((levels, 2, rows + 8, LANES), F32),
            pltpu.VMEM((2, rows + 16, LANES), jnp.int32),
            pltpu.VMEM((2, rows, LANES), jnp.int32),
            pltpu.VMEM((4, 2, rows, LANES), F32),
            pltpu.VMEM((2, rows + 8, LANES), F32),
            pltpu.VMEM((2, rows + 8, LANES), F32),
        ]
        + [pltpu.VMEM((8 * pl.cdiv(3 * levels + 1, 8), 2 * LANES), F32)] * 4
        + [
            pltpu.VMEM((4, HALO, LANES), F32),
        ]
        + [pltpu.VMEM((2, rows // 4, LANES), F32)]
        + [pltpu.VMEM((rows // 4, LANES), F32)] * 4
        + [pltpu.VMEM((rows, LANES), F32)]
        + [pltpu.VMEM((rows // 2, LANES), F32)] * 4
        + [
            pltpu.VMEM((6, 2, HALO, LANES), F32),
            pltpu.SemaphoreType.DMA((N_ICE_LOADS + 8 * levels,)),
            pltpu.SemaphoreType.DMA((N_REMOTE,)),
            pltpu.SemaphoreType.DMA((N_REMOTE,)),
        ],
        compiler_params=pltpu.CompilerParams(
            collective_id=0, has_side_effects=True, vmem_limit_bytes=48 * 1024 * 1024
        ),
        name="ocean",
    )(*args)
    moved = pltpu.with_memory_space_constraint(moved, pltpu.VMEM)
    ext = pltpu.with_memory_space_constraint(ext, pltpu.VMEM)
    turn = pltpu.with_memory_space_constraint(turn, pltpu.VMEM)
    shapes = (temp, temp, args[6], args[6])
    return pl.pallas_call(
        functools.partial(ice_kernel, levels, rows),
        out_shape=tuple(jax.ShapeDtypeStruct(a.shape, a.dtype) for a in shapes),
        in_specs=[vmem_space] * 3 + [any_space] * 2,
        out_specs=(any_space,) * 4,
        scratch_shapes=[
            pltpu.VMEM((2, 3, deep, LANES), F32),
            pltpu.VMEM((3, 3, deep, LANES), F32),
            pltpu.VMEM((2, 2, rows, LANES), F32),
            pltpu.VMEM((2, 2, rows, LANES), F32),
            pltpu.SemaphoreType.DMA((4,)),
            pltpu.SemaphoreType.DMA((4 * (levels - 1) + 8 * GROUPS,)),
        ],
        compiler_params=pltpu.CompilerParams(vmem_limit_bytes=48 * 1024 * 1024),
        name="ice",
    )(moved, ext, turn, args[2], args[3])


def solution(mesh):
    deep, flat = P(None, "lat", "lon"), P("lat", "lon")
    return jax.shard_map(
        functools.partial(per_device, mesh.shape["lat"], mesh.shape["lon"]),
        mesh=mesh,
        in_specs=(deep,) * 4 + (flat,) * 7,
        out_specs=(deep, deep, flat, flat),
        check_vma=False,
    )
```

```python
import functools

import jax
import jax.numpy as jnp
from jax import lax
from jax.experimental import pallas as pl
from jax.experimental.pallas import tpu as pltpu
from jax.sharding import PartitionSpec as P

SUBCYCLES = 4
LANES = 128
HALO = 2 * SUBCYCLES
PAD = 16
MESH = pl.DeviceIdType.MESH
F32 = jnp.float32


def lane_iota(rows=8):
    return lax.broadcasted_iota(jnp.int32, (rows, LANES), 1)


ICE_ROWS = 8
LAST_ROWS = 8
GROUPS = 2
PACK_ROWS = 96
FACE_ROWS = 8
EDGE_ROWS = 96
AHEAD = 8


def block(total, most):
    return max(n for n in range(8, most + 1, 8) if total % n == 0)


def rows8(k, first=0, count=8):
    start = k * count + first
    return pl.ds(start if isinstance(start, int) else pl.multiple_of(start, 8), count)


def loop(count, body):
    def step(k, carry):
        body(k)
        return carry

    lax.fori_loop(0, count, step, 0, unroll=count)


def from_east(tiles):
    rolled = [pltpu.roll(a, LANES - 1, 1) for a in tiles]
    n = len(tiles)
    lane = lane_iota(tiles[0].shape[0])
    return [jnp.where(lane == LANES - 1, rolled[(t + 1) % n], rolled[t]) for t in range(n)]


def from_west(tiles):
    rolled = [pltpu.roll(a, 1, 1) for a in tiles]
    n = len(tiles)
    lane = lane_iota(tiles[0].shape[0])
    return [jnp.where(lane == 0, rolled[(t - 1) % n], rolled[t]) for t in range(n)]


def ocean_kernel(
    levels, rows, lat_count, lon_count,
    temp, salt, east, north, land, icem, ice_u, ice_v, press, wind_x, wind_y,
    moved, ext, turn,
    tr, ev, nv, sea, icb, uvw, face_x, face_y, rim_s, rim_n, rim_up, rim_down, north_rim, corners,
    own, own_e, own_w, got_w, got_e, ice_own, ice_e, ice_w, ice_got_w, ice_got_e, fold,
    local_sem, send_sem, recv_sem,
):
    pack_rows, face_rows = block(rows, PACK_ROWS), block(rows + 8, FACE_ROWS)
    edge_rows, half_rows = block(rows // 4, EDGE_ROWS), block(rows // 2, PACK_ROWS)
    lat = lax.axis_index("lat")
    lon = lax.axis_index("lon")
    lon_e = lax.rem(lon + 1, lon_count)
    lon_w = lax.rem(lon + lon_count - 1, lon_count)
    top = lat == lat_count - 1
    bottom = lat == 0
    inner_top, inner_bottom = jnp.logical_not(top), jnp.logical_not(bottom)
    mirror = lon_count - 1 - lon
    fold_w = lax.rem(2 * lon_count - 2 - lon, lon_count)
    fold_e = lax.rem(lon_count - lon, lon_count)
    fold_w_far = top & (fold_w != lon)
    fold_e_far = top & (fold_e != lon)

    def dev(la, lo):
        return {"lat": la, "lon": lo}

    upper, lower = jnp.where(top, lat, lat + 1), jnp.where(bottom, lat, lat - 1)
    north_dev = dev(upper, jnp.where(top, mirror, lon))
    south_dev = dev(lower, lon)

    barrier = pltpu.get_barrier_semaphore()

    def greet(device):
        pl.semaphore_signal(barrier, inc=1, device_id=device, device_id_type=MESH)

    greet(dev(lat, lon_w))
    greet(dev(lat, lon_e))
    greet(north_dev)

    @pl.when(inner_top)
    def _():
        greet(dev(upper, lon_w))
        greet(dev(upper, lon_e))

    @pl.when(fold_w_far)
    def _():
        greet(dev(lat, fold_w))

    @pl.when(fold_e_far)
    def _():
        greet(dev(lat, fold_e))

    @pl.when(inner_bottom)
    def _():
        greet(south_dev)
        greet(dev(lower, lon_w))
        greet(dev(lower, lon_e))

    greeted = (
        3
        + 3 * inner_bottom.astype(jnp.int32)
        + 2 * inner_top.astype(jnp.int32)
        + fold_w_far.astype(jnp.int32)
        + fold_e_far.astype(jnp.int32)
    )

    started = []

    def load(src, dst):
        copy = pltpu.make_async_copy(src, dst, local_sem.at[len(started)])
        copy.start()
        started.append(copy)
        return copy

    def cols(t):
        return pl.ds(t * LANES, LANES)

    ice_loads = []
    for t in range(2):
        ice_loads += [
            load(land.at[:, cols(t)], sea.at[t, pl.ds(8, rows), :]),
            load(icem.at[:, cols(t)], icb.at[t]),
            load(ice_u.at[:, cols(t)], uvw.at[0, t]),
            load(ice_v.at[:, cols(t)], uvw.at[1, t]),
            load(wind_x.at[:, cols(t)], uvw.at[2, t]),
            load(wind_y.at[:, cols(t)], uvw.at[3, t]),
            load(press.at[:, cols(t)], ext.at[2, t, pl.ds(PAD, rows), :]),
        ]
    side_loads, north_loads = [], []

    def load_north(l):
        north_loads.append(
            [load(north.at[l, :, cols(t)], nv.at[l, t, pl.ds(8, rows), :]) for t in range(2)]
        )

    for l in range(levels):
        speeds = [load(east.at[l, :, cols(t)], ev.at[l, t]) for t in range(2)]
        if l == 0:
            load_north(0)
            rim_load = load(north.at[:, pl.ds(rows - 8, 8), :], north_rim)
        for t in range(2):
            speeds += [
                load(temp.at[l, :, cols(t)], tr.at[0, l, t, pl.ds(8, rows), :]),
                load(salt.at[l, :, cols(t)], tr.at[1, l, t, pl.ds(8, rows), :]),
            ]
        side_loads.append(speeds)
    for l in range(1, levels):
        load_north(l)

    def turning(k):
        g = lat * rows - HALO + k * 8 + lax.broadcasted_iota(jnp.int32, (8, LANES), 0)
        g = jnp.where(g >= grid_rows, 2 * grid_rows - 1 - g, g)
        coriolis = 0.5 * (2 * g + 1 - grid_rows).astype(F32) / grid_rows
        b = 0.5 * coriolis
        inverse = 1.0 / (2.25 + b * b)
        turn[0, rows8(k), :] = 4.5 * inverse
        turn[1, rows8(k), :] = 3.0 * b * inverse

    grid_rows = rows * lat_count
    loop((rows + 2 * HALO) // 8, turning)

    zero = jnp.zeros((8, LANES), F32)
    for t in range(2):
        for edge in (0, rows + 8):
            sea[t, pl.ds(edge, 8), :] = jnp.zeros((8, LANES), jnp.int32)
            for l in range(levels):
                for c in range(2):
                    tr[c, l, t, pl.ds(edge, 8), :] = zero
        for l in range(levels):
            nv[l, t, pl.ds(0, 8), :] = zero

    def remote(i, src, dst, device, arrival=None):
        return pltpu.make_async_remote_copy(
            src_ref=src, dst_ref=dst, send_sem=send_sem.at[i],
            recv_sem=recv_sem.at[i if arrival is None else arrival],
            device_id=device, device_id_type=MESH,
        )

    for copy in ice_loads:
        copy.wait()
    for copy in side_loads[0][:2] + north_loads[0]:
        copy.wait()

    def pack_ice(k):
        n = pack_rows
        here, mid, out = rows8(k, 0, n), rows8(k, 8, n), rows8(k, PAD, n)
        lanes = lane_iota(n)
        fields = []
        for t in range(2):
            covered = (sea[t, mid, :] * icb[t, here, :]).astype(F32)
            third = covered * (1.0 / 3.0)
            mine = (
                uvw[0, t, here, :] * covered,
                uvw[1, t, here, :] * covered,
                ext[2, t, out, :],
                0.5 * (uvw[2, t, here, :] + ev[0, t, here, :]),
                0.5 * (uvw[3, t, here, :] + nv[0, t, mid, :]),
                third,
            )
            for f in (0, 1, 3, 4, 5):
                ext[f, t, out, :] = mine[f]
            fields.append(mine)
        packed = jnp.zeros((n, LANES), F32)
        for f in range(6):
            both = jnp.where(lanes < HALO, fields[0][f], fields[1][f])
            both = pltpu.roll(both, 16 * f + 8, 1)
            packed = jnp.where((lanes >= 16 * f) & (lanes < 16 * f + 16), both, packed)
        ice_own[here, :] = packed

    loop(rows // pack_rows, pack_ice)

    def halve(k):
        upper = ice_own[rows8(k, 0, half_rows), :]
        lower = ice_own[rows8(k, rows // 2, half_rows), :]
        left = lane_iota(half_rows) % 16 < 8
        out = rows8(k, 0, half_rows)
        ice_e[out, :] = jnp.where(left, upper, pltpu.roll(lower, 8, 1))
        ice_w[out, :] = jnp.where(left, pltpu.roll(lower, LANES - 8, 1), upper)

    loop(rows // 2 // half_rows, halve)

    top_rows = pl.ds(PAD + rows - HALO, HALO)
    low_rows = pl.ds(PAD, HALO)
    north_guard = pl.ds(PAD + rows, HALO)
    south_guard = pl.ds(PAD - HALO, HALO)

    def turned(f, value):
        value = jnp.concatenate([value[r : r + 1] for r in range(HALO - 1, -1, -1)], axis=0)
        value = jnp.take_along_axis(value, LANES - 1 - lane_iota(), axis=1)
        return -value if f in (0, 1, 3, 4) else value

    @pl.when(top)
    def _():
        for f in range(6):
            for t in range(2):
                fold[f, 1 - t, :, :] = turned(f, ext[f, t, top_rows, :])

    def faces(k):
        n = face_rows
        here = rows8(k, 0, n)
        s = [sea[t, here, :].astype(F32) for t in range(2)]
        for t in range(2):
            up = sea[t, pl.ds(k * n + 1, n), :].astype(F32)
            face_y[t, here, :] = s[t] * up
        se = from_east(s)
        face_x[0, here, :] = s[0] * se[0]
        face_x[1, here, :] = jnp.where(lane_iota(n) == LANES - 1, 0.0, s[1] * se[1])

    loop((rows + 8) // face_rows, faces)

    pl.semaphore_wait(barrier, greeted)

    send_e = remote(0, ice_e, ice_got_w, dev(lat, lon_e))
    send_w = remote(1, ice_w, ice_got_e, dev(lat, lon_w))
    send_e.start()
    send_w.start()
    wide = pl.ds(0, 2)
    send_n = remote(
        2, ext.at[:, wide, top_rows, :], ext.at[:, wide, south_guard, :], north_dev
    )
    send_s = remote(
        3, ext.at[:, wide, low_rows, :], ext.at[:, wide, north_guard, :], south_dev
    )
    send_fold = remote(2, fold, ext.at[:, wide, north_guard, :], north_dev, arrival=3)
    slab_top, slab_low = ice_own.at[pl.ds(rows - HALO, HALO)], ice_own.at[pl.ds(0, HALO)]
    send_ne = remote(4, slab_top, corners.at[0], dev(upper, lon_e))
    send_nw = remote(5, slab_top, corners.at[1], dev(upper, lon_w))
    send_se = remote(6, slab_low, corners.at[2], dev(lower, lon_e))
    send_sw = remote(7, slab_low, corners.at[3], dev(lower, lon_w))
    send_fold_w = remote(4, slab_top, corners.at[2], dev(lat, fold_w), arrival=6)
    send_fold_e = remote(5, slab_top, corners.at[3], dev(lat, fold_e), arrival=7)

    @pl.when(inner_top)
    def _():
        for copy in (send_n, send_ne, send_nw):
            copy.start()

    @pl.when(inner_bottom)
    def _():
        for copy in (send_s, send_se, send_sw):
            copy.start()

    @pl.when(top)
    def _():
        send_fold.start()

    @pl.when(fold_w_far)
    def _():
        send_fold_w.start()

    @pl.when(fold_e_far)
    def _():
        send_fold_e.start()

    @pl.when(top & (fold_w == lon))
    def _():
        corners[2, :, :] = ice_own[pl.ds(rows - HALO, HALO), :]

    @pl.when(top & (fold_e == lon))
    def _():
        corners[3, :, :] = ice_own[pl.ds(rows - HALO, HALO), :]

    def pack_edges(l):
        def body(k):
            n = edge_rows
            lanes = lane_iota(n)
            place = lanes % 32
            out = rows8(k, 0, n)
            if l:
                value, speed = own[0, out, :], own[1, out, :]
            else:
                value = speed = jnp.zeros((n, LANES), F32)
            for q in range(4):
                first_row = q * (rows // 4)
                here, mid = rows8(k, first_row, n), rows8(k, first_row + 8, n)
                for c in range(2):
                    j = 32 * q + 2 * (c * levels + l)
                    both = jnp.where(lanes == 0, tr[c, l, 0, mid, :], tr[c, l, 1, mid, :])
                    both = pltpu.roll(both, j + 1, 1)
                    value = jnp.where((lanes == j) | (lanes == j + 1), both, value)
                sea_e = sea[1, mid, :].astype(F32)
                j = 32 * q + 2 * l
                pushed = pltpu.roll(ev[l, 1, here, :] * sea_e, j + 1, 1)
                speed = jnp.where(lanes == j, pushed, speed)
                if not l:
                    sea_w = sea[0, mid, pl.ds(0, 1)].astype(F32)
                    odd = (lanes >= 32 * q) & (lanes < 32 * q + 32) & (lanes % 2 == 1)
                    speed = jnp.where(odd, jnp.broadcast_to(sea_w, (n, LANES)), speed)
            if l == levels - 1:
                again = (place >= 2 * levels) & (place < 4 * levels) & (place % 2 == 0)
                speed = jnp.where(again, pltpu.roll(speed, 2 * levels, 1), speed)
            own[0, out, :] = value
            own[1, out, :] = speed
            if l == levels - 1:
                even = lanes % 2 == 0
                own_e[out, :] = jnp.where(even, value, pltpu.roll(speed, 1, 1))
                own_w[out, :] = jnp.where(even, pltpu.roll(speed, LANES - 1, 1), value)

        loop(rows // 4 // edge_rows, body)

    def pack_rim(out, row, with_speed):
        out[pl.ds(out.shape[0] - 8, 8), :] = jnp.zeros((8, 2 * LANES), F32)
        for t in range(2):
            at = pl.ds(t * LANES, LANES)
            for l in range(levels):
                for c in range(2):
                    out[pl.ds(c * levels + l, 1), at] = tr[c, l, t, row, :]
                if with_speed:
                    out[pl.ds(2 * levels + l, 1), at] = north_rim[l, pl.ds(7, 1), at]
            out[pl.ds(3 * levels, 1), at] = sea[t, row, :].astype(F32)

    both = [(c, t) for c in range(2) for t in range(2)]

    def advect(l):
        def ahead(k):
            return [pltpu.roll(tr[c, l, t, rows8(k, 8), :], LANES - 1, 1) for c, t in both]

        def east_flux(k, rolled):
            lanes = lane_iota()
            flux = []
            for c in range(2):
                a, b = rolled[2 * c], rolled[2 * c + 1]
                for t, xe in enumerate(
                    (jnp.where(lanes == LANES - 1, b, a), jnp.where(lanes == LANES - 1, a, b))
                ):
                    e = ev[l, t, rows8(k), :] * face_x[t, rows8(k, 8), :]
                    x = tr[c, l, t, rows8(k, 8), :]
                    flux.append(jnp.maximum(e, 0.0) * x + jnp.minimum(e, 0.0) * xe)
            return flux + [pltpu.roll(f, 1, 1) for f in flux]

        def finish(k, fluxes):
            lanes = lane_iota()
            mid, below, over = rows8(k, 8), pl.ds(k * 8 + 7, 8), pl.ds(k * 8 + 9, 8)
            for t in range(2):
                n = nv[l, t, mid, :] * face_y[t, mid, :]
                s = nv[l, t, below, :] * face_y[t, below, :]
                n_plus, n_minus = jnp.maximum(n, 0.0), jnp.minimum(n, 0.0)
                s_plus, s_minus = jnp.maximum(s, 0.0), jnp.minimum(s, 0.0)
                for c in range(2):
                    x = tr[c, l, t, mid, :]
                    fe = fluxes[2 * c + t]
                    fw = jnp.where(lanes == 0, fluxes[4 + 2 * c + 1 - t], fluxes[4 + 2 * c + t])
                    fn = n_plus * x + n_minus * tr[c, l, t, over, :]
                    fs = s_plus * tr[c, l, t, below, :] + s_minus * x
                    moved[c, l, t, rows8(k), :] = x - ((fe - fw) + (fn - fs))

        first, second = [], []
        n_blocks = rows // 8
        depth = min(AHEAD, n_blocks // 4)
        for k in range(depth):
            first.append(ahead(k))
        for k in range(depth):
            first.append(ahead(k + depth))
            second.append(east_flux(k, first.pop(0)))

        def step(k, carry):
            first, second = list(carry[0]), list(carry[1])
            first.append(ahead(k))
            second.append(east_flux(k - depth, first.pop(0)))
            finish(k - 2 * depth, second.pop(0))
            return first, second

        first, second = lax.fori_loop(
            2 * depth, n_blocks, step, (first, second), unroll=n_blocks - 2 * depth
        )
        for k in range(n_blocks, n_blocks + depth):
            second.append(east_flux(k - depth, first.pop(0)))
            finish(k - 2 * depth, second.pop(0))
        for k in range(n_blocks + depth, n_blocks + 2 * depth):
            finish(k - 2 * depth, second.pop(0))

    for l in range(levels):
        for copy in side_loads[l][2 if l == 0 else 0 :]:
            copy.wait()
        pack_edges(l)
    send_edge_e = remote(8, own_e, got_w, dev(lat, lon_e))
    send_edge_w = remote(9, own_w, got_e, dev(lat, lon_w))
    send_edge_e.start()
    send_edge_w.start()
    rim_load.wait()
    send_rim_n = remote(10, rim_up, rim_s, north_dev)
    send_rim_s = remote(11, rim_down, rim_n, south_dev)

    @pl.when(inner_top)
    def _():
        pack_rim(rim_up, pl.ds(rows + 7, 1), True)
        send_rim_n.start()

    @pl.when(inner_bottom)
    def _():
        pack_rim(rim_down, pl.ds(8, 1), False)
        send_rim_s.start()

    for l in range(levels):
        if l:
            for copy in north_loads[l]:
                copy.wait()
        advect(l)

    def unpack(value_w, value_e, n):
        lanes = lane_iota(n)
        both = jnp.where(lanes % 16 < 8, value_w, value_e)
        side = (lanes < 8) | (lanes >= LANES - 8)
        return [
            jnp.where(side, pltpu.roll(both, LANES - 16 * f - 8, 1), 0.0) for f in range(6)
        ]

    send_e.wait_recv()
    send_w.wait_recv()

    def unpack_ice(k):
        here = rows8(k, 0, half_rows)
        from_w, from_e = ice_got_w[here, :], ice_got_e[here, :]
        halves = (
            (from_w, from_e),
            (pltpu.roll(from_w, LANES - 8, 1), pltpu.roll(from_e, 8, 1)),
        )
        for h, (w, e) in enumerate(halves):
            for f, value in enumerate(unpack(w, e, half_rows)):
                ext[f, 2, rows8(k, PAD + h * (rows // 2), half_rows), :] = value

    loop(rows // 2 // half_rows, unpack_ice)

    @pl.when(inner_bottom)
    def _():
        send_ne.wait_recv()
        send_nw.wait_recv()
        for f, value in enumerate(unpack(corners[0], corners[1], HALO)):
            ext[f, 2, south_guard, :] = value

    @pl.when(bottom)
    def _():
        for f in range(6):
            for t in range(3):
                ext[f, t, south_guard, :] = zero

    @pl.when(inner_top | fold_w_far)
    def _():
        send_se.wait_recv()

    @pl.when(inner_top | fold_e_far)
    def _():
        send_sw.wait_recv()

    @pl.when(inner_top)
    def _():
        for f, value in enumerate(unpack(corners[2], corners[3], HALO)):
            ext[f, 2, north_guard, :] = value

    @pl.when(top)
    def _():
        for f, value in enumerate(unpack(corners[2], corners[3], HALO)):
            ext[f, 2, north_guard, :] = turned(f, value)

    def rim_row(i, t):
        return pl.ds(i, 1), pl.ds(t * LANES, LANES)

    @pl.when(inner_bottom)
    def _():
        send_rim_n.wait_recv()
        mine = pl.ds(8, 1)
        for t in range(2):
            face = rim_s[rim_row(3 * levels, t)] * sea[t, mine, :].astype(F32)
            for l in range(levels):
                speed = rim_s[rim_row(2 * levels + l, t)] * face
                for c in range(2):
                    there = rim_s[rim_row(c * levels + l, t)]
                    value = jnp.where(speed > 0, there, tr[c, l, t, mine, :])
                    moved[c, l, t, pl.ds(0, 1), :] += speed * value

    @pl.when(inner_top)
    def _():
        send_rim_s.wait_recv()
        mine = pl.ds(rows + 7, 1)
        for t in range(2):
            face = sea[t, mine, :].astype(F32) * rim_n[rim_row(3 * levels, t)]
            for l in range(levels):
                speed = nv[l, t, mine, :] * face
                for c in range(2):
                    there = rim_n[rim_row(c * levels + l, t)]
                    value = jnp.where(speed > 0, tr[c, l, t, mine, :], there)
                    moved[c, l, t, pl.ds(rows - 1, 1), :] -= speed * value

    send_edge_e.wait_recv()
    send_edge_w.wait_recv()

    def edge_update(k):
        n = edge_rows
        lanes = lane_iota(n)
        here = rows8(k, 0, n)
        x_own, s_own = own[0, here, :], own[1, here, :]
        x_w, x_e = got_w[here, :], got_e[here, :]
        e = pltpu.roll(x_w, LANES - 1, 1) * pltpu.roll(s_own, LANES - 1, 1)
        west = e * jnp.where(e > 0, x_w, pltpu.roll(x_own, LANES - 1, 1))
        e = s_own * x_e
        east_flux = e * jnp.where(e > 0, x_own, pltpu.roll(x_e, LANES - 1, 1))
        both = jnp.where(lanes % 2 == 0, -east_flux, pltpu.roll(west, 1, 1))
        for q in range(4):
            at = rows8(k, q * (rows // 4), n)
            for c in range(2):
                for l in range(levels):
                    j = 32 * q + 2 * (c * levels + l)
                    value = pltpu.roll(both, LANES - 1 - j, 1)
                    moved[c, l, 0, at, :] += jnp.where(lanes == 0, value, 0.0)
                    moved[c, l, 1, at, :] += jnp.where(lanes == LANES - 1, value, 0.0)

    loop(rows // 4 // edge_rows, edge_update)

    @pl.when(inner_bottom)
    def _():
        send_n.wait_recv()
        for copy in (send_s, send_se, send_sw, send_rim_s):
            copy.wait_send()

    @pl.when(inner_top)
    def _():
        for copy in (send_n, send_ne, send_nw, send_rim_n):
            copy.wait_send()

    @pl.when(top)
    def _():
        send_fold.wait_send()

    @pl.when(fold_w_far)
    def _():
        send_fold_w.wait_send()

    @pl.when(fold_e_far)
    def _():
        send_fold_e.wait_send()

    send_s.wait_recv()
    for copy in (send_e, send_w, send_edge_e, send_edge_w):
        copy.wait_send()


N_REMOTE = 12
N_ICE_LOADS = 14


def ice_kernel(
    levels, rows,
    moved, ext, turn, east, north,
    temp_out, salt_out, u_out, v_out,
    vel, stress, surf, water,
    load_sem, store_sem,
):
    n_ext = (rows + 2 * HALO) // 8
    ice_rows, last_rows = block(8 * n_ext, ICE_ROWS), block(rows, LAST_ROWS)

    def cols(t):
        return pl.ds(t * LANES, LANES)

    loads, stores = [], []
    for i, src in enumerate((east, north)):
        for t in range(2):
            copy = pltpu.make_async_copy(
                src.at[0, :, cols(t)], water.at[i, t], load_sem.at[2 * i + t]
            )
            copy.start()
            loads.append(copy)

    def store(src, dst):
        copy = pltpu.make_async_copy(src, dst, store_sem.at[len(stores)])
        copy.start()
        stores.append(copy)

    for l in range(1, levels):
        for c, dst in enumerate((temp_out, salt_out)):
            for t in range(2):
                store(moved.at[c, l, t], dst.at[l, :, cols(t)])

    def stresses(src, fresh):
        def body(k):
            mid = rows8(k, 8, ice_rows)
            below, over = pl.ds(k * ice_rows + 7, ice_rows), pl.ds(k * ice_rows + 9, ice_rows)
            u = [src[0, t, mid, :] for t in range(3)]
            v = [src[1, t, mid, :] for t in range(3)]
            ue, uw = from_east(u), from_west(u)
            ve, vw = from_east(v), from_west(v)
            for t in range(3):
                dudx, dvdx = ue[t] - uw[t], ve[t] - vw[t]
                dudy = src[0, t, over, :] - src[0, t, below, :]
                dvdy = src[1, t, over, :] - src[1, t, below, :]
                div, ten, shr = dudx + dvdy, dudx - dvdy, dudy + dvdx
                p = ext[2, t, mid, :]
                third = ext[5, t, mid, :]
                zeta = p * lax.rsqrt(div * div + 0.25 * (ten * ten + shr * shr) + 1.0)
                quarter = 0.25 * zeta
                a = zeta * div - p
                b = quarter * ten
                sxx, syy, sxy = a + b, a - b, quarter * shr
                if not fresh:
                    sxx = stress[0, t, mid, :] + sxx
                    syy = stress[1, t, mid, :] + syy
                    sxy = stress[2, t, mid, :] + sxy
                stress[0, t, mid, :] = sxx * third
                stress[1, t, mid, :] = syy * third
                stress[2, t, mid, :] = sxy * third

        loop(8 * n_ext // ice_rows, body)

    def momentum(src, k, first, tiles, count):
        mid = rows8(k, first, count)
        below, over = pl.ds(k * count + first - 1, count), pl.ds(k * count + first + 1, count)
        sxx = [stress[0, t, mid, :] for t in range(3)]
        sxy = [stress[2, t, mid, :] for t in range(3)]
        xxe, xxw = from_east(sxx), from_west(sxx)
        xye, xyw = from_east(sxy), from_west(sxy)
        a, b = (turn[i, rows8(k, first - 8, count), :] for i in range(2))
        out = []
        for t in range(tiles):
            fx = (xxe[t] - xxw[t]) + (stress[2, t, over, :] - stress[2, t, below, :])
            fy = (xye[t] - xyw[t]) + (stress[1, t, over, :] - stress[1, t, below, :])
            ru = src[0, t, mid, :] + (0.25 * fx + ext[3, t, mid, :])
            rv = src[1, t, mid, :] + (0.25 * fy + ext[4, t, mid, :])
            third = ext[5, t, mid, :]
            out.append(((a * ru + b * rv) * third, (a * rv - b * ru) * third))
        return out

    src = ext
    for subcycle in range(SUBCYCLES - 1):
        stresses(src, subcycle == 0)

        def body(k, src=src):
            for t, (u, v) in enumerate(momentum(src, k, 8, 3, ice_rows)):
                vel[0, t, rows8(k, 8, ice_rows), :] = u
                vel[1, t, rows8(k, 8, ice_rows), :] = v

        loop(8 * n_ext // ice_rows, body)
        src = vel
    stresses(src, False)
    for copy in loads:
        copy.wait()

    def final(k):
        here, mid = rows8(k, 0, last_rows), rows8(k, PAD, last_rows)
        for t, (u, v) in enumerate(momentum(vel, k, PAD, 2, last_rows)):
            vel[0, t, mid, :] = u
            vel[1, t, mid, :] = v
            slip_u = u - water[0, t, here, :]
            slip_v = v - water[1, t, here, :]
            sst, sss = moved[0, 0, t, here, :], moved[1, 0, t, here, :]
            heat = (
                0.3 * ext[5, t, mid, :]
                * (1.0 + (slip_u * slip_u + slip_v * slip_v))
                * (sst + 0.054 * sss)
            )
            surf[0, t, here, :] = sst - heat
            surf[1, t, here, :] = sss - 0.5 * heat

    steps = rows // last_rows
    for group in range(GROUPS):
        begin, end = steps * group // GROUPS, steps * (group + 1) // GROUPS
        loop(end - begin, lambda k, begin=begin: final(k + begin))
        at, count = begin * last_rows, (end - begin) * last_rows
        for t in range(2):
            here = pl.ds(at, count)
            store(vel.at[0, t, pl.ds(PAD + at, count), :], u_out.at[here, cols(t)])
            store(vel.at[1, t, pl.ds(PAD + at, count), :], v_out.at[here, cols(t)])
            store(surf.at[0, t, here, :], temp_out.at[0, here, cols(t)])
            store(surf.at[1, t, here, :], salt_out.at[0, here, cols(t)])
    for copy in stores:
        copy.wait()


def per_device(lat_count, lon_count, *args):
    temp = args[0]
    levels, rows, _ = temp.shape
    any_space = pl.BlockSpec(memory_space=pl.ANY)
    vmem_space = pl.BlockSpec(memory_space=pltpu.VMEM)
    deep = rows + 2 * PAD
    moved, ext, turn = pl.pallas_call(
        functools.partial(ocean_kernel, levels, rows, lat_count, lon_count),
        out_shape=(
            pltpu.VMEM((2, levels, 2, rows, LANES), F32),
            pltpu.VMEM((6, 3, deep, LANES), F32),
            pltpu.VMEM((2, rows + 2 * HALO, LANES), F32),
        ),
        in_specs=[any_space] * 11,
        out_specs=(vmem_space,) * 3,
        scratch_shapes=[
            pltpu.VMEM((2, levels, 2, rows + 16, LANES), F32),
            pltpu.VMEM((levels, 2, rows, LANES), F32),
            pltpu.VMEM((levels, 2, rows + 8, LANES), F32),
            pltpu.VMEM((2, rows + 16, LANES), jnp.int32),
            pltpu.VMEM((2, rows, LANES), jnp.int32),
            pltpu.VMEM((4, 2, rows, LANES), F32),
            pltpu.VMEM((2, rows + 8, LANES), F32),
            pltpu.VMEM((2, rows + 8, LANES), F32),
        ]
        + [pltpu.VMEM((8 * pl.cdiv(3 * levels + 1, 8), 2 * LANES), F32)] * 4
        + [
            pltpu.VMEM((levels, 8, 2 * LANES), F32),
            pltpu.VMEM((4, HALO, LANES), F32),
        ]
        + [pltpu.VMEM((2, rows // 4, LANES), F32)]
        + [pltpu.VMEM((rows // 4, LANES), F32)] * 4
        + [pltpu.VMEM((rows, LANES), F32)]
        + [pltpu.VMEM((rows // 2, LANES), F32)] * 4
        + [
            pltpu.VMEM((6, 2, HALO, LANES), F32),
            pltpu.SemaphoreType.DMA((N_ICE_LOADS + 8 * levels + 1,)),
            pltpu.SemaphoreType.DMA((N_REMOTE,)),
            pltpu.SemaphoreType.DMA((N_REMOTE,)),
        ],
        compiler_params=pltpu.CompilerParams(
            collective_id=0, has_side_effects=True, vmem_limit_bytes=48 * 1024 * 1024
        ),
        name="ocean",
    )(*args)
    moved = pltpu.with_memory_space_constraint(moved, pltpu.VMEM)
    ext = pltpu.with_memory_space_constraint(ext, pltpu.VMEM)
    turn = pltpu.with_memory_space_constraint(turn, pltpu.VMEM)
    shapes = (temp, temp, args[6], args[6])
    return pl.pallas_call(
        functools.partial(ice_kernel, levels, rows),
        out_shape=tuple(jax.ShapeDtypeStruct(a.shape, a.dtype) for a in shapes),
        in_specs=[vmem_space] * 3 + [any_space] * 2,
        out_specs=(any_space,) * 4,
        scratch_shapes=[
            pltpu.VMEM((2, 3, deep, LANES), F32),
            pltpu.VMEM((3, 3, deep, LANES), F32),
            pltpu.VMEM((2, 2, rows, LANES), F32),
            pltpu.VMEM((2, 2, rows, LANES), F32),
            pltpu.SemaphoreType.DMA((4,)),
            pltpu.SemaphoreType.DMA((4 * (levels - 1) + 8 * GROUPS,)),
        ],
        compiler_params=pltpu.CompilerParams(vmem_limit_bytes=48 * 1024 * 1024),
        name="ice",
    )(moved, ext, turn, args[2], args[3])


def solution(mesh):
    deep, flat = P(None, "lat", "lon"), P("lat", "lon")
    return jax.shard_map(
        functools.partial(per_device, mesh.shape["lat"], mesh.shape["lon"]),
        mesh=mesh,
        in_specs=(deep,) * 4 + (flat,) * 7,
        out_specs=(deep, deep, flat, flat),
        check_vma=False,
    )
```
